32 devices in a mesh: dp: 8 (over z, x), head: 4 (over y, core).
Axes of the slice: x: 2, y: 2, z: 4, core: 2. Of those that a mesh axis runs over, the one named last changes fastest.
Arguments:
- block_input: bfloat16 [16384, 768], P(('dp', 'head')), may hold values from -6 to 6
- norm1_gain: float32 [768], replicated, may hold values from 0.5 to 1.5
- norm1_bias: float32 [768], replicated, may hold values from -0.625 to 0.625
- qkv_weight: bfloat16 [3, 768, 768], P(None, None, 'head'), may hold values from -0.21875 to 0.21875
- qkv_bias: float32 [2, 12, 64], P(None, 'head'), may hold values from -0.625 to 0.625
- proj_weight: bfloat16 [768, 768], P('head'), may hold values from -1.75 to 1.75
- proj_bias: float32 [768], replicated, may hold values from -0.625 to 0.625
- norm2_gain: float32 [768], replicated, may hold values from 0.5 to 1.5
- norm2_bias: float32 [768], replicated, may hold values from -0.625 to 0.625
- router_weight: float32 [768, 8], replicated, may hold values from -0.15625 to 0.15625
- up_weight: bfloat16 [8, 768, 3072], P('dp'), may hold values from -0.21875 to 0.21875
- up_bias: float32 [8, 3072], P('dp'), may hold values from -0.625 to 0.625
- down_weight: bfloat16 [8, 3072, 768], P('dp'), may hold values from -1.25 to 1.25
- down_bias: float32 [8, 768], P('dp'), may hold values from -5 to 5
- routes: int32 [16384, 1], P(('dp', 'head')), may hold values from 0 to 7; in each aligned block of 512 rows (0 to 511, 512 to 1023, ...) at most 128 rows name the same one
- lengths: int32 [8, 4], P('dp'), may hold values from 1 to 1024, 2048 in all within a row
- cotangent: bfloat16 [16384, 768], P(('dp', 'head')), may hold values from -6 to 6
Outputs:
- mixed: bfloat16 [16384, 768], P(('dp', 'head'))
- balance: float32 [32], P(('dp', 'head'))
- input_grad: float32 [16384, 768], P(('dp', 'head'))
- norm1_gain_grad: float32 [768], P(('dp', 'head'))
- norm1_bias_grad: float32 [768], P(('dp', 'head'))
- qkv_weight_grad: float32 [3, 768, 768], P(None, 'dp', 'head')
- qkv_bias_grad: float32 [2, 12, 64], P(None, 'head', 'dp')
- proj_weight_grad: float32 [768, 768], P('head', 'dp')
- proj_bias_grad: float32 [768], P(('dp', 'head'))
- norm2_gain_grad: float32 [768], P(('dp', 'head'))
- norm2_bias_grad: float32 [768], P(('dp', 'head'))
- router_weight_grad: float32 [768, 8], P(('dp', 'head'))
- up_weight_grad: float32 [8, 768, 3072], P('dp', None, 'head')
- up_bias_grad: float32 [8, 3072], P('dp', 'head')
- down_weight_grad: float32 [8, 3072, 768], P('dp', 'head')
- down_bias_grad: float32 [8, 768], P('dp', 'head')
The draws below stay inside these ranges and needn't reach their ends.
Inputs may be any that keep to these rules, and one draw needn't show every extreme that they name: `routes`: among the rows of one device at most 128 name the same expert. `lengths`: each row sums to 2048, and its largest entry is 1024.
All inputs are finite; a program needn't handle non-finite values.
Results may differ from the reference program's by a relative error of at most 0.017.
Values may be sent and summed in bfloat16 or wider, within the bound.
A program may use at most 192 MiB of HBM per device.

```python
import math
import jax
import jax.numpy as jnp
import numpy as np
from jax import lax

D = 768
HEADS = 12
HD = 64
FF = 3072
TOK_DEV = 512
SEQ_GRP = 4
HHD = 768
GROUP_TOK = 2048
LONGEST = 1024
EXPERTS = 8
CAP = 128
TOKENS = 16384
N_DP = 8


def block_scale(stream_key, shape, cuts, smallest, high):
    level, own = 1.0, jax.random.fold_in(stream_key, 6)
    for dim, shards_of in cuts:
        draws = jnp.exp(jax.random.uniform(jax.random.fold_in(own, dim), (shards_of,), jnp.float32, smallest / len(cuts), high / len(cuts)))
        level = level * jnp.repeat(draws, shape[dim] // shards_of).reshape([-1 if axis == dim else 1 for axis in range(len(shape))])
    return level


def length_profile(count, total, reach, skew):
    portions = [(1 << 20) // math.isqrt(standing ** skew) + 1 for standing in range(2, count + 1)]
    rest, given = total - reach - (count - 1), [1] * (count - 1)
    while rest > 0:
        free = [i for i in range(count - 1) if given[i] < reach]
        whole, remaining = sum([portions[i] for i in free]), rest
        for i in free:
            addition = min(reach - given[i], max(1, remaining * portions[i] // whole), rest)
            given[i] = given[i] + addition
            rest = rest - addition
    return np.array([reach] + given)


def uneven_parts(rng, count, total, reach, lean):
    if count == 2:
        one = jax.random.randint(rng, (), max(1, total - reach), min(reach, total - 1) + 1)
        return jnp.stack([one, total - one])
    sizes = jnp.asarray(length_profile(count, total, reach, lean), jnp.int32)
    couples = (count - 1) // 2
    donor, sink = sizes[1:1 + 2 * couples:2], sizes[2:2 + 2 * couples:2]
    room = jnp.minimum(donor - 1, reach - sink)
    moved = jax.random.randint(jax.random.fold_in(rng, 1), (couples,), 0, 1 << 20) % (room + 1)
    sizes = sizes.at[1:1 + 2 * couples:2].set(donor - moved).at[2:2 + 2 * couples:2].set(sink + moved)
    return sizes[jax.random.permutation(jax.random.fold_in(rng, 2), count)]


def shared_out(key, own, number, rows, count, top, most, skew):
    sequence = jax.random.permutation(key, count)
    crowded, usual = load_shares(count, rows * top, most, skew, True), load_shares(count, rows * top, most, skew, False)
    places = jnp.arange(count)

    def named(sizes, offset_by):
        used = int((sizes > 0).sum())
        fixed = max(1, used // 4)
        moved = fixed + (places - fixed + offset_by * (used - fixed)) % max(1, count - fixed)
        return jnp.zeros((count,), jnp.int32).at[sequence[jnp.where(places < fixed, places, moved)]].set(jnp.asarray(sizes, jnp.int32))

    sizes = jnp.where(number % 4 == 0, named(crowded, number // 4), named(usual, number - number // 4 - 1))
    mixed = jax.random.permutation(jax.random.fold_in(own, 3), count)
    giver, receiver = mixed[0:count // 2 * 2:2], mixed[1:count // 2 * 2:2]
    room = jnp.minimum(sizes[giver] - 1, most - sizes[receiver]) // 2
    room = jnp.where((giver == sequence[0]) | (receiver == sequence[0]) | (sizes[receiver] == 0), 0, jnp.maximum(room, 0))
    moved = jax.random.randint(jax.random.fold_in(own, 4), (count // 2,), 0, 1 << 20) % (room + 1)
    sizes = sizes.at[giver].add(-moved).at[receiver].add(moved)
    members = jnp.searchsorted(jnp.cumsum(sizes), jnp.arange(rows * top), side="right").astype(jnp.int32)
    grid = members.reshape(top, rows).T
    grid = grid[jax.random.permutation(jax.random.fold_in(own, 1), rows)]
    offset_by = jax.random.randint(jax.random.fold_in(own, 2), (rows, 1), 0, top)
    return jnp.take_along_axis(grid, (jnp.arange(top)[None, :] + offset_by) % top, axis=1)


def load_shares(count, total, reach, skew, full):
    weights = [(1 << 20) // math.isqrt(rank ** skew) + 1 for rank in range(1, count + 1)]
    largest = reach if full else min(reach, max(-(-total // count), total * weights[0] // sum(weights)))
    least = 1 if total - largest >= count - 1 else 0
    given, rest = [largest] + [least] * (count - 1), total - largest - least * (count - 1)
    while rest > 0:
        movable = [i for i in range(1, count) if given[i] < largest] or [i for i in range(1, count) if given[i] < reach]
        pool, budget = sum([weights[i] for i in movable]), rest
        for i in movable:
            more = min(reach - given[i], max(1, budget * weights[i] // pool), rest)
            given[i] = given[i] + more
            rest = rest - more
    return np.array(given)


def bell_draw(rng, extent, scale, reach, split=(), kind=jnp.bfloat16):
    values = scale * jax.random.normal(rng, extent, jnp.float32)
    if split:
        values = values * block_scale(rng, extent, split, -0.22, 0.18)
    return jnp.clip(values, -reach, reach).astype(kind)


def setup_inputs(seed: int = 0) -> dict:
    key_list = jax.random.split(jax.random.key(seed), 18)
    block_input = bell_draw(key_list[0], (TOKENS, D), 1.0, 6.0, ((0, 32),))
    norm1_gain = jnp.clip(1.0 + 0.1 * jax.random.normal(key_list[1], (D,), jnp.float32), 0.5, 1.5)
    norm1_bias = bell_draw(key_list[2], (D,), 0.1, 0.625, (), jnp.float32)
    qkv_weight = bell_draw(key_list[3], (3, D, HHD), D ** -0.5, 0.21875, ((2, 4),))
    qkv_bias = bell_draw(key_list[4], (2, HEADS, HD), 0.1, 0.625, ((1, 4),), jnp.float32)
    proj_weight = bell_draw(key_list[5], (HHD, D), (HHD // 64) ** -0.5, 1.75, ((0, 4),))
    proj_bias = bell_draw(key_list[6], (D,), 0.1, 0.625, (), jnp.float32)
    norm2_gain = jnp.clip(1.0 + 0.1 * jax.random.normal(key_list[7], (D,), jnp.float32), 0.5, 1.5)
    norm2_bias = bell_draw(key_list[8], (D,), 0.1, 0.625, (), jnp.float32)
    router_weight = bell_draw(key_list[9], (D, EXPERTS), (2 * D) ** -0.5, 0.15625, (), jnp.float32)
    up_weight = bell_draw(key_list[10], (EXPERTS, D, FF), D ** -0.5, 0.21875, ((0, 8),))
    up_bias = bell_draw(key_list[11], (EXPERTS, FF), 0.1, 0.625, ((0, 8),), jnp.float32)
    down_weight = bell_draw(key_list[12], (EXPERTS, FF, D), (max(1, FF // (2 * EXPERTS * EXPERTS))) ** -0.5, 1.25, ((0, 8),))
    down_bias = bell_draw(key_list[13], (EXPERTS, D), (0.1 * EXPERTS), 5.0, ((0, 8),), jnp.float32)
    routes_keys = jax.random.split(jax.random.fold_in(key_list[14], 1), TOKENS // TOK_DEV)
    routes_turns = jax.random.permutation(jax.random.fold_in(key_list[14], 3), TOKENS // TOK_DEV)
    routes = jax.vmap(lambda own, number: shared_out(jax.random.fold_in(key_list[14], 2), own, number, TOK_DEV, EXPERTS, 1, CAP, 1))(routes_keys, routes_turns).reshape((TOKENS, 1))
    lengths = jax.vmap(lambda own: uneven_parts(own, SEQ_GRP, GROUP_TOK, LONGEST, 1))(jax.random.split(key_list[15], N_DP)).reshape((N_DP, SEQ_GRP)).astype(jnp.int32)
    cotangent = bell_draw(key_list[16], (TOKENS, D), 1.0, 6.0, ((0, 32),))
    return dict(block_input=block_input, norm1_gain=norm1_gain, norm1_bias=norm1_bias, qkv_weight=qkv_weight, qkv_bias=qkv_bias, proj_weight=proj_weight, proj_bias=proj_bias, norm2_gain=norm2_gain, norm2_bias=norm2_bias, router_weight=router_weight, up_weight=up_weight, up_bias=up_bias, down_weight=down_weight, down_bias=down_bias, routes=routes, lengths=lengths, cotangent=cotangent)


@jax.custom_vjp
def low(v):
    return lax.optimization_barrier(v.astype(jnp.bfloat16)).astype(jnp.float32)

@jax.custom_vjp
def low_back(v):
    return v

def low_keep(v):
    return (low(v), None)

def low_pass(kept, grad):
    return (grad,)

def back_keep(v):
    return (v, None)

def back_low(kept, grad):
    return (low(grad),)
low.defvjp(low_keep, low_pass)
low_back.defvjp(back_keep, back_low)
EPSILON = 1e-05
BAL_COEF = 0.01
HIGHEST = lax.Precision.HIGHEST
NEG_LARGE = -1e+30

def matmul(left, right):
    return jnp.dot(left, right, precision=HIGHEST, preferred_element_type=jnp.float32)

def normalize(values, gain, bias):
    average = lax.optimization_barrier(jnp.mean(values, axis=-1, keepdims=True))
    centred = values - average
    variance = lax.optimization_barrier(jnp.mean(centred * centred, axis=-1, keepdims=True))
    return centred * lax.rsqrt(variance + EPSILON) * gain + bias

def attend_group(queries, keys_all, values_all, group_lengths):
    count = queries.shape[0]
    positions = jnp.arange(count, dtype=jnp.int32)
    seq_ends = jnp.cumsum(group_lengths.astype(jnp.int32))
    segment = lax.optimization_barrier(jnp.sum((positions[:, None] >= seq_ends[None, :]).astype(jnp.int32), axis=1))
    allowed = (segment[:, None] == segment[None, :]) & (positions[None, :] <= positions[:, None])
    scores = jnp.einsum('qhd,khd->hqk', queries, keys_all, precision=HIGHEST) * HD ** (-0.5)
    scores = low_back(scores)
    scores = jnp.where(allowed[None], scores, NEG_LARGE)
    probability = low(jax.nn.softmax(scores, axis=-1))
    return jnp.einsum('hqk,khd->qhd', probability, values_all, precision=HIGHEST)

def expert_apply(expert_rows, up_one, up_bias_one, down_one, down_bias_one):
    preact = low_back(matmul(expert_rows, up_one) + up_bias_one)
    hidden = low(jax.nn.gelu(preact, approximate=False))
    return low_back(low(matmul(hidden, down_one) + down_bias_one))

def forward(block_input, gain_one, bias_one, qkv_weight, qkv_bias, proj_weight, proj_bias, gain_two, bias_two, router_weight, up_weight, up_bias, down_weight, down_bias, routes, lengths):
    num_tokens, width = block_input.shape
    normed_one = low(normalize(block_input, gain_one, bias_one))
    columns = HEADS * HD
    queries = low_back(low(matmul(normed_one, qkv_weight[0]) + qkv_bias[0].reshape(columns)))
    keys_all = low_back(low(matmul(normed_one, qkv_weight[1])))
    values_all = low_back(low(matmul(normed_one, qkv_weight[2]) + qkv_bias[1].reshape(columns)))
    groups = lengths.shape[0]
    group_shape = (groups, GROUP_TOK, HEADS, HD)
    context = lax.map(lambda packed: jax.checkpoint(attend_group)(*packed), (queries.reshape(group_shape), keys_all.reshape(group_shape), values_all.reshape(group_shape), lengths))
    context = low_back(low(context.reshape(num_tokens, columns)))
    attended = low_back(matmul(context, proj_weight))
    residual = block_input + attended + proj_bias
    normed_two = normalize(residual, gain_two, bias_two)
    logits = matmul(normed_two, router_weight)
    probability = jax.nn.softmax(logits, axis=-1)
    num_experts = router_weight.shape[1]
    expert_id = routes[:, 0].astype(jnp.int32)
    hot_int = (expert_id[:, None] == jnp.arange(num_experts, dtype=jnp.int32)[None, :]).astype(jnp.int32)
    hot_float = hot_int.astype(jnp.float32)
    gate_value = lax.optimization_barrier(jnp.sum(probability * hot_float, axis=1))
    num_blocks = num_tokens // TOK_DEV
    fraction = lax.optimization_barrier(jnp.mean(hot_float.reshape(num_blocks, TOK_DEV, num_experts), axis=1))
    mean_prob = lax.optimization_barrier(jnp.mean(probability.reshape(num_blocks, TOK_DEV, num_experts), axis=1))
    balance = num_experts * lax.optimization_barrier(jnp.sum(fraction * mean_prob, axis=1))
    expert_in = low_back(low(normed_two))
    ranks = jnp.cumsum(hot_int.reshape(num_blocks, TOK_DEV, num_experts), axis=1).reshape(num_tokens, num_experts)
    slot_index = (lax.optimization_barrier(jnp.sum(ranks * hot_int, axis=1)) - 1).astype(jnp.int32)
    device_id = (jnp.arange(num_tokens, dtype=jnp.int32) // TOK_DEV).astype(jnp.int32)
    send_buffer = jnp.zeros((num_blocks, num_experts, CAP, width), jnp.float32).at[device_id, expert_id, slot_index].set(expert_in)
    expert_rows = send_buffer.transpose(1, 0, 2, 3).reshape(num_experts, num_blocks * CAP, width)
    expert_outs = lax.map(lambda packed: jax.checkpoint(expert_apply)(*packed), (expert_rows, up_weight, up_bias, down_weight, down_bias))
    returned_buf = expert_outs.reshape(num_experts, num_blocks, CAP, width).transpose(1, 0, 2, 3)
    returned = returned_buf[device_id, expert_id, slot_index]
    mixed = residual + gate_value[:, None] * returned
    return (mixed, balance)

def reference(block_input, norm1_gain, norm1_bias, qkv_weight, qkv_bias, proj_weight, proj_bias, norm2_gain, norm2_bias, router_weight, up_weight, up_bias, down_weight, down_bias, routes, lengths, cotangent):

    def run_block(a_in, a_g1, a_b1, a_qkv, a_qb, a_pw, a_pb, a_g2, a_b2, a_rw, a_uw, a_ub, a_dw, a_db):
        return forward(a_in, a_g1, a_b1, a_qkv, a_qb, a_pw, a_pb, a_g2, a_b2, a_rw, a_uw, a_ub, a_dw, a_db, routes, lengths)
    (mixed, balance), pull_back = jax.vjp(run_block, block_input.astype(jnp.float32), norm1_gain.astype(jnp.float32), norm1_bias.astype(jnp.float32), qkv_weight.astype(jnp.float32), qkv_bias.astype(jnp.float32), proj_weight.astype(jnp.float32), proj_bias.astype(jnp.float32), norm2_gain.astype(jnp.float32), norm2_bias.astype(jnp.float32), router_weight.astype(jnp.float32), up_weight.astype(jnp.float32), up_bias.astype(jnp.float32), down_weight.astype(jnp.float32), down_bias.astype(jnp.float32))
    grads = pull_back((cotangent.astype(jnp.float32), jnp.full(balance.shape, BAL_COEF, jnp.float32)))
    return (mixed.astype(jnp.bfloat16), balance, grads[0], grads[1], grads[2], grads[3], grads[4], grads[5], grads[6], grads[7], grads[8], grads[9], grads[10], grads[11], grads[12], grads[13])
```

```python
import functools
import jax
import jax.numpy as jnp
from jax import lax
from jax.experimental import pallas as pl
from jax.experimental.pallas import tpu as pltpu
from jax.sharding import PartitionSpec as P

EPSILON = 1e-05
BAL_COEF = 0.01
HIGHEST = lax.Precision.HIGHEST
NEG_LARGE = -1e30
MESH = pl.DeviceIdType.MESH
F32 = jnp.float32
BF16 = jnp.bfloat16
TILE = 256
VMEM_LIMIT = 60 << 20


def flip(index, bits):
    out, bit = index, 1
    while bit <= bits:
        if bits & bit:
            out = out + bit - 2 * bit * lax.rem(lax.div(index, bit), 2)
        bit *= 2
    return out


def remote(src, dst, send_sem, recv_sem, device):
    return pltpu.make_async_remote_copy(
        src_ref=src, dst_ref=dst, send_sem=send_sem, recv_sem=recv_sem, device_id=device, device_id_type=MESH
    )


def dot(left, right, dims=((1,), (0,)), precision=None):
    return lax.dot_general(left, right, (dims, ((), ())), precision=precision, preferred_element_type=F32)


def normalize(values, gain, bias):
    average = jnp.mean(values, axis=-1, keepdims=True)
    centred = values - average
    variance = jnp.mean(centred * centred, axis=-1, keepdims=True)
    inverse = lax.rsqrt(variance + EPSILON)
    scaled = centred * inverse
    return (scaled * gain + bias, scaled, inverse)


def norm_backward(grad_normed, scaled, inverse, gain):
    grad_scaled = grad_normed * gain
    first_mean = jnp.mean(grad_scaled, axis=-1, keepdims=True)
    second_mean = jnp.mean(grad_scaled * scaled, axis=-1, keepdims=True)
    return inverse * (grad_scaled - first_mean - scaled * second_mean)


def slot_layouts(routes, experts, cap):
    rows = routes.shape[1]
    count = max(8, experts)
    expert = lax.broadcasted_iota(jnp.int32, (count, rows), 0)
    hot = (routes == expert).astype(F32)
    upto = lax.broadcasted_iota(jnp.int32, (rows, rows), 0) <= lax.broadcasted_iota(jnp.int32, (rows, rows), 1)
    rank = dot(hot.astype(BF16), upto.astype(F32).astype(BF16))
    slot_row = jnp.sum((rank - 1.0) * hot, axis=0, keepdims=True)
    flat_row = jnp.sum((rank - 1.0 + cap * expert.astype(F32)) * hot, axis=0, keepdims=True)
    return hot, flat_row.astype(jnp.int32), slot_row.astype(jnp.int32)


def barrier_signal(peers):
    barrier = pltpu.get_barrier_semaphore()
    for peer in peers:
        pl.semaphore_signal(barrier, inc=1, device_id=peer, device_id_type=MESH)


def barrier_wait(count):
    pl.semaphore_wait(pltpu.get_barrier_semaphore(), count)


def kernel_a(
    n_dp, x_ref, g1_ref, b1_ref, w_ref, qb_ref, proj_ref, routes_ref, cot_ref, len_ref,
    gath_o, qkv_o, p_o, ctx_o, ctxf_o, projf_o, cots_o,
    gath, qkv, p_st, bias_s, ctx_s, disp,
    ag_s, ag_r, pj_s, pj_r, cx_s, cx_r, ct_s, ct_r, p_sem, loc,
):
    tok, width = x_ref.shape
    heads = qb_ref.shape[0]
    hd = qb_ref.shape[2]
    group = 4 * tok
    tiles = group // TILE
    reach = group // 2 // TILE + 1
    cap = cots_o.shape[0] // n_dp
    d = lax.axis_index("dp")
    h = lax.axis_index("head")
    barrier_signal([(d, flip(h, k)) for k in (1, 2, 3)] + [(flip(d, r), h) for r in range(1, n_dp)])

    normed, _, _ = normalize(x_ref[...].astype(F32), g1_ref[...][None, :], b1_ref[...][None, :])

    def block(index):
        return pl.ds(pl.multiple_of(index * tok, tok), tok)

    gath[block(h), :] = normed.astype(BF16)
    barrier_wait(3 + n_dp - 1)

    chunks = 4
    step = tok // chunks

    def part(index, i):
        return gath.at[pl.ds(pl.multiple_of(index * tok + i * step, step), step), :]

    sib, cross, diag = flip(h, 1), flip(h, 2), flip(h, 3)
    to_cross = [remote(part(h, i), part(h, i), ag_s.at[i], ag_r.at[i], (d, cross)) for i in range(chunks)]
    to_sib = remote(gath.at[block(h), :], gath.at[block(h), :], ag_s.at[2 * chunks], ag_r.at[2 * chunks], (d, sib))
    onward = [
        remote(part(cross, i), part(cross, i), ag_s.at[chunks + i], ag_r.at[chunks + i], (d, sib)) for i in range(chunks)
    ]
    for copy in to_cross:
        copy.start()
    to_sib.start()
    proj_copies = [
        remote(proj_ref, projf_o.at[h], pj_s.at[k], pj_r.at[k], (d, flip(h, k))) for k in (1, 2, 3)
    ]

    hot_t, flat_row, slot_row = slot_layouts(routes_ref[...], n_dp, cap)
    slot_iota = lax.broadcasted_iota(jnp.int32, (cap, tok), 0)

    def dispatch(e, carry):
        hot = (flat_row == slot_iota + e * cap).astype(F32).astype(BF16)
        disp[pl.ds(pl.multiple_of(e * cap, cap), cap), :] = dot(hot, cot_ref[...]).astype(BF16)
        return carry

    lax.fori_loop(0, n_dp, dispatch, 0)

    def slots(index):
        return pl.ds(pl.multiple_of(index * cap, cap), cap)

    cot_copies = [
        remote(disp.at[slots(flip(d, r)), :], cots_o.at[pl.ds(r * cap, cap), :], ct_s.at[r], ct_r.at[r], (flip(d, r), h))
        for r in range(1, n_dp)
    ]
    for copy in cot_copies:
        copy.start()
    cot_own = pltpu.make_async_copy(disp.at[slots(d), :], cots_o.at[pl.ds(0, cap), :], ct_s.at[0])
    cot_own.start()

    def project(index):
        rows = gath[block(index), :]
        for c in range(3):
            out = dot(rows, w_ref[c], ((1,), (1,)))
            for a in range(heads):
                piece = out[:, a * hd : (a + 1) * hd]
                if c != 1:
                    piece = piece + qb_ref[a, c // 2 : c // 2 + 1, :]
                piece = piece.astype(BF16)
                if c == 0:
                    piece = piece * jnp.asarray(hd ** (-0.5), BF16)
                qkv[c, a, block(index), :] = piece

    project(h)
    to_sib.wait_recv()
    project(sib)
    for i in range(chunks):
        to_cross[i].wait_recv()
        onward[i].start()
    for copy in proj_copies:
        copy.start()
    proj_own = pltpu.make_async_copy(proj_ref, projf_o.at[h], loc.at[0])
    proj_own.start()
    project(cross)
    for i in range(chunks):
        onward[i].wait_recv()
    project(diag)
    gath_copy = pltpu.make_async_copy(gath, gath_o, loc.at[1])
    gath_copy.start()
    qkv_copy = pltpu.make_async_copy(qkv, qkv_o, loc.at[2])
    qkv_copy.start()

    ends = [len_ref[0, 0]]
    for i in range(1, len_ref.shape[1] - 1):
        ends.append(ends[-1] + len_ref[0, i])

    order = []
    for i in range(tiles // 2):
        order += [tiles - 1 - i, tiles // 2 - 1 - i]
    per_block = tok // TILE

    def p_copy(t, a):
        size = min(t + 1, reach) * TILE
        return pltpu.make_async_copy(p_st.at[a, :, pl.ds(0, size)], p_o.at[a, t, :, pl.ds(0, size)], p_sem.at[a])

    previous = None
    for t in order:
        size = min(t + 1, reach) * TILE
        first = (t + 1) * TILE - size
        row = t * TILE + lax.broadcasted_iota(jnp.int32, (TILE, 1), 0)
        start = jnp.zeros((TILE, 1), jnp.int32)
        for end in ends:
            start = jnp.where(row >= end, end, start)
        col = first + lax.broadcasted_iota(jnp.int32, (TILE, size), 1)
        bias_s[:, :size] = jnp.where((col >= start) & (col <= row), 0.0, NEG_LARGE)
        outs = []
        for a in range(heads):
            q = qkv[0, a, t * TILE : (t + 1) * TILE, :]
            k = qkv[1, a, first : (t + 1) * TILE, :]
            v = qkv[2, a, first : (t + 1) * TILE, :]
            s = dot(q, k, ((1,), (1,))) + bias_s[:, :size]
            top = jnp.max(s, axis=1, keepdims=True)
            e = jnp.exp(s - top)
            total = jnp.sum(e, axis=1, keepdims=True)
            p = (e * (1.0 / total)).astype(BF16)
            if previous is not None:
                p_copy(previous, a).wait()
            p_st[a, :, :size] = p
            p_copy(t, a).start()
            outs.append(dot(p, v))
        ctx_s[t] = jnp.concatenate(outs, axis=1).astype(BF16)
        previous = t
        owner, sub = t // per_block, t % per_block
        rows = pl.ds(sub * TILE, TILE)

        @pl.when(h != owner)
        def _():
            remote(ctx_s.at[t], ctxf_o.at[h, rows, :], cx_s.at[t], cx_r.at[h, sub], (d, owner)).start()

        @pl.when(h == owner)
        def _():
            pltpu.make_async_copy(ctx_s.at[t], ctxf_o.at[h, rows, :], cx_s.at[t]).start()

    ctx_copy = pltpu.make_async_copy(ctx_s, ctx_o, loc.at[3])
    ctx_copy.start()
    for a in range(heads):
        p_copy(previous, a).wait()
    for t in range(tiles):
        owner, sub = t // per_block, t % per_block
        rows = pl.ds(sub * TILE, TILE)

        @pl.when(h != owner)
        def _():
            remote(ctx_s.at[t], ctxf_o.at[h, rows, :], cx_s.at[t], cx_r.at[h, sub], (d, owner)).wait_send()

        @pl.when(h == owner)
        def _():
            pltpu.make_async_copy(ctx_s.at[t], ctxf_o.at[h, rows, :], cx_s.at[t]).wait()

    for k in (1, 2, 3):
        peer = flip(h, k)
        for sub in range(per_block):
            remote(
                ctx_s.at[0], ctxf_o.at[peer, pl.ds(sub * TILE, TILE), :], cx_s.at[0], cx_r.at[peer, sub], (d, peer)
            ).wait_recv()
    for copy in to_cross:
        copy.wait_send()
    to_sib.wait_send()
    for copy in onward:
        copy.wait_send()
    for k in (1, 2, 3):
        proj_copies[k - 1].wait_send()
        peer = flip(h, k)
        remote(proj_ref, projf_o.at[peer], pj_s.at[k], pj_r.at[k], (d, peer)).wait_recv()
    for copy in cot_copies:
        copy.wait()
    for copy in (cot_own, proj_own, gath_copy, qkv_copy, ctx_copy):
        copy.wait()


VM = pl.BlockSpec(memory_space=pltpu.VMEM)
SM = pl.BlockSpec(memory_space=pltpu.SMEM)
ANY = pl.BlockSpec(memory_space=pl.ANY)
DMA = pltpu.SemaphoreType.DMA


def stage_a(n_dp, x, g1, b1, w, qb, proj, routes, cot, lengths, cap):
    tok, width = x.shape
    heads, hd = qb.shape[1:]
    w, qb, routes = w.transpose(0, 2, 1), qb.transpose(1, 0, 2), routes.T
    group = 4 * tok
    tiles = group // TILE
    span = (group // 2 // TILE + 1) * TILE
    cols = heads * hd
    sds = jax.ShapeDtypeStruct
    return pl.pallas_call(
        functools.partial(kernel_a, n_dp),
        out_shape=(
            sds((group, width), BF16),
            sds((3, heads, group, hd), BF16),
            sds((heads, tiles, TILE, span), BF16),
            sds((tiles, TILE, cols), BF16),
            sds((4, tok, cols), BF16),
            sds((4, cols, width), BF16),
            sds((n_dp * cap, width), BF16),
        ),
        in_specs=[VM] * 8 + [SM],
        out_specs=(ANY,) * 7,
        scratch_shapes=[
            pltpu.VMEM((group, width), BF16),
            pltpu.VMEM((3, heads, group, hd), BF16),
            pltpu.VMEM((heads, TILE, span), BF16),
            pltpu.VMEM((TILE, span), F32),
            pltpu.VMEM((tiles, TILE, cols), BF16),
            pltpu.VMEM((n_dp * cap, width), BF16),
            DMA((9,)), DMA((9,)), DMA((4,)), DMA((4,)), DMA((tiles,)), DMA((4, tok // TILE)),
            DMA((n_dp,)), DMA((n_dp,)), DMA((heads,)), DMA((4,)),
        ],
        compiler_params=pltpu.CompilerParams(collective_id=0, has_side_effects=True, vmem_limit_bytes=VMEM_LIMIT),
    )(x, g1, b1, w, qb, proj, routes, cot, lengths)


def local(
    block_input,
    norm1_gain,
    norm1_bias,
    qkv_weight,
    qkv_bias,
    proj_weight,
    proj_bias,
    norm2_gain,
    norm2_bias,
    router_weight,
    up_weight,
    up_bias,
    down_weight,
    down_bias,
    routes,
    lengths,
    cotangent,
):
    tok_rows, width = block_input.shape
    input_float = block_input.astype(jnp.float32)
    normed_one, scaled_one, inverse_one = normalize(input_float, norm1_gain, norm1_bias)
    num_experts = router_weight.shape[1]
    capacity = 2 * tok_rows // num_experts
    gathered, qkv_heads, kept_probs, context_tiles, context_full, proj_full, cot_slots = stage_a(
        num_experts, block_input, norm1_gain, norm1_bias, qkv_weight, qkv_bias, proj_weight, routes, cotangent, lengths, capacity
    )
    group_rows = gathered.shape[0]
    local_heads = qkv_bias.shape[1]
    head_size = qkv_bias.shape[2]
    local_cols = local_heads * head_size
    head_shape = (group_rows, local_heads, head_size)
    context = context_tiles.reshape(group_rows, local_cols)
    queries, keys_all, values_all = (qkv_heads[i].transpose(1, 0, 2) for i in range(3))
    positions = jnp.arange(group_rows, dtype=jnp.int32)
    seq_ends = jnp.cumsum(lengths[0])
    segment = jnp.sum((positions[:, None] >= seq_ends[None, :]).astype(jnp.int32), axis=1)
    block_rows = min(512, group_rows)
    blocks = group_rows // block_rows
    score_scale = head_size ** (-0.5)

    def block_scores(first_row):
        query_block = lax.dynamic_slice_in_dim(queries, first_row, block_rows, 0)
        seg_block = lax.dynamic_slice_in_dim(segment, first_row, block_rows, 0)
        pos_block = first_row + jnp.arange(block_rows, dtype=jnp.int32)
        allowed = (seg_block[:, None] == segment[None, :]) & (
            positions[None, :] <= pos_block[:, None]
        )
        scores = jnp.einsum("qhd,khd->hqk", query_block, keys_all, preferred_element_type=jnp.float32)
        return (query_block, jnp.where(allowed[None], scores, NEG_LARGE))

    attended = jnp.einsum("hrc,hcd->rd", context_full, proj_full, preferred_element_type=jnp.float32)
    residual = input_float + attended + proj_bias
    normed_two, scaled_two, inverse_two = normalize(residual, norm2_gain, norm2_bias)
    logits = jnp.dot(
        normed_two, router_weight, precision=HIGHEST, preferred_element_type=jnp.float32
    )
    probability = jax.nn.softmax(logits, axis=-1)
    expert_id = routes[:, 0]
    one_hot = (expert_id[:, None] == jnp.arange(num_experts, dtype=jnp.int32)[None, :]).astype(
        jnp.int32
    )
    slot_index = jnp.sum(jnp.cumsum(one_hot, axis=0) * one_hot, axis=1) - 1
    flat_index = expert_id * capacity + slot_index
    hot_float = one_hot.astype(jnp.float32)
    gate_value = jnp.sum(probability * hot_float, axis=1)
    fraction = jnp.mean(hot_float, axis=0)
    balance = num_experts * jnp.sum(fraction * jnp.mean(probability, axis=0))
    send_rows = (
        jnp.zeros((num_experts * capacity, width), jnp.bfloat16)
        .at[flat_index]
        .set(normed_two.astype(jnp.bfloat16))
    )
    received = lax.all_to_all(
        send_rows.reshape(num_experts, capacity, width),
        "dp",
        split_axis=0,
        concat_axis=0,
        tiled=True,
    )
    expert_rows = received.reshape(num_experts * capacity, width)
    preact_out = jnp.dot(expert_rows, up_weight[0], preferred_element_type=jnp.float32) + up_bias[0]
    hidden = jax.nn.gelu(preact_out, approximate=False).astype(jnp.bfloat16)
    produced = (
        jnp.dot(hidden, down_weight[0], preferred_element_type=jnp.float32) + down_bias[0]
    ).astype(jnp.bfloat16)
    returned = lax.all_to_all(
        produced.reshape(num_experts, capacity, width),
        "dp",
        split_axis=0,
        concat_axis=0,
        tiled=True,
    )
    expert_out = returned.reshape(num_experts * capacity, width)[flat_index].astype(jnp.float32)
    mixed = (residual + gate_value[:, None] * expert_out).astype(jnp.bfloat16)
    grad_out = cotangent.astype(jnp.float32)
    grad_gate = jnp.sum(grad_out * expert_out, axis=1)
    grad_produced = (gate_value[:, None] * grad_out).astype(jnp.bfloat16)
    send_gates = jnp.zeros((num_experts * capacity,), jnp.float32).at[flat_index].set(gate_value)
    gates_in = lax.all_to_all(
        send_gates.reshape(num_experts, capacity), "dp", split_axis=0, concat_axis=0, tiled=True
    )
    order = jnp.arange(num_experts, dtype=jnp.int32) ^ lax.axis_index("dp")
    cots_in = cot_slots.reshape(num_experts, capacity, width)[order]
    grads_in = (gates_in[:, :, None] * cots_in.astype(jnp.float32)).astype(jnp.bfloat16).reshape(num_experts * capacity, width)
    preact_back, hidden_back = (preact_out, hidden)
    grad_hidden = jnp.einsum(
        "rd,fd->rf", grads_in, down_weight[0], preferred_element_type=jnp.float32
    )
    down_grad = jnp.einsum("rf,rd->fd", hidden_back, grads_in, preferred_element_type=jnp.float32)
    down_bias_grad = jnp.sum(grads_in.astype(jnp.float32), axis=0)
    unused_value, gelu_pull = jax.vjp(
        lambda inner: jax.nn.gelu(inner, approximate=False), preact_back
    )
    grad_preact = gelu_pull(grad_hidden)[0].astype(jnp.bfloat16)
    up_grad = jnp.einsum("rd,rf->df", expert_rows, grad_preact, preferred_element_type=jnp.float32)
    up_bias_grad = jnp.sum(grad_preact.astype(jnp.float32), axis=0)
    grad_rows = jnp.einsum(
        "rf,df->rd", grad_preact, up_weight[0], preferred_element_type=jnp.float32
    ).astype(jnp.bfloat16)
    grads_back = lax.all_to_all(
        grad_rows.reshape(num_experts, capacity, width),
        "dp",
        split_axis=0,
        concat_axis=0,
        tiled=True,
    )
    grad_expert_in = grads_back.reshape(num_experts * capacity, width)[flat_index].astype(
        jnp.float32
    )
    up_sum, down_sum, up_bias_sum, down_bias_sum = (
        lax.psum_scatter(
            up_grad[None].astype(jnp.bfloat16), "head", scatter_dimension=2, tiled=True
        ).astype(jnp.float32),
        lax.psum_scatter(
            down_grad[None].astype(jnp.bfloat16), "head", scatter_dimension=1, tiled=True
        ).astype(jnp.float32),
        lax.psum_scatter(
            up_bias_grad[None].astype(jnp.bfloat16), "head", scatter_dimension=1, tiled=True
        ).astype(jnp.float32),
        lax.psum_scatter(
            down_bias_grad[None].astype(jnp.bfloat16), "head", scatter_dimension=1, tiled=True
        ).astype(jnp.float32),
    )
    grad_prob = (
        hot_float * grad_gate[:, None] + BAL_COEF * num_experts * fraction[None, :] / tok_rows
    )
    grad_logits = probability * (
        grad_prob - jnp.sum(probability * grad_prob, axis=1, keepdims=True)
    )
    grad_normed_two = grad_expert_in + jnp.einsum(
        "te,de->td",
        grad_logits,
        router_weight,
        precision=HIGHEST,
        preferred_element_type=jnp.float32,
    )
    router_grad = jnp.einsum(
        "td,te->de", normed_two, grad_logits, precision=HIGHEST, preferred_element_type=jnp.float32
    )
    gain_two_grad = jnp.sum(grad_normed_two * scaled_two, axis=0)
    bias_two_grad = jnp.sum(grad_normed_two, axis=0)
    grad_residual = grad_out + norm_backward(grad_normed_two, scaled_two, inverse_two, norm2_gain)
    proj_bias_grad = jnp.sum(grad_residual, axis=0)
    grad_local = grad_residual.astype(jnp.bfloat16)
    grad_attended = lax.all_gather(grad_local, "head", axis=0, tiled=True)
    proj_grad = jnp.einsum("tc,td->cd", context, grad_attended, preferred_element_type=jnp.float32)
    grad_context = (
        jnp.einsum("td,cd->tc", grad_attended, proj_weight, preferred_element_type=jnp.float32)
        .astype(jnp.bfloat16)
        .reshape(head_shape)
    )

    def attend_back(state_in, block_index):
        grad_keys, grad_values = state_in
        first_row = block_index * block_rows
        query_block, scores = block_scores(first_row)
        prob_block = jax.nn.softmax(scores, axis=-1)
        grad_ctx_block = lax.dynamic_slice_in_dim(grad_context, first_row, block_rows, 0)
        grad_prob_block = jnp.einsum(
            "qhd,khd->hqk", grad_ctx_block, values_all, preferred_element_type=jnp.float32
        )
        row_delta = jnp.sum(prob_block * grad_prob_block, axis=-1, keepdims=True)
        grad_scores = (prob_block * (grad_prob_block - row_delta)).astype(jnp.bfloat16)
        grad_query = (
            jnp.einsum("hqk,khd->qhd", grad_scores, keys_all, preferred_element_type=jnp.float32)
            * score_scale
        )
        grad_keys = (
            grad_keys
            + jnp.einsum(
                "hqk,qhd->khd", grad_scores, query_block, preferred_element_type=jnp.float32
            )
        )
        grad_values = grad_values + jnp.einsum(
            "hqk,qhd->khd",
            prob_block.astype(jnp.bfloat16),
            grad_ctx_block,
            preferred_element_type=jnp.float32,
        )
        return ((grad_keys, grad_values), grad_query.astype(jnp.bfloat16))

    zero_heads = jnp.zeros(head_shape, jnp.float32)
    (grad_keys_all, grad_values_all), grad_query_blocks = lax.scan(
        attend_back, (zero_heads, zero_heads), jnp.arange(blocks)
    )
    flat_shape = (group_rows, local_cols)
    grad_proj = jnp.stack(
        [
            grad_query_blocks.reshape(flat_shape),
            grad_keys_all.astype(jnp.bfloat16).reshape(flat_shape),
            grad_values_all.astype(jnp.bfloat16).reshape(flat_shape),
        ]
    )
    qkv_grad = jnp.einsum("td,cte->cde", gathered, grad_proj, preferred_element_type=jnp.float32)
    qkv_bias_grad = jnp.stack(
        [
            jnp.sum(grad_proj[0].astype(jnp.float32), axis=0),
            jnp.sum(grad_proj[2].astype(jnp.float32), axis=0),
        ]
    ).reshape(2, local_heads, head_size)
    piece = grad_proj
    grad_normed_one = lax.psum_scatter(
        jnp.einsum("cte,cde->td", piece, qkv_weight, preferred_element_type=jnp.float32).astype(
            jnp.bfloat16
        ),
        "head",
        scatter_dimension=0,
        tiled=True,
    ).astype(jnp.float32)
    gain_one_grad = jnp.sum(grad_normed_one * scaled_one, axis=0)
    bias_one_grad = jnp.sum(grad_normed_one, axis=0)
    input_grad = grad_residual + norm_backward(grad_normed_one, scaled_one, inverse_one, norm1_gain)
    qkv_sum, proj_sum, qkv_bias_sum = (
        lax.psum_scatter(
            qkv_grad.astype(jnp.bfloat16), "dp", scatter_dimension=1, tiled=True
        ).astype(jnp.float32),
        lax.psum_scatter(
            proj_grad.astype(jnp.bfloat16), "dp", scatter_dimension=1, tiled=True
        ).astype(jnp.float32),
        lax.psum_scatter(
            qkv_bias_grad.astype(jnp.bfloat16), "dp", scatter_dimension=2, tiled=True
        ).astype(jnp.float32),
    )
    gain_one_sum, bias_one_sum, proj_bias_sum, gain_two_sum, bias_two_sum, router_sum = (
        lax.psum_scatter(gain_one_grad, ("dp", "head"), scatter_dimension=0, tiled=True),
        lax.psum_scatter(bias_one_grad, ("dp", "head"), scatter_dimension=0, tiled=True),
        lax.psum_scatter(proj_bias_grad, ("dp", "head"), scatter_dimension=0, tiled=True),
        lax.psum_scatter(gain_two_grad, ("dp", "head"), scatter_dimension=0, tiled=True),
        lax.psum_scatter(bias_two_grad, ("dp", "head"), scatter_dimension=0, tiled=True),
        lax.psum_scatter(router_grad, ("dp", "head"), scatter_dimension=0, tiled=True),
    )
    return (
        mixed,
        balance.reshape(1),
        input_grad,
        gain_one_sum,
        bias_one_sum,
        qkv_sum,
        qkv_bias_sum,
        proj_sum,
        proj_bias_sum,
        gain_two_sum,
        bias_two_sum,
        router_sum,
        up_sum,
        up_bias_sum,
        down_sum,
        down_bias_sum,
    )


def solution(mesh):
    placed = (
        P(("dp", "head"), None),
        P(),
        P(),
        P(None, None, "head"),
        P(None, "head", None),
        P("head", None),
        P(),
        P(),
        P(),
        P(),
        P("dp", None, None),
        P("dp", None),
        P("dp", None, None),
        P("dp", None),
        P(("dp", "head"), None),
        P("dp", None),
        P(("dp", "head"), None),
    )
    return jax.shard_map(
        local,
        mesh=mesh,
        in_specs=placed,
        out_specs=(
            P(("dp", "head"), None),
            P(("dp", "head")),
            P(("dp", "head"), None),
            P(("dp", "head")),
            P(("dp", "head")),
            P(None, "dp", "head"),
            P(None, "head", "dp"),
            P("head", "dp"),
            P(("dp", "head")),
            P(("dp", "head")),
            P(("dp", "head")),
            P(("dp", "head"), None),
            P("dp", None, "head"),
            P("dp", "head"),
            P("dp", "head", None),
            P("dp", "head"),
        ),
        check_vma=False,
    )
```

```python
import functools
import jax
import jax.numpy as jnp
from jax import lax
from jax.experimental import pallas as pl
from jax.experimental.pallas import tpu as pltpu
from jax.sharding import PartitionSpec as P

EPSILON = 1e-05
BAL_COEF = 0.01
HIGHEST = lax.Precision.HIGHEST
NEG_LARGE = -1e30
MESH = pl.DeviceIdType.MESH
F32 = jnp.float32
BF16 = jnp.bfloat16
TILE = 256
VMEM_LIMIT = 60 << 20


def flip(index, bits):
    out, bit = index, 1
    while bit <= bits:
        if bits & bit:
            out = out + bit - 2 * bit * lax.rem(lax.div(index, bit), 2)
        bit *= 2
    return out


def remote(src, dst, send_sem, recv_sem, device):
    return pltpu.make_async_remote_copy(
        src_ref=src, dst_ref=dst, send_sem=send_sem, recv_sem=recv_sem, device_id=device, device_id_type=MESH
    )


def dot(left, right, dims=((1,), (0,)), precision=None):
    return lax.dot_general(left, right, (dims, ((), ())), precision=precision, preferred_element_type=F32)


def normalize(values, gain, bias):
    average = jnp.mean(values, axis=-1, keepdims=True)
    centred = values - average
    variance = jnp.mean(centred * centred, axis=-1, keepdims=True)
    inverse = lax.rsqrt(variance + EPSILON)
    scaled = centred * inverse
    return (scaled * gain + bias, scaled, inverse)


def norm_backward(grad_normed, scaled, inverse, gain):
    grad_scaled = grad_normed * gain
    first_mean = jnp.mean(grad_scaled, axis=-1, keepdims=True)
    second_mean = jnp.mean(grad_scaled * scaled, axis=-1, keepdims=True)
    return inverse * (grad_scaled - first_mean - scaled * second_mean)


def slot_layouts(routes, experts, cap):
    rows = routes.shape[1]
    count = max(8, experts)
    expert = lax.broadcasted_iota(jnp.int32, (count, rows), 0)
    hot = (routes == expert).astype(F32)
    upto = lax.broadcasted_iota(jnp.int32, (rows, rows), 0) <= lax.broadcasted_iota(jnp.int32, (rows, rows), 1)
    rank = dot(hot.astype(BF16), upto.astype(F32).astype(BF16))
    slot_row = jnp.sum((rank - 1.0) * hot, axis=0, keepdims=True)
    flat_row = jnp.sum((rank - 1.0 + cap * expert.astype(F32)) * hot, axis=0, keepdims=True)
    return hot, flat_row.astype(jnp.int32), slot_row.astype(jnp.int32)


def barrier_signal(peers):
    barrier = pltpu.get_barrier_semaphore()
    for peer in peers:
        pl.semaphore_signal(barrier, inc=1, device_id=peer, device_id_type=MESH)


def barrier_wait(count):
    pl.semaphore_wait(pltpu.get_barrier_semaphore(), count)


def kernel_a(
    n_dp, x_ref, g1_ref, b1_ref, w_ref, qb_ref, proj_ref, routes_ref, cot_ref, len_ref,
    gath_o, qkv_o, p_o, ctx_o, ctxf_o, projf_o, cots_o,
    gath, qkv, p_st, bias_s, ctx_s, disp,
    ag_s, ag_r, pj_s, pj_r, cx_s, cx_r, ct_s, ct_r, p_sem, loc,
):
    tok, width = x_ref.shape
    heads = qb_ref.shape[0]
    hd = qb_ref.shape[2]
    group = 4 * tok
    tiles = group // TILE
    reach = group // 2 // TILE + 1
    cap = cots_o.shape[0] // n_dp
    d = lax.axis_index("dp")
    h = lax.axis_index("head")
    barrier_signal([(d, flip(h, k)) for k in (1, 2, 3)] + [(flip(d, r), h) for r in range(1, n_dp)])

    normed, _, _ = normalize(x_ref[...].astype(F32), g1_ref[...][None, :], b1_ref[...][None, :])

    def block(index):
        return pl.ds(pl.multiple_of(index * tok, tok), tok)

    gath[block(h), :] = normed.astype(BF16)
    barrier_wait(3 + n_dp - 1)

    chunks = 4
    step = tok // chunks

    def part(index, i):
        return gath.at[pl.ds(pl.multiple_of(index * tok + i * step, step), step), :]

    sib, cross, diag = flip(h, 1), flip(h, 2), flip(h, 3)
    to_cross = [remote(part(h, i), part(h, i), ag_s.at[i], ag_r.at[i], (d, cross)) for i in range(chunks)]
    to_sib = remote(gath.at[block(h), :], gath.at[block(h), :], ag_s.at[2 * chunks], ag_r.at[2 * chunks], (d, sib))
    onward = [
        remote(part(cross, i), part(cross, i), ag_s.at[chunks + i], ag_r.at[chunks + i], (d, sib)) for i in range(chunks)
    ]
    for copy in to_cross:
        copy.start()
    to_sib.start()
    proj_copies = [
        remote(proj_ref, projf_o.at[h], pj_s.at[k], pj_r.at[k], (d, flip(h, k))) for k in (1, 2, 3)
    ]

    hot_t, flat_row, slot_row = slot_layouts(routes_ref[...], n_dp, cap)
    slot_iota = lax.broadcasted_iota(jnp.int32, (cap, tok), 0)

    def dispatch(e, carry):
        hot = (flat_row == slot_iota + e * cap).astype(F32).astype(BF16)
        disp[pl.ds(pl.multiple_of(e * cap, cap), cap), :] = dot(hot, cot_ref[...]).astype(BF16)
        return carry

    lax.fori_loop(0, n_dp, dispatch, 0)

    def slots(index):
        return pl.ds(pl.multiple_of(index * cap, cap), cap)

    cot_copies = [
        remote(disp.at[slots(flip(d, r)), :], cots_o.at[pl.ds(r * cap, cap), :], ct_s.at[r], ct_r.at[r], (flip(d, r), h))
        for r in range(1, n_dp)
    ]
    for copy in cot_copies:
        copy.start()
    cot_own = pltpu.make_async_copy(disp.at[slots(d), :], cots_o.at[pl.ds(0, cap), :], ct_s.at[0])
    cot_own.start()

    def project(index):
        rows = gath[block(index), :]
        for c in range(3):
            out = dot(rows, w_ref[c], ((1,), (1,)))
            for a in range(heads):
                piece = out[:, a * hd : (a + 1) * hd]
                if c != 1:
                    piece = piece + qb_ref[a, c // 2 : c // 2 + 1, :]
                piece = piece.astype(BF16)
                if c == 0:
                    piece = piece * jnp.asarray(hd ** (-0.5), BF16)
                qkv[c, a, block(index), :] = piece

    project(h)
    to_sib.wait_recv()
    project(sib)
    for i in range(chunks):
        to_cross[i].wait_recv()
        onward[i].start()
    for copy in proj_copies:
        copy.start()
    proj_own = pltpu.make_async_copy(proj_ref, projf_o.at[h], loc.at[0])
    proj_own.start()
    project(cross)
    for i in range(chunks):
        onward[i].wait_recv()
    project(diag)
    gath_copy = pltpu.make_async_copy(gath, gath_o, loc.at[1])
    gath_copy.start()
    qkv_copy = pltpu.make_async_copy(qkv, qkv_o, loc.at[2])
    qkv_copy.start()

    ends = [len_ref[0, 0]]
    for i in range(1, len_ref.shape[1] - 1):
        ends.append(ends[-1] + len_ref[0, i])

    order = []
    for i in range(tiles // 2):
        order += [tiles - 1 - i, tiles // 2 - 1 - i]
    per_block = tok // TILE

    def p_copy(t, a):
        size = min(t + 1, reach) * TILE
        return pltpu.make_async_copy(p_st.at[a, :, pl.ds(0, size)], p_o.at[a, t, :, pl.ds(0, size)], p_sem.at[a])

    previous = None
    for t in order:
        size = min(t + 1, reach) * TILE
        first = (t + 1) * TILE - size
        row = t * TILE + lax.broadcasted_iota(jnp.int32, (TILE, 1), 0)
        start = jnp.zeros((TILE, 1), jnp.int32)
        for end in ends:
            start = jnp.where(row >= end, end, start)
        col = first + lax.broadcasted_iota(jnp.int32, (TILE, size), 1)
        bias_s[:, :size] = jnp.where((col >= start) & (col <= row), 0.0, NEG_LARGE)
        outs = []
        for a in range(heads):
            q = qkv[0, a, t * TILE : (t + 1) * TILE, :]
            k = qkv[1, a, first : (t + 1) * TILE, :]
            v = qkv[2, a, first : (t + 1) * TILE, :]
            s = dot(q, k, ((1,), (1,))) + bias_s[:, :size]
            top = jnp.max(s, axis=1, keepdims=True)
            e = jnp.exp(s - top)
            total = jnp.sum(e, axis=1, keepdims=True)
            p = (e * (1.0 / total)).astype(BF16)
            if previous is not None:
                p_copy(previous, a).wait()
            p_st[a, :, :size] = p
            p_copy(t, a).start()
            outs.append(dot(p, v))
        ctx_s[t] = jnp.concatenate(outs, axis=1).astype(BF16)
        previous = t
        owner, sub = t // per_block, t % per_block
        rows = pl.ds(sub * TILE, TILE)

        @pl.when(h != owner)
        def _():
            remote(ctx_s.at[t], ctxf_o.at[h, rows, :], cx_s.at[t], cx_r.at[h, sub], (d, owner)).start()

        @pl.when(h == owner)
        def _():
            pltpu.make_async_copy(ctx_s.at[t], ctxf_o.at[h, rows, :], cx_s.at[t]).start()

    ctx_copy = pltpu.make_async_copy(ctx_s, ctx_o, loc.at[3])
    ctx_copy.start()
    for a in range(heads):
        p_copy(previous, a).wait()
    for t in range(tiles):
        owner, sub = t // per_block, t % per_block
        rows = pl.ds(sub * TILE, TILE)

        @pl.when(h != owner)
        def _():
            remote(ctx_s.at[t], ctxf_o.at[h, rows, :], cx_s.at[t], cx_r.at[h, sub], (d, owner)).wait_send()

        @pl.when(h == owner)
        def _():
            pltpu.make_async_copy(ctx_s.at[t], ctxf_o.at[h, rows, :], cx_s.at[t]).wait()

    for k in (1, 2, 3):
        peer = flip(h, k)
        for sub in range(per_block):
            remote(
                ctx_s.at[0], ctxf_o.at[peer, pl.ds(sub * TILE, TILE), :], cx_s.at[0], cx_r.at[peer, sub], (d, peer)
            ).wait_recv()
    for copy in to_cross:
        copy.wait_send()
    to_sib.wait_send()
    for copy in onward:
        copy.wait_send()
    for k in (1, 2, 3):
        proj_copies[k - 1].wait_send()
        peer = flip(h, k)
        remote(proj_ref, projf_o.at[peer], pj_s.at[k], pj_r.at[k], (d, peer)).wait_recv()
    for copy in cot_copies:
        copy.wait()
    for copy in (cot_own, proj_own, gath_copy, qkv_copy, ctx_copy):
        copy.wait()


VM = pl.BlockSpec(memory_space=pltpu.VMEM)
SM = pl.BlockSpec(memory_space=pltpu.SMEM)
ANY = pl.BlockSpec(memory_space=pl.ANY)
DMA = pltpu.SemaphoreType.DMA


def stage_a(n_dp, x, g1, b1, w, qb, proj, routes, cot, lengths, cap):
    tok, width = x.shape
    heads, hd = qb.shape[1:]
    w, qb, routes = w.transpose(0, 2, 1), qb.transpose(1, 0, 2), routes.T
    group = 4 * tok
    tiles = group // TILE
    span = (group // 2 // TILE + 1) * TILE
    cols = heads * hd
    sds = jax.ShapeDtypeStruct
    return pl.pallas_call(
        functools.partial(kernel_a, n_dp),
        out_shape=(
            sds((group, width), BF16),
            sds((3, heads, group, hd), BF16),
            sds((heads, tiles, TILE, span), BF16),
            sds((tiles, TILE, cols), BF16),
            sds((4, tok, cols), BF16),
            sds((4, cols, width), BF16),
            sds((n_dp * cap, width), BF16),
        ),
        in_specs=[VM] * 8 + [SM],
        out_specs=(ANY,) * 7,
        scratch_shapes=[
            pltpu.VMEM((group, width), BF16),
            pltpu.VMEM((3, heads, group, hd), BF16),
            pltpu.VMEM((heads, TILE, span), BF16),
            pltpu.VMEM((TILE, span), F32),
            pltpu.VMEM((tiles, TILE, cols), BF16),
            pltpu.VMEM((n_dp * cap, width), BF16),
            DMA((9,)), DMA((9,)), DMA((4,)), DMA((4,)), DMA((tiles,)), DMA((4, tok // TILE)),
            DMA((n_dp,)), DMA((n_dp,)), DMA((heads,)), DMA((4,)),
        ],
        compiler_params=pltpu.CompilerParams(collective_id=0, has_side_effects=True, vmem_limit_bytes=VMEM_LIMIT),
    )(x, g1, b1, w, qb, proj, routes, cot, lengths)


def far_first(n_dp):
    half = n_dp // 2
    return list(range(half, n_dp)) + [r for r in range(2, half)] + [1]


def gelu_parts(u):
    density = jnp.exp(u * u * -0.5)
    t = 1.0 / (1.0 + jnp.abs(u) * (0.3275911 * 0.7071067811865476))
    poly = ((((1.061405429 * t - 1.453152027) * t + 1.421413741) * t - 0.284496736) * t + 0.254829592) * t
    tail = 0.5 * poly * density
    return jnp.where(u < 0.0, tail, 1.0 - tail), density * 0.3989422804014327


def row_to_col(row):
    return jnp.broadcast_to(row, (128, row.shape[1])).T[:, :1]


def col_to_rows(col):
    return jnp.broadcast_to(col, (col.shape[0], 128)).T[:8]


def kernel_m(
    n_dp, x_ref, ctxf, projf, pb_ref, g2_ref, b2_ref, rt_ref, routes_ref, cot_ref, cots, up_h, upb_ref, down_h, downb_ref,
    res_o, gate_o, prod_o, gres_o, gctx_o, upc_o, upo_o, dng_o, sm_o, bg_o, bal_o,
    res, stat, disp, gsend, rows, grecv, up, down, ghu, hid, gg, gacc, gin, ggs, ginr, ggr, dsend, dacc, drecv, urecv,
    ld, ra_s, ra_r, ga_s, ga_r, rb_s, rb_r, gb_s, gb_r, ds_s, ds_r, us_s, us_r, out_sem,
):
    tok, width = x_ref.shape
    ff = up.shape[1]
    slots = rows.shape[0]
    cap = slots // n_dp
    per = TILE // cap
    groups = slots // TILE
    experts = n_dp
    quarter = ff // 4
    d = lax.axis_index("dp")
    h = lax.axis_index("head")
    sib, cross = (d, flip(h, 1)), (d, flip(h, 2))
    loads = [pltpu.make_async_copy(down_h.at[0], down, ld.at[0]), pltpu.make_async_copy(up_h.at[0], up, ld.at[1])]
    for copy in loads:
        copy.start()
    barrier_signal([(d, flip(h, k)) for k in (1, 2, 3)] + [(flip(d, r), h) for r in range(1, n_dp)])

    attended = dot(ctxf[0], projf[0])
    for b in range(1, 4):
        attended += dot(ctxf[b], projf[b])
    residual = x_ref[...].astype(F32) + attended + pb_ref[...][None, :]
    res[...] = residual
    average = jnp.mean(residual, axis=-1, keepdims=True)
    centred = residual - average
    inverse = lax.rsqrt(jnp.mean(centred * centred, axis=-1, keepdims=True) + EPSILON)
    stat[0] = average
    stat[1] = inverse
    gain, bias = g2_ref[...][None, :], b2_ref[...][None, :]
    normed = centred * inverse * gain + bias
    logits = dot(rt_ref[...], normed, ((1,), (1,)), HIGHEST)
    raised = jnp.exp(logits - jnp.max(logits, axis=0, keepdims=True))
    prob = raised / jnp.sum(raised, axis=0, keepdims=True)
    hot, flat_row, slot_row = slot_layouts(routes_ref[...], experts, cap)
    hot = hot[:experts]
    gate_row = jnp.sum(prob * hot, axis=0, keepdims=True)
    gate_o[...] = row_to_col(gate_row)
    fraction = jnp.mean(hot, axis=1, keepdims=True)
    bal_o[...] = experts * jnp.sum(fraction * jnp.mean(prob, axis=1, keepdims=True), axis=0, keepdims=True)

    expert_row = jnp.sum(hot * lax.broadcasted_iota(jnp.int32, hot.shape, 0).astype(F32), axis=0, keepdims=True)
    other_row = jnp.bitwise_xor(expert_row.astype(jnp.int32), d)
    flat_x = other_row * cap + slot_row
    at_slot = (slot_row == lax.broadcasted_iota(jnp.int32, (128, tok), 0)).astype(F32)
    other_hot = (other_row == lax.broadcasted_iota(jnp.int32, (max(8, n_dp), tok), 0)).astype(F32)
    gates = dot(other_hot * gate_row, at_slot, ((1,), (1,)), HIGHEST)
    normed_low = normed.astype(BF16)
    barrier_wait(3 + n_dp - 1)
    order = far_first(n_dp)

    def send_rows(r):
        return remote(disp.at[pl.ds(r * cap, cap), :], rows.at[pl.ds(r * cap, cap), :], ra_s.at[r], ra_r.at[r], (flip(d, r), h))

    def send_gate(r):
        return remote(gsend.at[r], grecv.at[r], ga_s.at[r], ga_r.at[r], (flip(d, r), h))

    slot_iota = lax.broadcasted_iota(jnp.int32, (cap, tok), 0)
    for r in order + [0]:
        hits = (flat_x == slot_iota + r * cap).astype(F32).astype(BF16)
        block = dot(hits, normed_low).astype(BF16)
        gsend[r] = jnp.broadcast_to(gates[r : r + 1], (8, 128))
        if r:
            disp[r * cap : (r + 1) * cap, :] = block
            send_rows(r).start()
            send_gate(r).start()
        else:
            rows[:cap, :] = block
            grecv[0] = gsend[0]

    loads[0].wait()

    def hidden_grad(i, carry):
        at = pl.ds(pl.multiple_of(lax.div(i, 4) * TILE, TILE), TILE)
        cols = pl.ds(pl.multiple_of(lax.rem(i, 4) * quarter, quarter), quarter)
        ghu[at, cols] = dot(cots[at, :], down[cols, :], ((1,), (1,))).astype(BF16)
        return carry

    lax.fori_loop(0, 4 * groups, hidden_grad, 0)
    loads[1].wait()

    step = 512

    def send_back(r):
        return remote(gin.at[pl.ds(r * cap, cap), :], ginr.at[pl.ds(r * cap, cap), :], rb_s.at[r], rb_r.at[r], (flip(d, r), h))

    def send_gg(r):
        return remote(ggs.at[r // per], ggr.at[r], gb_s.at[r], gb_r.at[r], (flip(d, r), h))

    for g in range(groups):
        mine = [r for r in range(g * per, (g + 1) * per)]
        for r in mine:
            if r:
                send_rows(r).wait_recv()
                send_gate(r).wait_recv()
        at = slice(g * TILE, (g + 1) * TILE)
        gate = jnp.concatenate([grecv[r].T[:cap, :1] for r in mine], axis=0)
        gacc[...] = jnp.zeros_like(gacc)
        gg[...] = jnp.zeros_like(gg)

        def expert(f, carry):
            cols = pl.ds(pl.multiple_of(f * step, step), step)
            u = dot(rows[at, :], up[:, cols]) + upb_ref[:, cols]
            share, density = gelu_parts(u)
            out = u * share
            low = out.astype(BF16)
            back = ghu[at, cols].astype(F32)
            hid[at, cols] = low
            meet = low.astype(F32) * back
            folded = meet[:, :128]
            for j in range(1, step // 128):
                folded += meet[:, j * 128 : (j + 1) * 128]
            gg[...] += folded
            pre = (gate * back * (share + u * density)).astype(BF16)
            ghu[at, cols] = pre
            gacc[...] += dot(pre, up[:, cols], ((1,), (1,)))
            return carry

        lax.fori_loop(0, ff // step, expert, 0)
        cot_g = cots[at, :].astype(F32)
        gg_col = jnp.sum(gg[...], axis=1, keepdims=True) + jnp.sum(cot_g * downb_ref[...], axis=1, keepdims=True)
        ggs[g] = col_to_rows(gg_col)
        if g == 0:
            gin[at, :] = gacc[...].astype(BF16)
            ginr[:cap, :] = gin[:cap, :]
            ggr[0] = ggs[0]
        else:
            gin[at, :] = gacc[...].astype(BF16)
        for r in mine:
            if r:
                send_back(r).start()
                send_gg(r).start()
        cots[at, :] = (gate * cot_g).astype(BF16)

    third = quarter // 3

    def block_cols(index):
        return pl.ds(pl.multiple_of(index * quarter, quarter), quarter)

    def down_block(index, put):
        def body(i, carry):
            cols = pl.ds(pl.multiple_of(index * quarter + i * third, third), third)
            put(pl.ds(pl.multiple_of(i * third, third), third), dot(hid[:, cols], cots[...], ((0,), (0,))))
            return carry

        lax.fori_loop(0, 3, body, 0)

    def up_block(index, put):
        part = width // 3

        def body(i, carry):
            cols = pl.ds(pl.multiple_of(i * part, part), part)
            put(cols, dot(rows[:, cols], ghu[:, block_cols(index)], ((0,), (0,))))
            return carry

        lax.fori_loop(0, 3, body, 0)

    def store(ref, kind):
        def put(at, value):
            ref[at, :] = value.astype(kind)

        return put

    down_sib = [remote(dsend.at[i], drecv.at[i], ds_s.at[i], ds_r.at[i], sib) for i in range(2)]
    down_cross = remote(dacc, drecv.at[2], ds_s.at[2], ds_r.at[2], cross)
    up_sib = [remote(dsend.at[i], urecv.at[i], us_s.at[i], us_r.at[i], sib) for i in range(2)]
    down_block(flip(h, 3), store(dsend.at[1], BF16))
    down_sib[1].start()
    down_block(flip(h, 1), store(dsend.at[0], BF16))
    down_sib[0].start()
    down_block(flip(h, 2), store(dacc, BF16))
    down_sib[1].wait_recv()
    dacc[...] = (dacc[...].astype(F32) + drecv[1].astype(F32)).astype(BF16)
    down_cross.start()
    for r in order:
        send_rows(r).wait_send()

    def produce(i, carry):
        at = pl.ds(pl.multiple_of(i * TILE, TILE), TILE)
        disp[at, :] = (dot(hid[at, :], down[...]) + downb_ref[...]).astype(BF16)
        return carry

    lax.fori_loop(0, groups, produce, 0)
    prod_copy = pltpu.make_async_copy(disp, prod_o, out_sem.at[0])
    prod_copy.start()
    res_copy = pltpu.make_async_copy(res, res_o, out_sem.at[1])
    res_copy.start()
    for copy in down_sib:
        copy.wait_send()
    up_block(flip(h, 3), store(dsend.at[1], BF16))
    up_sib[1].start()
    up_block(flip(h, 1), store(dsend.at[0], BF16))
    up_sib[0].start()
    up_block(flip(h, 2), store(upc_o, BF16))
    up_block(h, store(upo_o, F32))
    down_block(h, store(dng_o, F32))
    ones = jnp.ones((8, slots), BF16)
    up_bias = dot(ones, ghu[...])
    down_bias = dot(ones, cots[...])
    short = width // 4
    for b in range(4):
        bg_o[b, 0:1, :] = up_bias[:1, b * quarter : (b + 1) * quarter]
        bg_o[b, 1:2, :short] = down_bias[:1, b * short : (b + 1) * short]
    up_sib[1].wait_recv()
    upc_o[...] = (upc_o[...].astype(F32) + urecv[1].astype(F32)).astype(BF16)
    up_sib[0].wait_recv()
    upo_o[...] = upo_o[...] + urecv[0].astype(F32)
    down_sib[0].wait_recv()
    dng_o[...] = dng_o[...] + drecv[0].astype(F32)

    flat_col = row_to_col(flat_x.astype(F32)).astype(jnp.int32)
    pick = (flat_col == lax.broadcasted_iota(jnp.int32, (tok, slots), 1)).astype(F32).astype(BF16)
    for r in order:
        send_back(r).wait_recv()
        send_gg(r).wait_recv()
    gin_tok = dot(pick, ginr[...])
    slot_gg = [ggr[r][:1, (r % per) * cap : (r % per) * cap + cap] for r in range(n_dp)]
    slot_gg = jnp.concatenate(slot_gg + [jnp.zeros_like(slot_gg[0])] * (max(8, n_dp) - n_dp), axis=0)
    grad_gate = jnp.sum(dot(slot_gg, at_slot[:cap], precision=HIGHEST) * other_hot, axis=0, keepdims=True)
    grad_prob = hot * grad_gate + (BAL_COEF * experts / tok) * fraction
    grad_logits = prob * (grad_prob - jnp.sum(prob * grad_prob, axis=0, keepdims=True))
    average, inverse = stat[0], stat[1]
    scaled = (res[...] - average) * inverse
    normed = scaled * gain + bias
    padded = jnp.concatenate([grad_logits, jnp.zeros((128 - experts, tok), F32)], axis=0)
    logits_col = padded.T[:, :experts]
    grad_normed = gin_tok + dot(logits_col, rt_ref[...], precision=HIGHEST)
    grad_res = cot_ref[...].astype(F32) + norm_backward(grad_normed, scaled, inverse, gain)
    gres_o[...] = grad_res
    sm_o[...] = jnp.zeros_like(sm_o)
    sm_o[0:1, :] = jnp.sum(grad_normed * scaled, axis=0, keepdims=True)
    sm_o[1:2, :] = jnp.sum(grad_normed, axis=0, keepdims=True)
    sm_o[2:3, :] = jnp.sum(grad_res, axis=0, keepdims=True)
    sm_o[8 : 8 + experts, :] = dot(grad_logits, normed, precision=HIGHEST)
    low = grad_res.astype(BF16)
    for b in range(4):
        gctx_o[b] = dot(low, projf[b], ((1,), (1,))).astype(BF16)

    down_cross.wait_recv()
    dng_o[...] = dng_o[...] + drecv[2].astype(F32)
    down_cross.wait_send()
    for copy in up_sib:
        copy.wait_send()
    for r in order:
        send_gate(r).wait_send()
        send_back(r).wait_send()
        send_gg(r).wait_send()
    prod_copy.wait()
    res_copy.wait()


def stage_m(n_dp, x, ctxf, projf, pb, g2, b2, router, routes, cot, cots, up, upb, down, downb):
    tok, width = x.shape
    slots = cots.shape[0]
    ff = up.shape[2]
    cols = ctxf.shape[2]
    cap = slots // n_dp
    groups = slots // TILE
    quarter = ff // 4
    sds = jax.ShapeDtypeStruct
    return pl.pallas_call(
        functools.partial(kernel_m, n_dp),
        out_shape=(
            sds((tok, width), F32),
            sds((tok, 1), F32),
            sds((slots, width), BF16),
            sds((tok, width), F32),
            sds((4, tok, cols), BF16),
            sds((width, quarter), BF16),
            sds((width, quarter), F32),
            sds((quarter, width), F32),
            sds((8 + max(8, n_dp), width), F32),
            sds((4, 8, quarter), F32),
            sds((1, 1), F32),
        ),
        in_specs=[VM] * 10 + [ANY, VM, ANY, VM],
        out_specs=(ANY, VM, ANY) + (VM,) * 8,
        scratch_shapes=[
            pltpu.VMEM((tok, width), F32),
            pltpu.VMEM((2, tok, 1), F32),
            pltpu.VMEM((slots, width), BF16),
            pltpu.VMEM((n_dp, 8, 128), F32),
            pltpu.VMEM((slots, width), BF16),
            pltpu.VMEM((n_dp, 8, 128), F32),
            pltpu.VMEM((width, ff), BF16),
            pltpu.VMEM((ff, width), BF16),
            pltpu.VMEM((slots, ff), BF16),
            pltpu.VMEM((slots, ff), BF16),
            pltpu.VMEM((TILE, 128), F32),
            pltpu.VMEM((TILE, width), F32),
            pltpu.VMEM((slots, width), BF16),
            pltpu.VMEM((groups, 8, TILE), F32),
            pltpu.VMEM((slots, width), BF16),
            pltpu.VMEM((n_dp, 8, TILE), F32),
            pltpu.VMEM((2, quarter, width), BF16),
            pltpu.VMEM((quarter, width), BF16),
            pltpu.VMEM((3, quarter, width), BF16),
            pltpu.VMEM((2, width, quarter), BF16),
            DMA((2,)), DMA((n_dp,)), DMA((n_dp,)), DMA((n_dp,)), DMA((n_dp,)), DMA((n_dp,)), DMA((n_dp,)),
            DMA((n_dp,)), DMA((n_dp,)), DMA((3,)), DMA((3,)), DMA((2,)), DMA((2,)), DMA((2,)),
        ],
        compiler_params=pltpu.CompilerParams(collective_id=1, has_side_effects=True, vmem_limit_bytes=VMEM_LIMIT),
    )(x, ctxf, projf, pb, g2, b2, router.T, routes.T, cot, cots, up, upb, down, downb)


def kernel_b(
    n_dp, gctx, qkv_h, p_h, ctx, ctxf, gath_h, w_ref, x_ref, g1_ref, b1_ref, gres, prod_h, upc_h, sm_ref, bg_ref,
    igrad_o, prodr_o, upr_o, qg_o, pg_o, qb_o, sums_o, ends_o, bgs_o,
    gcr, qkv, p_v, gath, dk, dv, grads, gsend, gacc, grecv, qg, qgr, pg, pgr, pacc, qb, qbr, smr, smd, smt, en, enr, ent, enq, bgr,
    ld, p_sem, gc_s, gc_r, pr_s, pr_r, uc_s, uc_r, gn_s, gn_r, qg_s, qg_r, pg_s, pg_r, pt_s, pt_r, qb_s, qb_r,
    sh_s, sh_r, sd_s, sd_r, eh_s, eh_r, ed_s, ed_r, bg_s, bg_r,
):
    tok, width = x_ref.shape
    heads, group, hd = qkv.shape[1:]
    cols = heads * hd
    tiles = group // TILE
    reach = group // 2 // TILE + 1
    per_block = tok // TILE
    slots = prod_h.shape[0]
    cap = slots // n_dp
    share = width // n_dp
    d = lax.axis_index("dp")
    h = lax.axis_index("head")
    sib, cross = (d, flip(h, 1)), (d, flip(h, 2))
    order = far_first(n_dp)

    def at_head(k):
        return (d, flip(h, k))

    def at_dp(r):
        return (flip(d, r), h)

    def p_load(t, slot):
        size = min(t + 1, reach) * TILE
        return pltpu.make_async_copy(p_h.at[:, t, :, pl.ds(0, size)], p_v.at[slot, :, :, pl.ds(0, size)], p_sem.at[slot])

    load_qkv = pltpu.make_async_copy(qkv_h, qkv, ld.at[0])
    load_qkv.start()
    barrier_signal([at_head(k) for k in (1, 2, 3)] + [at_dp(r) for r in range(1, n_dp)])
    load_gath = pltpu.make_async_copy(gath_h, gath, ld.at[1])
    dk[...] = jnp.zeros_like(dk)
    dv[...] = jnp.zeros_like(dv)
    barrier_wait(3 + n_dp - 1)

    def send_ctx(k):
        return remote(gctx.at[flip(h, k)], gcr.at[h], gc_s.at[k], gc_r.at[k], at_head(k))

    for k in (2, 3, 1):
        send_ctx(k).start()

    def send_prod(r):
        rows = pl.ds(r * cap, cap)
        return remote(prod_h.at[rows, :], prodr_o.at[rows, :], pr_s.at[r], pr_r.at[r], at_dp(r))

    for r in order:
        send_prod(r).start()
    prod_own = pltpu.make_async_copy(prod_h.at[pl.ds(0, cap), :], prodr_o.at[pl.ds(0, cap), :], pr_s.at[0])
    prod_own.start()
    gcr[h] = gctx[h]

    sm_head = [remote(sm_ref, smr.at[k], sh_s.at[k], sh_r.at[k], at_head(k)) for k in (1, 2, 3)]
    for copy in sm_head:
        copy.start()
    bg_head = [remote(bg_ref.at[flip(h, k)], bgr.at[k], bg_s.at[k], bg_r.at[k], at_head(k)) for k in (1, 2, 3)]
    for copy in bg_head:
        copy.start()

    low = gres[...].astype(BF16)

    def proj_block(index):
        return dot(low, ctxf[index], ((0,), (0,))).astype(BF16)

    pg[1] = proj_block(flip(h, 3))
    pg[0] = proj_block(flip(h, 1))
    pg_sib = [remote(pg.at[i], pgr.at[i], pg_s.at[i], pg_r.at[i], sib) for i in range(2)]
    for copy in pg_sib:
        copy.start()
    pg[2] = proj_block(flip(h, 2))
    pacc[...] = dot(low, ctxf[h], ((0,), (0,)))
    pg_cross = remote(pg.at[2], pgr.at[2], pg_s.at[2], pg_r.at[2], cross)

    up_cross = remote(upc_h, upr_o, uc_s.at[0], uc_r.at[0], cross)
    load_qkv.wait()

    def wait_block(b):
        for k in (1, 2, 3):

            @pl.when(flip(h, k) == b)
            def _():
                remote(gctx.at[0], gcr.at[b], gc_s.at[k], gc_r.at[k], at_head(k)).wait_recv()

    def attention(sequence):
        for i, t in enumerate(sequence[:2]):
            p_load(t, i).start()
        for i, t in enumerate(sequence):
            slot = i % 3
            if i + 2 < tiles:
                p_load(sequence[i + 2], (i + 2) % 3).start()
            b, sub = t // per_block, t % per_block
            if sub == 0:
                wait_block(b)
            p_load(t, slot).wait()
            size = min(t + 1, reach) * TILE
            first = (t + 1) * TILE - size
            grad = gcr[b, sub * TILE : (sub + 1) * TILE, :]
            meet = grad.astype(F32) * ctx[t].astype(F32)
            outs = []
            for a in range(heads):
                g = grad[:, a * hd : (a + 1) * hd]
                delta = jnp.sum(meet[:, a * hd : (a + 1) * hd], axis=1, keepdims=True)
                q = qkv[0, a, t * TILE : (t + 1) * TILE, :]
                k = qkv[1, a, first : (t + 1) * TILE, :]
                v = qkv[2, a, first : (t + 1) * TILE, :]
                p = p_v[slot, a, :, :size]
                ds = (p.astype(F32) * (dot(g, v, ((1,), (1,))) - delta)).astype(BF16)
                outs.append(dot(ds, k) * (hd ** (-0.5)))
                dk[a, first : (t + 1) * TILE, :] += dot(ds, q, ((0,), (0,)))
                dv[a, first : (t + 1) * TILE, :] += dot(p, g, ((0,), (0,)))
            grads[0, t * TILE : (t + 1) * TILE, :] = jnp.concatenate(outs, axis=1).astype(BF16)
            if i == 3:
                up_cross.start()

    half = tiles // 2

    @pl.when(h < 2)
    def _():
        attention(list(range(tiles)))

    @pl.when(h >= 2)
    def _():
        attention(list(range(half, tiles)) + list(range(half)))

    load_gath.start()
    for t in range(tiles):
        rows = slice(t * TILE, (t + 1) * TILE)
        grads[1, rows, :] = jnp.concatenate([dk[a, rows, :] for a in range(heads)], axis=1).astype(BF16)
        grads[2, rows, :] = jnp.concatenate([dv[a, rows, :] for a in range(heads)], axis=1).astype(BF16)

    def normed_block(index):
        at = pl.ds(pl.multiple_of(index * tok, tok), tok)
        total = dot(grads[0, at, :], w_ref[0])
        for c in (1, 2):
            total += dot(grads[c, at, :], w_ref[c])
        return total

    gn_sib = [remote(gsend.at[i], grecv.at[i], gn_s.at[i], gn_r.at[i], sib) for i in range(2)]
    gn_cross = remote(gacc, grecv.at[2], gn_s.at[2], gn_r.at[2], cross)
    gsend[1] = normed_block(flip(h, 3)).astype(BF16)
    gn_sib[1].start()
    mine = normed_block(flip(h, 2))
    gn_sib[1].wait_recv()
    gacc[...] = (mine + grecv[1].astype(F32)).astype(BF16)
    gn_cross.start()
    gsend[0] = normed_block(flip(h, 1)).astype(BF16)
    gn_sib[0].start()

    pg_sib[1].wait_recv()
    pg_sib[0].wait_recv()
    pg_sib[1].wait_send()
    for copy in sm_head:
        copy.wait_recv()
    smt[...] = sm_ref[...] + smr[1] + smr[2] + smr[3]
    sm_dp = [remote(smt, smd.at[r], sd_s.at[r], sd_r.at[r], at_dp(r)) for r in range(1, n_dp)]
    for copy in sm_dp:
        copy.start()
    pg[2] = (pg[2].astype(F32) + pgr[1].astype(F32)).astype(BF16)
    pg_cross.start()

    load_gath.wait()
    part = width // 3
    for c in range(3):
        for i in range(3):
            at = slice(i * part, (i + 1) * part)
            qg[c, at, :] = dot(gath[:, at], grads[c], ((0,), (0,))).astype(BF16)
    ones = jnp.ones((8, group), BF16)
    qb[...] = jnp.concatenate([dot(ones, grads[0]), dot(ones, grads[2])], axis=1)

    def send_qg(r):
        src = qg.at[:, pl.ds(pl.multiple_of(flip(d, r) * share, share), share), :]
        return remote(src, qgr.at[r], qg_s.at[r], qg_r.at[r], at_dp(r))

    def send_qb(r):
        return remote(qb, qbr.at[r], qb_s.at[r], qb_r.at[r], at_dp(r))

    for r in order:
        send_qg(r).start()
        send_qb(r).start()
    pg_cross.wait_recv()
    pg_sib[0].wait_send()
    pg[0] = (pacc[...] + pgr[0].astype(F32) + pgr[2].astype(F32)).astype(BF16)

    def send_pg(r):
        src = pg.at[0, pl.ds(pl.multiple_of(flip(d, r) * share, share), share), :]
        return remote(src, qgr.at[r, 3] if False else pgr.at[3, pl.ds(r * share, share), :], pt_s.at[r], pt_r.at[r], at_dp(r))

    for r in order:
        send_pg(r).start()
    own = normed_block(h)
    _, scaled, inverse = normalize(x_ref[...].astype(F32), g1_ref[...][None, :], b1_ref[...][None, :])
    gn_sib[0].wait_recv()
    own = own + grecv[0].astype(F32)
    gn_cross.wait_recv()
    own = own + grecv[2].astype(F32)
    en[0:1, :] = jnp.sum(own * scaled, axis=0, keepdims=True)
    en[1:2, :] = jnp.sum(own, axis=0, keepdims=True)
    en_head = [remote(en, enr.at[k], eh_s.at[k], eh_r.at[k], at_head(k)) for k in (1, 2, 3)]
    for copy in en_head:
        copy.start()
    igrad_o[...] = gres[...] + norm_backward(own, scaled, inverse, g1_ref[...][None, :])
    for copy in en_head:
        copy.wait_recv()
    ent[...] = en[...] + enr[1] + enr[2] + enr[3]
    en_dp = [remote(ent, enq.at[r], ed_s.at[r], ed_r.at[r], at_dp(r)) for r in range(1, n_dp)]
    for copy in en_dp:
        copy.start()

    for r in order:
        send_qg(r).wait_recv()
        send_qb(r).wait_recv()
        send_pg(r).wait_recv()
    here = pl.ds(pl.multiple_of(d * share, share), share)
    for c in range(3):
        total = qg[c, here, :].astype(F32)
        for r in range(1, n_dp):
            total += qgr[r, c].astype(F32)
        qg_o[c] = total
    total = pg[0, here, :].astype(F32)
    for r in range(1, n_dp):
        total += pgr[3, r * share : (r + 1) * share, :].astype(F32)
    pg_o[...] = total
    bias = qb[...]
    for r in range(1, n_dp):
        bias += qbr[r]
    qb_o[...] = bias
    for copy in sm_dp:
        copy.wait_recv()
    total = smt[...]
    for r in range(1, n_dp):
        total += smd[r]
    sums_o[...] = total
    for copy in bg_head:
        copy.wait_recv()
    bgs_o[...] = bg_ref[h] + bgr[1] + bgr[2] + bgr[3]
    for copy in en_dp:
        copy.wait_recv()
    total = ent[...]
    for r in range(1, n_dp):
        total += enq[r]
    ends_o[...] = total

    for k in (1, 2, 3):
        send_ctx(k).wait_send()
    for r in order:
        send_prod(r).wait()
        send_qg(r).wait_send()
        send_qb(r).wait_send()
        send_pg(r).wait_send()
    prod_own.wait()
    up_cross.wait()
    pg_cross.wait_send()
    gn_cross.wait_send()
    for copy in gn_sib + sm_head + bg_head + en_head + sm_dp + en_dp:
        copy.wait_send()


def stage_b(n_dp, gctx, qkv, probs, ctx, ctxf, gath, w, x, g1, b1, gres, prod, upc, sm, bg):
    tok, width = x.shape
    _, heads, group, hd = qkv.shape
    cols = heads * hd
    tiles = group // TILE
    span = probs.shape[3]
    share = width // n_dp
    sds = jax.ShapeDtypeStruct
    vm = pltpu.VMEM
    return pl.pallas_call(
        functools.partial(kernel_b, n_dp),
        out_shape=(
            sds((tok, width), F32),
            sds(prod.shape, BF16),
            sds(upc.shape, BF16),
            sds((3, share, cols), F32),
            sds((share, cols), F32),
            sds((8, 2 * cols), F32),
            sds(sm.shape, F32),
            sds((2, width), F32),
            sds(bg.shape[1:], F32),
        ),
        in_specs=[VM, ANY, ANY, VM, VM, ANY] + [VM] * 5 + [ANY, ANY, VM, VM],
        out_specs=(VM, ANY, ANY) + (VM,) * 6,
        scratch_shapes=[
            vm((4, tok, cols), BF16), vm((3, heads, group, hd), BF16), vm((3, heads, TILE, span), BF16), vm((group, width), BF16),
            vm((heads, group, hd), F32), vm((heads, group, hd), F32), vm((3, group, cols), BF16),
            vm((2, tok, width), BF16), vm((tok, width), BF16), vm((3, tok, width), BF16),
            vm((3, width, cols), BF16), vm((n_dp, 3, share, cols), BF16),
            vm((3, width, cols), BF16), vm((4, width, cols), BF16), vm((width, cols), F32),
            vm((8, 2 * cols), F32), vm((n_dp, 8, 2 * cols), F32),
            vm((4,) + sm.shape, F32), vm((n_dp,) + sm.shape, F32), vm(sm.shape, F32),
            vm((2, width), F32), vm((4, 2, width), F32), vm((2, width), F32), vm((n_dp, 2, width), F32),
            vm((4,) + bg.shape[1:], F32),
            DMA((2,)), DMA((3,)), DMA((4,)), DMA((4,)), DMA((n_dp,)), DMA((n_dp,)), DMA((1,)), DMA((1,)), DMA((3,)), DMA((3,)),
            DMA((n_dp,)), DMA((n_dp,)), DMA((3,)), DMA((3,)), DMA((n_dp,)), DMA((n_dp,)), DMA((n_dp,)), DMA((n_dp,)),
            DMA((4,)), DMA((4,)), DMA((n_dp,)), DMA((n_dp,)), DMA((4,)), DMA((4,)), DMA((n_dp,)), DMA((n_dp,)), DMA((4,)), DMA((4,)),
        ],
        compiler_params=pltpu.CompilerParams(collective_id=2, has_side_effects=True, vmem_limit_bytes=VMEM_LIMIT),
    )(gctx, qkv, probs, ctx, ctxf, gath, w.transpose(0, 2, 1), x, g1, b1, gres, prod, upc, sm, bg)


def local(
    block_input, norm1_gain, norm1_bias, qkv_weight, qkv_bias, proj_weight, proj_bias, norm2_gain, norm2_bias, router_weight,
    up_weight, up_bias, down_weight, down_bias, routes, lengths, cotangent,
):
    tok, width = block_input.shape
    experts = router_weight.shape[1]
    cap = 2 * tok // experts
    gath, qkv, probs, ctx, ctxf, projf, cots = stage_a(
        experts, block_input, norm1_gain, norm1_bias, qkv_weight, qkv_bias, proj_weight, routes, cotangent, lengths, cap
    )
    res, gate, prod, gres, gctx, upc, upo, dng, sm, bg, balance = stage_m(
        experts, block_input, ctxf, projf, proj_bias, norm2_gain, norm2_bias, router_weight, routes, cotangent, cots,
        up_weight, up_bias, down_weight, down_bias,
    )
    igrad, prodr, upr, qg, pg, qb, sums, ends, bgs = stage_b(
        experts, gctx, qkv, probs, ctx, ctxf, gath, qkv_weight, block_input, norm1_gain, norm1_bias, gres, prod, upc, sm, bg
    )
    d = lax.axis_index("dp")
    device = d * 4 + lax.axis_index("head")
    expert = routes[:, 0]
    hot = (expert[:, None] == jnp.arange(experts, dtype=jnp.int32)[None, :]).astype(jnp.int32)
    slot = jnp.sum(jnp.cumsum(hot, axis=0) * hot, axis=1) - 1
    mixed = (res + gate * prodr[(expert ^ d) * cap + slot].astype(F32)).astype(BF16)
    part = width // (4 * experts)

    def mine(row):
        return lax.dynamic_slice_in_dim(row, device * part, part, axis=0)

    hd = qkv_bias.shape[2]
    heads = qkv_bias.shape[1]
    qkv_bias_grad = lax.dynamic_slice_in_dim(qb[0].reshape(2, heads, hd), d * (hd // experts), hd // experts, axis=2)
    return (
        mixed, balance.reshape(1), igrad, mine(ends[0]), mine(ends[1]), qg, qkv_bias_grad, pg.T, mine(sums[2]), mine(sums[0]),
        mine(sums[1]), mine(sums[8 : 8 + experts].T), (upo + upr.astype(F32))[None], bgs[None, 0], dng[None], bgs[None, 1, : width // 4],
    )


def solution(mesh):
    placed = (
        P(("dp", "head"), None), P(), P(), P(None, None, "head"), P(None, "head", None), P("head", None), P(), P(), P(), P(),
        P("dp", None, None), P("dp", None), P("dp", None, None), P("dp", None), P(("dp", "head"), None), P("dp", None),
        P(("dp", "head"), None),
    )
    tokens = P(("dp", "head"))
    return jax.shard_map(
        local,
        mesh=mesh,
        in_specs=placed,
        out_specs=(
            P(("dp", "head"), None), tokens, P(("dp", "head"), None), tokens, tokens, P(None, "dp", "head"), P(None, "head", "dp"),
            P("head", "dp"), tokens, tokens, tokens, P(("dp", "head"), None), P("dp", None, "head"), P("dp", "head"),
            P("dp", "head", None), P("dp", "head"),
        ),
        check_vma=False,
    )
```

```python
import functools
import jax
import jax.numpy as jnp
from jax import lax
from jax.experimental import pallas as pl
from jax.experimental.pallas import tpu as pltpu
from jax.sharding import PartitionSpec as P

EPSILON = 1e-05
BAL_COEF = 0.01
HIGHEST = lax.Precision.HIGHEST
NEG_LARGE = -1e30
MESH = pl.DeviceIdType.MESH
F32 = jnp.float32
BF16 = jnp.bfloat16
TILE = 256
VMEM_LIMIT = 60 << 20


def flip(index, bits):
    out, bit = index, 1
    while bit <= bits:
        if bits & bit:
            out = out + bit - 2 * bit * lax.rem(lax.div(index, bit), 2)
        bit *= 2
    return out


def remote(src, dst, send_sem, recv_sem, device):
    return pltpu.make_async_remote_copy(
        src_ref=src, dst_ref=dst, send_sem=send_sem, recv_sem=recv_sem, device_id=device, device_id_type=MESH
    )


def dot(left, right, dims=((1,), (0,)), precision=None):
    return lax.dot_general(left, right, (dims, ((), ())), precision=precision, preferred_element_type=F32)


def normalize(values, gain, bias):
    average = jnp.mean(values, axis=-1, keepdims=True)
    centred = values - average
    variance = jnp.mean(centred * centred, axis=-1, keepdims=True)
    inverse = lax.rsqrt(variance + EPSILON)
    scaled = centred * inverse
    return (scaled * gain + bias, scaled, inverse)


def norm_backward(grad_normed, scaled, inverse, gain):
    grad_scaled = grad_normed * gain
    first_mean = jnp.mean(grad_scaled, axis=-1, keepdims=True)
    second_mean = jnp.mean(grad_scaled * scaled, axis=-1, keepdims=True)
    return inverse * (grad_scaled - first_mean - scaled * second_mean)


def slot_layouts(routes, experts, cap):
    rows = routes.shape[1]
    count = max(8, experts)
    expert = lax.broadcasted_iota(jnp.int32, (count, rows), 0)
    hot = (routes == expert).astype(F32)
    upto = lax.broadcasted_iota(jnp.int32, (rows, rows), 0) <= lax.broadcasted_iota(jnp.int32, (rows, rows), 1)
    rank = dot(hot.astype(BF16), upto.astype(F32).astype(BF16))
    slot_row = jnp.sum((rank - 1.0) * hot, axis=0, keepdims=True)
    flat_row = jnp.sum((rank - 1.0 + cap * expert.astype(F32)) * hot, axis=0, keepdims=True)
    return hot, flat_row.astype(jnp.int32), slot_row.astype(jnp.int32)


def barrier_signal(peers):
    barrier = pltpu.get_barrier_semaphore()
    for peer in peers:
        pl.semaphore_signal(barrier, inc=1, device_id=peer, device_id_type=MESH)


def barrier_wait(count):
    pl.semaphore_wait(pltpu.get_barrier_semaphore(), count)


def kernel_a(
    n_dp, x_ref, g1_ref, b1_ref, w_ref, qb_ref, proj_ref, routes_ref, cot_ref, len_ref,
    gath_o, qkv_o, p_o, ctx_o, ctxf_o, projf_o, cots_o,
    gath, qkv, p_st, bias_s, ctx_s, disp,
    ag_s, ag_r, pj_s, pj_r, cx_s, cx_r, ct_s, ct_r, p_sem, loc,
):
    tok, width = x_ref.shape
    heads = qb_ref.shape[0]
    hd = qb_ref.shape[2]
    group = 4 * tok
    tiles = group // TILE
    reach = group // 2 // TILE + 1
    cap = cots_o.shape[0] // n_dp
    d = lax.axis_index("dp")
    h = lax.axis_index("head")
    barrier_signal([(d, flip(h, k)) for k in (1, 2, 3)] + [(flip(d, r), h) for r in range(1, n_dp)])

    normed, _, _ = normalize(x_ref[...].astype(F32), g1_ref[...][None, :], b1_ref[...][None, :])

    def block(index):
        return pl.ds(pl.multiple_of(index * tok, tok), tok)

    gath[block(h), :] = normed.astype(BF16)
    barrier_wait(3 + n_dp - 1)

    chunks = 4
    step = tok // chunks

    def part(index, i):
        return gath.at[pl.ds(pl.multiple_of(index * tok + i * step, step), step), :]

    sib, cross, diag = flip(h, 1), flip(h, 2), flip(h, 3)
    to_cross = [remote(part(h, i), part(h, i), ag_s.at[i], ag_r.at[i], (d, cross)) for i in range(chunks)]
    to_sib = remote(gath.at[block(h), :], gath.at[block(h), :], ag_s.at[2 * chunks], ag_r.at[2 * chunks], (d, sib))
    onward = [
        remote(part(cross, i), part(cross, i), ag_s.at[chunks + i], ag_r.at[chunks + i], (d, sib)) for i in range(chunks)
    ]
    for copy in to_cross:
        copy.start()
    to_sib.start()
    proj_copies = [
        remote(proj_ref, projf_o.at[h], pj_s.at[k], pj_r.at[k], (d, flip(h, k))) for k in (1, 2, 3)
    ]

    hot_t, flat_row, slot_row = slot_layouts(routes_ref[...], n_dp, cap)
    slot_iota = lax.broadcasted_iota(jnp.int32, (cap, tok), 0)

    def dispatch(e, carry):
        hot = (flat_row == slot_iota + e * cap).astype(F32).astype(BF16)
        disp[pl.ds(pl.multiple_of(e * cap, cap), cap), :] = dot(hot, cot_ref[...]).astype(BF16)
        return carry

    lax.fori_loop(0, n_dp, dispatch, 0)

    def slots(index):
        return pl.ds(pl.multiple_of(index * cap, cap), cap)

    cot_copies = [
        remote(disp.at[slots(flip(d, r)), :], cots_o.at[pl.ds(r * cap, cap), :], ct_s.at[r], ct_r.at[r], (flip(d, r), h))
        for r in range(1, n_dp)
    ]
    for copy in cot_copies:
        copy.start()
    cot_own = pltpu.make_async_copy(disp.at[slots(d), :], cots_o.at[pl.ds(0, cap), :], ct_s.at[0])
    cot_own.start()

    def project(index):
        rows = gath[block(index), :]
        for c in range(3):
            out = dot(rows, w_ref[c], ((1,), (1,)))
            for a in range(heads):
                piece = out[:, a * hd : (a + 1) * hd]
                if c != 1:
                    piece = piece + qb_ref[a, c // 2 : c // 2 + 1, :]
                piece = piece.astype(BF16)
                if c == 0:
                    piece = piece * jnp.asarray(hd ** (-0.5), BF16)
                qkv[c, a, block(index), :] = piece

    project(h)
    to_sib.wait_recv()
    project(sib)
    for i in range(chunks):
        to_cross[i].wait_recv()
        onward[i].start()
    for copy in proj_copies:
        copy.start()
    proj_own = pltpu.make_async_copy(proj_ref, projf_o.at[h], loc.at[0])
    proj_own.start()
    project(cross)
    for i in range(chunks):
        onward[i].wait_recv()
    project(diag)
    gath_copy = pltpu.make_async_copy(gath, gath_o, loc.at[1])
    gath_copy.start()
    qkv_copy = pltpu.make_async_copy(qkv, qkv_o, loc.at[2])
    qkv_copy.start()

    ends = [len_ref[0, 0]]
    for i in range(1, len_ref.shape[1] - 1):
        ends.append(ends[-1] + len_ref[0, i])

    order = []
    for i in range(tiles // 2):
        order += [tiles - 1 - i, tiles // 2 - 1 - i]
    per_block = tok // TILE

    def p_copy(t, a):
        size = min(t + 1, reach) * TILE
        return pltpu.make_async_copy(p_st.at[a, :, pl.ds(0, size)], p_o.at[a, t, :, pl.ds(0, size)], p_sem.at[a])

    previous = None
    for t in order:
        size = min(t + 1, reach) * TILE
        first = (t + 1) * TILE - size
        row = t * TILE + lax.broadcasted_iota(jnp.int32, (TILE, 1), 0)
        start = jnp.zeros((TILE, 1), jnp.int32)
        for end in ends:
            start = jnp.where(row >= end, end, start)
        col = first + lax.broadcasted_iota(jnp.int32, (TILE, size), 1)
        bias_s[:, :size] = jnp.where((col >= start) & (col <= row), 0.0, NEG_LARGE)
        outs = []
        for a in range(heads):
            q = qkv[0, a, t * TILE : (t + 1) * TILE, :]
            k = qkv[1, a, first : (t + 1) * TILE, :]
            v = qkv[2, a, first : (t + 1) * TILE, :]
            s = dot(q, k, ((1,), (1,))) + bias_s[:, :size]
            top = jnp.max(s, axis=1, keepdims=True)
            e = jnp.exp(s - top)
            total = jnp.sum(e, axis=1, keepdims=True)
            p = (e * (1.0 / total)).astype(BF16)
            if previous is not None:
                p_copy(previous, a).wait()
            p_st[a, :, :size] = p
            p_copy(t, a).start()
            outs.append(dot(p, v))
        ctx_s[t] = pack(outs).astype(BF16)
        previous = t
        owner, sub = t // per_block, t % per_block
        rows = pl.ds(sub * (TILE * 3 // 2), TILE * 3 // 2)

        @pl.when(h != owner)
        def _():
            remote(ctx_s.at[t], ctxf_o.at[h, rows, :], cx_s.at[t], cx_r.at[h, sub], (d, owner)).start()

        @pl.when(h == owner)
        def _():
            pltpu.make_async_copy(ctx_s.at[t], ctxf_o.at[h, rows, :], cx_s.at[t]).start()

    ctx_copy = pltpu.make_async_copy(ctx_s, ctx_o, loc.at[3])
    ctx_copy.start()
    for a in range(heads):
        p_copy(previous, a).wait()
    for t in range(tiles):
        owner, sub = t // per_block, t % per_block
        rows = pl.ds(sub * (TILE * 3 // 2), TILE * 3 // 2)

        @pl.when(h != owner)
        def _():
            remote(ctx_s.at[t], ctxf_o.at[h, rows, :], cx_s.at[t], cx_r.at[h, sub], (d, owner)).wait_send()

        @pl.when(h == owner)
        def _():
            pltpu.make_async_copy(ctx_s.at[t], ctxf_o.at[h, rows, :], cx_s.at[t]).wait()

    for k in (1, 2, 3):
        peer = flip(h, k)
        for sub in range(per_block):
            remote(
                ctx_s.at[0], ctxf_o.at[peer, pl.ds(sub * (TILE * 3 // 2), TILE * 3 // 2), :], cx_s.at[0], cx_r.at[peer, sub], (d, peer)
            ).wait_recv()
    for copy in to_cross:
        copy.wait_send()
    to_sib.wait_send()
    for copy in onward:
        copy.wait_send()
    for k in (1, 2, 3):
        proj_copies[k - 1].wait_send()
        peer = flip(h, k)
        remote(proj_ref, projf_o.at[peer], pj_s.at[k], pj_r.at[k], (d, peer)).wait_recv()
    for copy in cot_copies:
        copy.wait()
    for copy in (cot_own, proj_own, gath_copy, qkv_copy, ctx_copy):
        copy.wait()


VM = pl.BlockSpec(memory_space=pltpu.VMEM)
SM = pl.BlockSpec(memory_space=pltpu.SMEM)
ANY = pl.BlockSpec(memory_space=pl.ANY)
DMA = pltpu.SemaphoreType.DMA


def stage_a(n_dp, x, g1, b1, w, qb, proj, routes, cot, lengths, cap):
    tok, width = x.shape
    heads, hd = qb.shape[1:]
    w, qb, routes = w.transpose(0, 2, 1), qb.transpose(1, 0, 2), routes.T
    group = 4 * tok
    tiles = group // TILE
    span = (group // 2 // TILE + 1) * TILE
    cols = heads * hd
    sds = jax.ShapeDtypeStruct
    return pl.pallas_call(
        functools.partial(kernel_a, n_dp),
        out_shape=(
            sds((group, width), BF16),
            sds((3, heads, group, hd), BF16),
            sds((heads, tiles, TILE, span), BF16),
            sds((tiles, TILE * 3 // 2, 128), BF16),
            sds((4, tok * 3 // 2, 128), BF16),
            sds((4, cols, width), BF16),
            sds((n_dp * cap, width), BF16),
        ),
        in_specs=[VM] * 8 + [SM],
        out_specs=(ANY,) * 7,
        scratch_shapes=[
            pltpu.VMEM((group, width), BF16),
            pltpu.VMEM((3, heads, group, hd), BF16),
            pltpu.VMEM((heads, TILE, span), BF16),
            pltpu.VMEM((TILE, span), F32),
            pltpu.VMEM((tiles, TILE * 3 // 2, 128), BF16),
            pltpu.VMEM((n_dp * cap, width), BF16),
            DMA((9,)), DMA((9,)), DMA((4,)), DMA((4,)), DMA((tiles,)), DMA((4, tok // TILE)),
            DMA((n_dp,)), DMA((n_dp,)), DMA((heads,)), DMA((4,)),
        ],
        compiler_params=pltpu.CompilerParams(collective_id=0, has_side_effects=True, vmem_limit_bytes=VMEM_LIMIT),
    )(x, g1, b1, w, qb, proj, routes, cot, lengths)


def far_first(n_dp):
    half = n_dp // 2
    return list(range(half, n_dp)) + [r for r in range(2, half)] + [1]


def gelu_parts(u):
    return 0.5 * lax.erf(u * 0.7071067811865476) + 0.5, jnp.exp(u * u * -0.5) * 0.3989422804014327


def split3(value):
    high = value.astype(BF16)
    rest = value - high.astype(F32)
    middle = rest.astype(BF16)
    return high, middle, (rest - middle.astype(F32)).astype(BF16)


def fold3(stacked):
    count = stacked.shape[0] // 3
    return stacked[:count] + stacked[count : 2 * count] + stacked[2 * count :]


def row_to_col(row):
    return jnp.broadcast_to(row, (128, row.shape[1])).T[:, :1]


def col_to_rows(col):
    return jnp.broadcast_to(col, (col.shape[0], 128)).T[:8]


def kernel_m(
    n_dp, x_ref, ctxf, projf, pb_ref, g2_ref, b2_ref, rt_ref, routes_ref, cot_ref, cots, up_h, upb_ref, down_h, downb_ref,
    res, gate_o, prod_o, gres_o, gctx_o, upc_o, upo_o, dno_o, dnr_o, sm_o, bg_o, bal_o,
    stat, nhigh, nlow, disp, gsend, rows, rowst, grecv, up, down, ghu, hid, gg, gacc, gin, ggs, ginr, ggr, dsend, dacc, drecv, urecv,
    ld, ra_s, ra_r, ga_s, ga_r, rb_s, rb_r, gb_s, gb_r, ds_s, ds_r, us_s, us_r, out_sem,
):
    tok, width = x_ref.shape
    ff = up.shape[1]
    slots = rows.shape[0]
    cap = slots // n_dp
    per = TILE // cap
    groups = slots // TILE
    experts = n_dp
    quarter = ff // 4
    size_t = TILE * 3 // 2
    hd = 64
    d = lax.axis_index("dp")
    h = lax.axis_index("head")
    sib, cross = (d, flip(h, 1)), (d, flip(h, 2))
    loads = [pltpu.make_async_copy(down_h.at[0], down, ld.at[0]), pltpu.make_async_copy(up_h.at[0], up, ld.at[1])]
    for copy in loads:
        copy.start()
    barrier_signal([(d, flip(h, k)) for k in (1, 2, 3)] + [(flip(d, r), h) for r in range(1, n_dp)])

    proj = projf[...].reshape(width, width)
    for i in range(tok // TILE):
        heads = []
        for b in range(4):
            heads += unpack(ctxf[b, i * size_t : (i + 1) * size_t, :])
        at = slice(i * TILE, (i + 1) * TILE)
        res[at, :] = x_ref[at, :].astype(F32) + dot(jnp.concatenate(heads, axis=1), proj) + pb_ref[...][None, :]
    gain, bias = g2_ref[...][None, :], b2_ref[...][None, :]
    chunk = 64

    def norm_rows(i, carry):
        at = pl.ds(pl.multiple_of(i * chunk, chunk), chunk)
        residual = res[at, :]
        average = jnp.mean(residual, axis=-1, keepdims=True)
        centred = residual - average
        inverse = lax.rsqrt(jnp.mean(centred * centred, axis=-1, keepdims=True) + EPSILON)
        stat[0, at, :] = average
        stat[1, at, :] = inverse
        normed = centred * inverse * gain + bias
        high = normed.astype(BF16)
        nhigh[at, :] = high
        nlow[at, :] = (normed - high.astype(F32)).astype(BF16)
        return carry

    lax.fori_loop(0, tok // chunk, norm_rows, 0)

    router3 = jnp.concatenate(split3(rt_ref[...]), axis=0)
    logits = fold3(dot(router3, nhigh[...], ((1,), (1,))) + dot(router3, nlow[...], ((1,), (1,))))
    raised = jnp.exp(logits - jnp.max(logits, axis=0, keepdims=True))
    prob = raised / jnp.sum(raised, axis=0, keepdims=True)
    hot, flat_row, slot_row = slot_layouts(routes_ref[...], experts, cap)
    gate_row = jnp.sum(prob * hot, axis=0, keepdims=True)
    gate_o[...] = row_to_col(gate_row)
    fraction = jnp.mean(hot, axis=1, keepdims=True)
    bal_o[...] = experts * jnp.sum(fraction * jnp.mean(prob, axis=1, keepdims=True), axis=0, keepdims=True)

    expert_row = jnp.sum(hot * lax.broadcasted_iota(jnp.int32, hot.shape, 0).astype(F32), axis=0, keepdims=True)
    other_row = jnp.bitwise_xor(expert_row.astype(jnp.int32), d)
    flat_x = other_row * cap + slot_row
    at_slot = (slot_row == lax.broadcasted_iota(jnp.int32, (128, tok), 0)).astype(F32).astype(BF16)
    other_hot = (other_row == lax.broadcasted_iota(jnp.int32, hot.shape, 0)).astype(F32)
    gates3 = jnp.concatenate([other_hot * part.astype(F32) for part in split3(gate_row)], axis=0).astype(BF16)
    gates = fold3(dot(gates3, at_slot, ((1,), (1,))))
    barrier_wait(3 + n_dp - 1)
    order = far_first(n_dp)

    def send_rows(r):
        return remote(disp.at[pl.ds(r * cap, cap), :], rows.at[pl.ds(r * cap, cap), :], ra_s.at[r], ra_r.at[r], (flip(d, r), h))

    def send_gate(r):
        return remote(gsend.at[r], grecv.at[r], ga_s.at[r], ga_r.at[r], (flip(d, r), h))

    slot_iota = lax.broadcasted_iota(jnp.int32, (cap, tok), 0)

    def fill(r):
        hits = (flat_x == slot_iota + r * cap).astype(F32).astype(BF16)
        gsend[r] = jnp.broadcast_to(gates[r : r + 1], (8, 128))
        return dot(hits, nhigh[...]).astype(BF16)

    for r in order:
        disp[r * cap : (r + 1) * cap, :] = fill(r)
        send_rows(r).start()
        send_gate(r).start()
    rows[:cap, :] = fill(0)
    grecv[0] = gsend[0]

    loads[0].wait()

    def hidden_grad(i, carry):
        at = pl.ds(pl.multiple_of(lax.div(i, 4) * TILE, TILE), TILE)
        cols = pl.ds(pl.multiple_of(lax.rem(i, 4) * quarter, quarter), quarter)
        ghu[at, cols] = dot(cots[at, :], down[cols, :], ((1,), (1,))).astype(BF16)
        return carry

    lax.fori_loop(0, 4 * groups, hidden_grad, 0)
    loads[1].wait()

    step = quarter

    def send_back(r):
        return remote(gin.at[pl.ds(r * cap, cap), :], ginr.at[pl.ds(r * cap, cap), :], rb_s.at[r], rb_r.at[r], (flip(d, r), h))

    def send_gg(r):
        return remote(ggs.at[r // per], ggr.at[r], gb_s.at[r], gb_r.at[r], (flip(d, r), h))

    for g in range(groups):
        mine = [r for r in range(g * per, (g + 1) * per)]
        for r in mine:
            if r:
                send_rows(r).wait_recv()
                send_gate(r).wait_recv()
        at = slice(g * TILE, (g + 1) * TILE)
        gate = jnp.concatenate([grecv[r].T[:cap, :1] for r in mine], axis=0)
        gacc[...] = jnp.zeros_like(gacc)
        gg[...] = jnp.zeros_like(gg)

        def expert(f, carry):
            cols = pl.ds(pl.multiple_of(f * step, step), step)
            u = dot(rows[at, :], up[:, cols]) + upb_ref[:, cols]
            share, density = gelu_parts(u)
            low = (u * share).astype(BF16)
            back = ghu[at, cols].astype(F32)
            hid[at, cols] = low
            meet = low.astype(F32) * back
            folded = meet[:, :128]
            for j in range(1, step // 128):
                folded += meet[:, j * 128 : (j + 1) * 128]
            gg[...] += folded
            pre = (gate * back * (share + u * density)).astype(BF16)
            ghu[at, cols] = pre
            gacc[...] += dot(pre, up[:, cols], ((1,), (1,)))
            return carry

        lax.fori_loop(0, ff // step, expert, 0)
        gin[at, :] = gacc[...].astype(BF16)
        cot_g = cots[at, :].astype(F32)
        gg_col = jnp.sum(gg[...], axis=1, keepdims=True) + jnp.sum(cot_g * downb_ref[...], axis=1, keepdims=True)
        ggs[g] = col_to_rows(gg_col)
        for r in mine:
            if r:
                send_back(r).start()
                send_gg(r).start()
            else:
                ginr[:cap, :] = gin[:cap, :]
                ggr[0] = ggs[0]
        cots[at, :] = (gate * cot_g).astype(BF16)
        rowst[:, at] = flip_t(rows[at, :])

    third = quarter // 3

    def block_cols(index):
        return pl.ds(pl.multiple_of(index * quarter, quarter), quarter)

    def down_block(index, ref):
        def body(i, carry):
            cols = pl.ds(pl.multiple_of(index * quarter + i * third, third), third)
            ref[pl.ds(pl.multiple_of(i * third, third), third), :] = dot(hid[:, cols], cots[...], ((0,), (0,))).astype(BF16)
            return carry

        lax.fori_loop(0, 3, body, 0)

    def up_block(index, ref):
        part = width // 3

        def body(i, carry):
            at = pl.ds(pl.multiple_of(i * part, part), part)
            ref[at, :] = dot(rowst[at, :], ghu[:, block_cols(index)]).astype(BF16)
            return carry

        lax.fori_loop(0, 3, body, 0)

    def add_into(ref, other):
        def body(i, carry):
            at = pl.ds(pl.multiple_of(i * 64, 64), 64)
            ref[at, :] = (ref[at, :].astype(F32) + other[at, :].astype(F32)).astype(BF16)
            return carry

        lax.fori_loop(0, ref.shape[0] // 64, body, 0)

    down_sib = [remote(dsend.at[i], drecv.at[i], ds_s.at[i], ds_r.at[i], sib) for i in range(2)]
    down_cross = remote(dacc, dnr_o, ds_s.at[2], ds_r.at[2], cross)
    up_sib = [remote(dsend.at[i], urecv.at[i], us_s.at[i], us_r.at[i], sib) for i in range(2)]
    down_block(flip(h, 3), dsend.at[1])
    down_sib[1].start()
    down_block(flip(h, 2), dacc)
    down_sib[1].wait_recv()
    add_into(dacc, drecv.at[1])
    down_cross.start()
    down_block(flip(h, 1), dsend.at[0])
    down_sib[0].start()
    for r in order:
        send_rows(r).wait_send()

    def produce(i, carry):
        at = pl.ds(pl.multiple_of(i * TILE, TILE), TILE)
        disp[at, :] = (dot(hid[at, :], down[...]) + downb_ref[...]).astype(BF16)
        return carry

    lax.fori_loop(0, groups, produce, 0)
    prod_copy = pltpu.make_async_copy(disp, prod_o, out_sem.at[0])
    prod_copy.start()
    for copy in down_sib:
        copy.wait_send()
    up_block(flip(h, 3), dsend.at[1])
    up_sib[1].start()
    up_block(flip(h, 1), dsend.at[0])
    up_sib[0].start()
    up_block(flip(h, 2), upc_o)
    up_block(h, upo_o)
    down_block(h, dno_o)
    ones = jnp.ones((8, slots), BF16)
    up_bias = dot(ones, ghu[...])
    down_bias = dot(ones, cots[...])
    short = width // 4
    for b in range(4):
        bg_o[b, 0:1, :] = up_bias[:1, b * quarter : (b + 1) * quarter]
        bg_o[b, 1:2, :short] = down_bias[:1, b * short : (b + 1) * short]
    up_sib[1].wait_recv()
    add_into(upc_o, urecv.at[1])
    up_sib[0].wait_recv()
    add_into(upo_o, urecv.at[0])
    down_sib[0].wait_recv()
    add_into(dno_o, drecv.at[0])

    flat_col = row_to_col(flat_x.astype(F32)).astype(jnp.int32)
    for r in order:
        send_gg(r).wait_recv()
    slot_gg = [ggr[r][:1, (r % per) * cap : (r % per) * cap + cap] for r in range(n_dp)]
    slot_gg = jnp.concatenate(slot_gg, axis=0)
    grad_gate = jnp.sum(
        fold3(dot(jnp.concatenate(split3(slot_gg), axis=0), at_slot[:cap])) * other_hot, axis=0, keepdims=True
    )
    grad_prob = hot * grad_gate + (BAL_COEF * experts / tok) * fraction
    grad_logits = prob * (grad_prob - jnp.sum(prob * grad_prob, axis=0, keepdims=True))
    high, middle, low = split3(grad_logits)
    grads3 = jnp.concatenate([high, middle, low], axis=0)
    r_high, r_middle, r_low = split3(rt_ref[...])
    inner = 6 * experts
    padded = -(-inner // 128) * 128
    left = [v.astype(F32) for v in (high, high, high, middle, middle, low)]
    left = jnp.concatenate(left + [jnp.zeros((padded - inner, tok), F32)], axis=0).T.astype(BF16)
    right = jnp.concatenate([r_high, r_middle, r_low, r_high, r_middle, r_high, jnp.zeros((padded - inner, width), BF16)], axis=0)
    sm_o[...] = jnp.zeros_like(sm_o)
    sm_o[8 : 8 + experts, :] = fold3(dot(grads3, nhigh[...]) + dot(grads3, nlow[...]))
    for r in order:
        send_back(r).wait_recv()
    gain_sum, bias_sum, res_sum = (jnp.zeros((1, width), F32) for _ in range(3))
    part = 128
    for i in range(tok // TILE):
        lows = []
        for j in range(TILE // part):
            at = slice(i * TILE + j * part, i * TILE + (j + 1) * part)
            pick = (flat_col[at] == lax.broadcasted_iota(jnp.int32, (part, slots), 1)).astype(F32).astype(BF16)
            grad_normed = dot(pick, ginr[...]) + dot(left[at], right)
            inverse = stat[1, at, :]
            scaled = (res[at, :] - stat[0, at, :]) * inverse
            grad_res = cot_ref[at, :].astype(F32) + norm_backward(grad_normed, scaled, inverse, gain)
            gres_o[at, :] = grad_res
            gain_sum += jnp.sum(grad_normed * scaled, axis=0, keepdims=True)
            bias_sum += jnp.sum(grad_normed, axis=0, keepdims=True)
            res_sum += jnp.sum(grad_res, axis=0, keepdims=True)
            lows.append(grad_res.astype(BF16))
        back = dot(jnp.concatenate(lows, axis=0), proj, ((1,), (1,)))
        for b in range(4):
            outs = [back[:, (3 * b + a) * hd : (3 * b + a + 1) * hd] for a in range(3)]
            gctx_o[b, i * size_t : (i + 1) * size_t, :] = pack(outs).astype(BF16)
    sm_o[0:1, :] = gain_sum
    sm_o[1:2, :] = bias_sum
    sm_o[2:3, :] = res_sum
    down_cross.wait()
    for copy in up_sib:
        copy.wait_send()
    for r in order:
        send_gate(r).wait_send()
        send_back(r).wait_send()
        send_gg(r).wait_send()
    prod_copy.wait()


def stage_m(n_dp, x, ctxf, projf, pb, g2, b2, router, routes, cot, cots, up, upb, down, downb):
    tok, width = x.shape
    slots = cots.shape[0]
    ff = up.shape[2]
    groups = slots // TILE
    quarter = ff // 4
    sds = jax.ShapeDtypeStruct
    vm = pltpu.VMEM
    return pl.pallas_call(
        functools.partial(kernel_m, n_dp),
        out_shape=(
            sds((tok, width), F32),
            sds((tok, 1), F32),
            sds((slots, width), BF16),
            sds((tok, width), F32),
            sds(ctxf.shape, BF16),
            sds((width, quarter), BF16),
            sds((width, quarter), BF16),
            sds((quarter, width), BF16),
            sds((quarter, width), BF16),
            sds((8 + n_dp, width), F32),
            sds((4, 8, quarter), F32),
            sds((1, 1), F32),
        ),
        in_specs=[VM] * 10 + [ANY, VM, ANY, VM],
        out_specs=(VM, VM, ANY, VM, VM, VM, VM, VM, ANY, VM, VM, VM),
        scratch_shapes=[
            vm((2, tok, 1), F32),
            vm((tok, width), BF16),
            vm((tok, width), BF16),
            vm((slots, width), BF16),
            vm((n_dp, 8, 128), F32),
            vm((slots, width), BF16),
            vm((width, slots), BF16),
            vm((n_dp, 8, 128), F32),
            vm((width, ff), BF16),
            vm((ff, width), BF16),
            vm((slots, ff), BF16),
            vm((slots, ff), BF16),
            vm((TILE, 128), F32),
            vm((TILE, width), F32),
            vm((slots, width), BF16),
            vm((groups, 8, TILE), F32),
            vm((slots, width), BF16),
            vm((n_dp, 8, TILE), F32),
            vm((2, quarter, width), BF16),
            vm((quarter, width), BF16),
            vm((2, quarter, width), BF16),
            vm((2, width, quarter), BF16),
            DMA((2,)), DMA((n_dp,)), DMA((n_dp,)), DMA((n_dp,)), DMA((n_dp,)), DMA((n_dp,)), DMA((n_dp,)),
            DMA((n_dp,)), DMA((n_dp,)), DMA((3,)), DMA((3,)), DMA((2,)), DMA((2,)), DMA((1,)),
        ],
        compiler_params=pltpu.CompilerParams(collective_id=1, has_side_effects=True, vmem_limit_bytes=VMEM_LIMIT),
    )(x, ctxf, projf, pb, g2, b2, router.T, routes.T, cot, cots, up, upb, down, downb)


def pack(outs):
    half = outs[2].shape[0] // 2
    return jnp.concatenate(
        [jnp.concatenate(outs[:2], axis=1), jnp.concatenate([outs[2][:half], outs[2][half:]], axis=1)], axis=0
    )


def unpack(tile):
    rows = tile.shape[0] * 2 // 3
    third = jnp.concatenate([tile[rows:, :64], tile[rows:, 64:]], axis=0)
    return [tile[:rows, :64], tile[:rows, 64:], third]


def unpack_t(tile):
    rows = tile.shape[1] * 2 // 3
    third = jnp.concatenate([tile[:64, rows:], tile[64:, rows:]], axis=1)
    return [tile[:64, :rows], tile[64:, :rows], third]


def flip_t(value):
    return value.astype(F32).T.astype(BF16)


def kernel_b(
    n_dp, gctx, qkv_h, p_h, ctx, ctxf, gath_h, w_ref, x_ref, g1_ref, b1_ref, gres, res, gate_ref, routes_ref, prod_h, upc_h, sm_ref, bg_ref,
    mixed_o, igrad_o, upr_o, comb_o, qb_o, sums_o, ends_o, bgs_o,
    gcr, qkv, p_v, gath, prodr, dkt, dvt, grads, gradst, gsend, gacc, grecv, comb, combx, comba, combr, pg, pgr, pacc,
    qb, qbr, smr, smd, smt, en, enr, ent, enq, bgr,
    ld, p_sem, gc_s, gc_r, pr_s, pr_r, uc_s, uc_r, gn_s, gn_r, gx_s, gx_r, qx_s, qx_r, qg_s, qg_r, pg_s, pg_r, qb_s, qb_r,
    sh_s, sh_r, sd_s, sd_r, eh_s, eh_r, ed_s, ed_r, bg_s, bg_r,
):
    tok, width = x_ref.shape
    heads, group, hd = qkv.shape[1:]
    cols = heads * hd
    tiles = group // TILE
    reach = group // 2 // TILE + 1
    per_block = tok // TILE
    slots = prod_h.shape[0]
    cap = slots // n_dp
    share = width // n_dp
    size_t = TILE * 3 // 2
    d = lax.axis_index("dp")
    h = lax.axis_index("head")
    sib, cross = (d, flip(h, 1)), (d, flip(h, 2))
    order = far_first(n_dp)

    def at_head(k):
        return (d, flip(h, k))

    def at_dp(r):
        return (flip(d, r), h)

    def p_load(t, slot):
        size = min(t + 1, reach) * TILE
        return pltpu.make_async_copy(p_h.at[:, t, :, pl.ds(0, size)], p_v.at[slot, :, :, pl.ds(0, size)], p_sem.at[slot])

    barrier_signal([at_head(k) for k in (1, 2, 3)] + [at_dp(r) for r in range(1, n_dp)])
    load_qkv = pltpu.make_async_copy(qkv_h, qkv, ld.at[0])
    load_qkv.start()
    load_gath = pltpu.make_async_copy(gath_h, gath, ld.at[1])
    dkt[...] = jnp.zeros_like(dkt)
    dvt[...] = jnp.zeros_like(dvt)
    barrier_wait(3 + n_dp - 1)

    def send_ctx(k):
        return remote(gctx.at[flip(h, k)], gcr.at[h], gc_s.at[k], gc_r.at[k], at_head(k))

    for k in (2, 3, 1):
        send_ctx(k).start()

    def send_prod(r):
        rows = pl.ds(r * cap, cap)
        return remote(prod_h.at[rows, :], prodr.at[rows, :], pr_s.at[r], pr_r.at[r], at_dp(r))

    for r in order:
        send_prod(r).start()
    prod_own = pltpu.make_async_copy(prod_h.at[pl.ds(0, cap), :], prodr.at[pl.ds(0, cap), :], pr_s.at[0])
    prod_own.start()
    gcr[h] = gctx[h]

    sm_head = [remote(sm_ref, smr.at[k], sh_s.at[k], sh_r.at[k], at_head(k)) for k in (1, 2, 3)]
    bg_head = [remote(bg_ref.at[flip(h, k)], bgr.at[k], bg_s.at[k], bg_r.at[k], at_head(k)) for k in (1, 2, 3)]
    up_half = width // 2
    up_cross = [
        remote(upc_h.at[pl.ds(i * up_half, up_half), :], upr_o.at[pl.ds(i * up_half, up_half), :], uc_s.at[i], uc_r.at[i], cross)
        for i in range(2)
    ]

    low_t = gres[...].T.astype(BF16)

    def proj_block(index):
        total = []
        for i in range(per_block):
            outs = unpack(ctxf[index, i * size_t : (i + 1) * size_t, :])
            total.append(jnp.concatenate(outs, axis=1))
        out = dot(low_t, jnp.concatenate(total, axis=0))
        return pack([out[:, a * hd : (a + 1) * hd] for a in range(heads)])

    pg_sib = [remote(pg.at[i], pgr.at[i], pg_s.at[i], pg_r.at[i], sib) for i in range(2)]
    pg[1] = proj_block(flip(h, 3)).astype(BF16)
    pg_sib[1].start()
    pg[0] = proj_block(flip(h, 1)).astype(BF16)
    pg_sib[0].start()
    for_cross = proj_block(flip(h, 2))
    pg_cross = remote(pg.at[2], pgr.at[2], pg_s.at[2], pg_r.at[2], cross)
    pg_sib[1].wait_recv()
    pg[2] = (for_cross + pgr[1].astype(F32)).astype(BF16)
    pg_cross.start()
    pacc[...] = proj_block(h)
    for copy in sm_head + bg_head:
        copy.start()
    load_qkv.wait()

    def wait_block(b):
        for k in (1, 2, 3):

            @pl.when(flip(h, k) == b)
            def _():
                remote(gctx.at[0], gcr.at[b], gc_s.at[k], gc_r.at[k], at_head(k)).wait_recv()

    def attention(sequence):
        for i, t in enumerate(sequence[:2]):
            p_load(t, i).start()
        for i, t in enumerate(sequence):
            slot = i % 3
            if i + 2 < tiles:
                p_load(sequence[i + 2], (i + 2) % 3).start()
            b, sub = t // per_block, t % per_block
            if sub == 0:
                wait_block(b)
            if i == tiles // 2:
                up_cross[0].start()
            p_load(t, slot).wait()
            size = min(t + 1, reach) * TILE
            first = (t + 1) * TILE - size
            rows = slice(t * TILE, (t + 1) * TILE)
            win = slice(first, (t + 1) * TILE)
            grad = gcr[b, sub * size_t : (sub + 1) * size_t, :]
            meets = unpack(grad.astype(F32) * ctx[t].astype(F32))
            gs = unpack(grad)
            gts = unpack_t(flip_t(grad))
            qts = unpack_t(flip_t(pack([qkv[0, a, rows, :] for a in range(heads)])))
            outs = []
            for a in range(heads):
                delta = jnp.sum(meets[a], axis=1, keepdims=True)
                p = p_v[slot, a, :, :size]
                ds = (p.astype(F32) * (dot(gs[a], qkv[2, a, win, :], ((1,), (1,))) - delta)).astype(BF16)
                outs.append(dot(ds, qkv[1, a, win, :]) * (hd ** (-0.5)))
                at = slice(a * hd, (a + 1) * hd)
                dkt[at, win] += dot(qts[a], ds)
                dvt[at, win] += dot(gts[a], p)
            dq = jnp.concatenate(outs, axis=1)
            grads[rows, :cols] = dq.astype(BF16)
            gradst[:cols, rows] = dq.T.astype(BF16)

    half = tiles // 2

    @pl.when(h < 2)
    def _():
        attention(list(range(tiles)))

    @pl.when(h >= 2)
    def _():
        attention(list(range(half, tiles)) + list(range(half)))

    load_gath.start()

    def settle(t, carry):
        at = pl.ds(pl.multiple_of(t * TILE, TILE), TILE)
        both = jnp.concatenate([dkt[:, at], dvt[:, at]], axis=0)
        gradst[cols:, at] = both.astype(BF16)
        grads[at, cols:] = both.T.astype(BF16)
        return carry

    lax.fori_loop(0, tiles, settle, 0)

    pieces = 2
    piece = tok // pieces

    def normed_piece(index, i):
        at = pl.ds(pl.multiple_of(index * tok + i * piece, piece), piece)
        total = dot(grads[at, :cols], w_ref[0])
        for c in range(1, 3):
            total += dot(grads[at, c * cols : (c + 1) * cols], w_ref[c])
        return total

    def part(i):
        return pl.ds(i * piece, piece)

    gn_sib = [
        [remote(gsend.at[j, part(i), :], grecv.at[j, part(i), :], gn_s.at[j, i], gn_r.at[j, i], sib) for i in range(pieces)]
        for j in range(2)
    ]
    gn_cross = [remote(gacc.at[part(i), :], grecv.at[2, part(i), :], gx_s.at[i], gx_r.at[i], cross) for i in range(pieces)]
    for i in range(pieces):
        gsend[1, part(i), :] = normed_piece(flip(h, 3), i).astype(BF16)
        gn_sib[1][i].start()
        mine = normed_piece(flip(h, 2), i)
        gn_sib[1][i].wait_recv()
        gacc[part(i), :] = (mine + grecv[1, part(i), :].astype(F32)).astype(BF16)
        gn_cross[i].start()
    for i in range(pieces):
        gsend[0, part(i), :] = normed_piece(flip(h, 1), i).astype(BF16)
        gn_sib[0][i].start()

    pg_sib[0].wait_recv()
    pg_cross.wait_recv()
    done = unpack(pacc[...] + pgr[0].astype(F32) + pgr[2].astype(F32))
    comb[:, 3 * cols :] = jnp.concatenate(done, axis=1).astype(BF16)
    load_gath.wait()
    for c in range(3):
        comb[:, c * cols : (c + 1) * cols] = dot(gradst[c * cols : (c + 1) * cols, :], gath[...]).T.astype(BF16)
    ones = jnp.ones((8, group), BF16)
    qb[...] = jnp.concatenate([dot(ones, grads[:, :cols])[:1], dot(ones, grads[:, 2 * cols :])[:1]], axis=1)

    pairs = n_dp // 2
    side, place = lax.rem(d, 2), lax.div(d, 2)

    def comb_rows(index):
        return pl.ds(pl.multiple_of(index * share, share), share)

    def send_side(j):
        return remote(comb.at[comb_rows(2 * j + 1 - side), :], combx.at[j], qx_s.at[j], qx_r.at[j], at_dp(1))

    def send_qg(r):
        return remote(comba.at[flip(place, r)], combr.at[r], qg_s.at[r], qg_r.at[r], at_dp(2 * r))

    def send_qb(r):
        return remote(qb, qbr.at[r], qb_s.at[r], qb_r.at[r], at_dp(r))

    pair_order = list(range(pairs // 2, pairs)) + list(range(1, pairs // 2))
    for j in range(pairs):
        send_side(j).start()
    for r in order:
        send_qb(r).start()
    for copy in sm_head:
        copy.wait_recv()
    total = sm_ref[...] + smr[1] + smr[2] + smr[3]
    for e in range(n_dp):
        smt[e] = (pltpu.roll(total, width - e * share, 1) if e else total)[:, :128]

    def send_sm(r):
        return remote(smt.at[flip(d, r)], smd.at[r], sd_s.at[r], sd_r.at[r], at_dp(r))

    for r in order:
        send_sm(r).start()
    for j in range(pairs):
        send_side(j).wait_recv()
        comba[j] = (comb[comb_rows(2 * j + side), :].astype(F32) + combx[j].astype(F32)).astype(BF16)
    for r in pair_order:
        send_qg(r).start()

    hot, flat_row, slot_row = slot_layouts(routes_ref[...], n_dp, cap)
    expert_row = jnp.sum(hot * lax.broadcasted_iota(jnp.int32, hot.shape, 0).astype(F32), axis=0, keepdims=True)
    flat_x = jnp.bitwise_xor(expert_row.astype(jnp.int32), d) * cap + slot_row
    flat_col = row_to_col(flat_x.astype(F32)).astype(jnp.int32)
    for r in order:
        send_prod(r).wait_recv()
    prod_own.wait()
    for i in range(tok // 128):
        at = slice(i * 128, (i + 1) * 128)
        pick = (flat_col[at] == lax.broadcasted_iota(jnp.int32, (128, slots), 1)).astype(F32).astype(BF16)
        mixed_o[at, :] = (res[at, :] + gate_ref[at, :] * dot(pick, prodr[...])).astype(BF16)

    gain, bias = g1_ref[...][None, :], b1_ref[...][None, :]
    gain_sum = jnp.zeros((1, width), F32)
    bias_sum = jnp.zeros((1, width), F32)
    for i in range(pieces):
        own = normed_piece(h, i)
        gn_sib[0][i].wait_recv()
        own = own + grecv[0, part(i), :].astype(F32)
        gn_cross[i].wait_recv()
        own = own + grecv[2, part(i), :].astype(F32)
        at = slice(i * piece, (i + 1) * piece)
        _, scaled, inverse = normalize(x_ref[at, :].astype(F32), gain, bias)
        gain_sum += jnp.sum(own * scaled, axis=0, keepdims=True)
        bias_sum += jnp.sum(own, axis=0, keepdims=True)
        igrad_o[at, :] = gres[at, :] + norm_backward(own, scaled, inverse, gain)
    en[0:1, :] = gain_sum
    en[1:2, :] = bias_sum
    en_head = [remote(en, enr.at[k], eh_s.at[k], eh_r.at[k], at_head(k)) for k in (1, 2, 3)]
    for copy in en_head:
        copy.start()
    up_cross[1].start()
    for copy in en_head:
        copy.wait_recv()
    ent[...] = en[...] + enr[1] + enr[2] + enr[3]
    en_dp = [remote(ent, enq.at[r], ed_s.at[r], ed_r.at[r], at_dp(r)) for r in range(1, n_dp)]
    for copy in en_dp:
        copy.start()

    for r in pair_order:
        send_qg(r).wait_recv()
    for r in order:
        send_qb(r).wait_recv()
        send_sm(r).wait_recv()
    total = comb[comb_rows(d), :].astype(F32) + combx[place].astype(F32)
    for r in range(1, pairs):
        total += combr[r].astype(F32)
    comb_o[...] = total
    sums = qb[...]
    for r in range(1, n_dp):
        sums += qbr[r]
    qb_o[...] = sums
    total = smt[d]
    for r in range(1, n_dp):
        total += smd[r]
    sums_o[...] = total
    for copy in bg_head:
        copy.wait_recv()
    bgs_o[...] = bg_ref[h] + bgr[1] + bgr[2] + bgr[3]
    for copy in en_dp:
        copy.wait_recv()
    total = ent[...]
    for r in range(1, n_dp):
        total += enq[r]
    ends_o[...] = total

    for k in (1, 2, 3):
        send_ctx(k).wait_send()
    for r in order:
        send_prod(r).wait_send()
        send_qb(r).wait_send()
        send_sm(r).wait_send()
    for r in pair_order:
        send_qg(r).wait_send()
    for j in range(pairs):
        send_side(j).wait_send()
    for copy in up_cross:
        copy.wait()
    pg_cross.wait_send()
    for copy in pg_sib + gn_cross + gn_sib[0] + gn_sib[1] + sm_head + bg_head + en_head + en_dp:
        copy.wait_send()


def stage_b(n_dp, gctx, qkv, probs, ctx, ctxf, gath, w, x, g1, b1, gres, res, gate, routes, prod, upc, sm, bg):
    tok, width = x.shape
    _, heads, group, hd = qkv.shape
    cols = heads * hd
    span = probs.shape[3]
    share = width // n_dp
    sds = jax.ShapeDtypeStruct
    vm = pltpu.VMEM
    packed = width * 3 // 2
    return pl.pallas_call(
        functools.partial(kernel_b, n_dp),
        out_shape=(
            sds((tok, width), BF16),
            sds((tok, width), F32),
            sds(upc.shape, BF16),
            sds((share, width), F32),
            sds((1, 2 * cols), F32),
            sds((sm.shape[0], 128), F32),
            sds((2, width), F32),
            sds(bg.shape[1:], F32),
        ),
        in_specs=[VM, ANY, ANY, VM, VM, ANY] + [VM] * 8 + [ANY, ANY, VM, VM],
        out_specs=(VM, VM, ANY) + (VM,) * 5,
        scratch_shapes=[
            vm(gctx.shape, BF16), vm((3, heads, group, hd), BF16), vm((3, heads, TILE, span), BF16), vm((group, width), BF16),
            vm(prod.shape, BF16), vm((cols, group), F32), vm((cols, group), F32), vm((group, 3 * cols), BF16), vm((3 * cols, group), BF16),
            vm((2, tok, width), BF16), vm((tok, width), BF16), vm((3, tok, width), BF16),
            vm((width, 4 * cols), BF16), vm((n_dp // 2, share, 4 * cols), BF16), vm((n_dp // 2, share, 4 * cols), BF16),
            vm((n_dp // 2, share, 4 * cols), BF16),
            vm((3, packed, 128), BF16), vm((3, packed, 128), BF16), vm((packed, 128), F32),
            vm((1, 2 * cols), F32), vm((n_dp, 1, 2 * cols), F32),
            vm((4,) + sm.shape, F32), vm((n_dp, sm.shape[0], 128), F32), vm((n_dp, sm.shape[0], 128), F32),
            vm((2, width), F32), vm((4, 2, width), F32), vm((2, width), F32), vm((n_dp, 2, width), F32),
            vm((4,) + bg.shape[1:], F32),
            DMA((2,)), DMA((3,)), DMA((4,)), DMA((4,)), DMA((n_dp,)), DMA((n_dp,)), DMA((2,)), DMA((2,)), DMA((2, 2)), DMA((2, 2)),
            DMA((2,)), DMA((2,)), DMA((n_dp // 2,)), DMA((n_dp // 2,)), DMA((n_dp // 2,)), DMA((n_dp // 2,)), DMA((3,)), DMA((3,)),
            DMA((n_dp,)), DMA((n_dp,)),
            DMA((4,)), DMA((4,)), DMA((n_dp,)), DMA((n_dp,)), DMA((4,)), DMA((4,)), DMA((n_dp,)), DMA((n_dp,)), DMA((4,)), DMA((4,)),
        ],
        compiler_params=pltpu.CompilerParams(collective_id=2, has_side_effects=True, vmem_limit_bytes=VMEM_LIMIT),
    )(gctx, qkv, probs, ctx, ctxf, gath, w.transpose(0, 2, 1), x, g1, b1, gres, res, gate, routes.T, prod, upc, sm, bg)


def kernel_f(
    n_dp, mixed, igrad, upo, upr, dno, dnr, comb, qb, sums, ends, bgs, bal,
    mixed_o, bal_o, igrad_o, g1_o, b1_o, qkv_o, qkvb_o, proj_o, pb_o, g2_o, b2_o, router_o, up_o, upb_o, down_o, downb_o,
):
    mixed_o[...] = mixed[...]
    igrad_o[...] = igrad[...]
    up_o[0] = upo[...].astype(F32) + upr[...].astype(F32)
    down_o[0] = dno[...].astype(F32) + dnr[...].astype(F32)

    @pl.when(pl.program_id(0) == 0)
    def _():
        d = lax.axis_index("dp")
        device = d * 4 + lax.axis_index("head")
        width = ends.shape[1]
        part = g1_o.shape[0]
        cols = qkv_o.shape[2]
        hd = cols // 3
        share = qkvb_o.shape[2]
        bal_o[...] = bal[0]
        shift = lax.rem(width - device * part, width)
        mine = pltpu.roll(sums[...], lax.rem(128 - lax.axis_index("head") * part, 128), 1)[:, :part]
        tail = pltpu.roll(jnp.concatenate([ends[...], jnp.zeros((6, width), F32)], axis=0), shift, 1)[:, :part]
        g1_o[...] = tail[0]
        b1_o[...] = tail[1]
        g2_o[...] = mine[0]
        b2_o[...] = mine[1]
        pb_o[...] = mine[2]
        router_o[...] = mine[8 : 8 + n_dp]
        for c in range(3):
            qkv_o[c] = comb[:, c * cols : (c + 1) * cols]
        proj_o[...] = comb[:, 3 * cols :].T
        turned = pltpu.roll(jnp.broadcast_to(qb[...], (8, 2 * cols)), lax.rem(2 * cols - d * share, 2 * cols), 1)
        for a in range(3):
            for c in range(2):
                at = c * cols + a * hd
                qkvb_o[a, c : c + 1, :] = turned[:1, at : at + share]
        upb_o[...] = bgs[0:1, :]
        downb_o[...] = bgs[1:2, : downb_o.shape[1]]


def stage_f(n_dp, mixed, igrad, upo, upr, dno, dnr, comb, qb, sums, ends, bgs, bal):
    tok, width = mixed.shape
    cols = qb.shape[1] // 2
    part = width // (4 * n_dp)
    share = width // n_dp
    steps = 4
    sds = jax.ShapeDtypeStruct

    def rows(shape):
        if len(shape) == 3:
            return pl.BlockSpec((1, shape[1] // steps, shape[2]), lambda i: (0, i, 0))
        return pl.BlockSpec((shape[0] // steps, shape[1]), lambda i: (i, 0))

    def whole(shape):
        return pl.BlockSpec(shape, lambda i: (0,) * len(shape))

    args = (mixed, igrad, upo, upr, dno, dnr, comb, qb, sums, ends, bgs, bal)
    outs = (
        sds((tok, width), BF16), sds((1,), F32), sds((tok, width), F32), sds((part,), F32), sds((part,), F32),
        sds((3, share, cols), F32), sds((3, 2, cols // 3 // n_dp), F32), sds((cols, share), F32), sds((part,), F32), sds((part,), F32),
        sds((part,), F32), sds((n_dp, part), F32), sds((1,) + upo.shape, F32), sds((1, upo.shape[1]), F32),
        sds((1,) + dno.shape, F32), sds((1, width // 4), F32),
    )
    return pl.pallas_call(
        functools.partial(kernel_f, n_dp),
        out_shape=outs,
        grid=(steps,),
        in_specs=[rows(a.shape) for a in args[:6]] + [whole(a.shape) for a in args[6:]],
        out_specs=tuple(rows(o.shape) if i in (0, 2, 12, 14) else whole(o.shape) for i, o in enumerate(outs)),
        compiler_params=pltpu.CompilerParams(vmem_limit_bytes=VMEM_LIMIT),
    )(*args)


def local(
    block_input, norm1_gain, norm1_bias, qkv_weight, qkv_bias, proj_weight, proj_bias, norm2_gain, norm2_bias, router_weight,
    up_weight, up_bias, down_weight, down_bias, routes, lengths, cotangent,
):
    tok, width = block_input.shape
    experts = router_weight.shape[1]
    cap = 2 * tok // experts
    gath, qkv, probs, ctx, ctxf, projf, cots = stage_a(
        experts, block_input, norm1_gain, norm1_bias, qkv_weight, qkv_bias, proj_weight, routes, cotangent, lengths, cap
    )
    res, gate, prod, gres, gctx, upc, upo, dno, dnr, sm, bg, balance = stage_m(
        experts, block_input, ctxf, projf, proj_bias, norm2_gain, norm2_bias, router_weight, routes, cotangent, cots,
        up_weight, up_bias, down_weight, down_bias,
    )
    mixed, igrad, upr, comb, qb, sums, ends, bgs = stage_b(
        experts, gctx, qkv, probs, ctx, ctxf, gath, qkv_weight, block_input, norm1_gain, norm1_bias, gres, res, gate, routes, prod,
        upc, sm, bg,
    )
    outs = list(stage_f(experts, mixed, igrad, upo, upr, dno, dnr, comb, qb, sums, ends, bgs, balance))
    outs[6] = outs[6].transpose(1, 0, 2)
    outs[11] = outs[11].T
    return tuple(outs)


def solution(mesh):
    placed = (
        P(("dp", "head"), None), P(), P(), P(None, None, "head"), P(None, "head", None), P("head", None), P(), P(), P(), P(),
        P("dp", None, None), P("dp", None), P("dp", None, None), P("dp", None), P(("dp", "head"), None), P("dp", None),
        P(("dp", "head"), None),
    )
    tokens = P(("dp", "head"))
    return jax.shard_map(
        local,
        mesh=mesh,
        in_specs=placed,
        out_specs=(
            P(("dp", "head"), None), tokens, P(("dp", "head"), None), tokens, tokens, P(None, "dp", "head"), P(None, "head", "dp"),
            P("head", "dp"), tokens, tokens, tokens, P(("dp", "head"), None), P("dp", None, "head"), P("dp", "head"),
            P("dp", "head", None), P("dp", "head"),
        ),
        check_vma=False,
    )
```

```python
import functools
import jax
import jax.numpy as jnp
from jax import lax
from jax.experimental import pallas as pl
from jax.experimental.pallas import tpu as pltpu
from jax.sharding import PartitionSpec as P

EPSILON = 1e-05
BAL_COEF = 0.01
HIGHEST = lax.Precision.HIGHEST
NEG_LARGE = -1e30
MESH = pl.DeviceIdType.MESH
F32 = jnp.float32
BF16 = jnp.bfloat16
TILE = 256
VMEM_LIMIT = 60 << 20
UNROLL_A = True
UNROLL_B = False


def flip(index, bits):
    out, bit = index, 1
    while bit <= bits:
        if bits & bit:
            out = out + bit - 2 * bit * lax.rem(lax.div(index, bit), 2)
        bit *= 2
    return out


def remote(src, dst, send_sem, recv_sem, device):
    return pltpu.make_async_remote_copy(
        src_ref=src, dst_ref=dst, send_sem=send_sem, recv_sem=recv_sem, device_id=device, device_id_type=MESH
    )


def dot(left, right, dims=((1,), (0,)), precision=None):
    return lax.dot_general(left, right, (dims, ((), ())), precision=precision, preferred_element_type=F32)


def normalize(values, gain, bias):
    average = jnp.mean(values, axis=-1, keepdims=True)
    centred = values - average
    variance = jnp.mean(centred * centred, axis=-1, keepdims=True)
    inverse = lax.rsqrt(variance + EPSILON)
    scaled = centred * inverse
    return (scaled * gain + bias, scaled, inverse)


def norm_backward(grad_normed, scaled, inverse, gain):
    grad_scaled = grad_normed * gain
    first_mean = jnp.mean(grad_scaled, axis=-1, keepdims=True)
    second_mean = jnp.mean(grad_scaled * scaled, axis=-1, keepdims=True)
    return inverse * (grad_scaled - first_mean - scaled * second_mean)


def slot_layouts(routes, experts, cap):
    rows = routes.shape[1]
    count = max(8, experts)
    expert = lax.broadcasted_iota(jnp.int32, (count, rows), 0)
    hot = (routes == expert).astype(F32)
    upto = lax.broadcasted_iota(jnp.int32, (rows, rows), 0) <= lax.broadcasted_iota(jnp.int32, (rows, rows), 1)
    rank = dot(hot.astype(BF16), upto.astype(F32).astype(BF16))
    slot_row = jnp.sum((rank - 1.0) * hot, axis=0, keepdims=True)
    flat_row = jnp.sum((rank - 1.0 + cap * expert.astype(F32)) * hot, axis=0, keepdims=True)
    return hot, flat_row.astype(jnp.int32), slot_row.astype(jnp.int32)


def barrier_signal(peers):
    barrier = pltpu.get_barrier_semaphore()
    for peer in peers:
        pl.semaphore_signal(barrier, inc=1, device_id=peer, device_id_type=MESH)


def barrier_wait(count):
    pl.semaphore_wait(pltpu.get_barrier_semaphore(), count)


def kernel_a(
    n_dp, x_ref, g1_ref, b1_ref, w_ref, qb_ref, proj_ref, routes_ref, cot_ref, len_ref,
    gath_o, qkv_o, p_o, ctx_o, ctxf_o, projf_o, cots_o,
    gath, qkv, p_st, bias_s, ctx_s, out_s, disp,
    ag_s, ag_r, pj_s, pj_r, cx_s, cx_r, ct_s, ct_r, p_sem, loc,
):
    tok, width = x_ref.shape
    heads = qb_ref.shape[0]
    hd = qb_ref.shape[2]
    group = 4 * tok
    tiles = group // TILE
    reach = group // 2 // TILE + 1
    cap = cots_o.shape[0] // n_dp
    d = lax.axis_index("dp")
    h = lax.axis_index("head")
    barrier_signal([(d, flip(h, k)) for k in (1, 2, 3)] + [(flip(d, r), h) for r in range(1, n_dp)])

    def block(index):
        return pl.ds(pl.multiple_of(index * tok, tok), tok)

    gain, bias = g1_ref[...][None, :], b1_ref[...][None, :]

    def norm_rows(i, carry):
        normed, _, _ = normalize(x_ref[pl.ds(pl.multiple_of(i * 64, 64), 64), :].astype(F32), gain, bias)
        gath[pl.ds(pl.multiple_of(h * tok + i * 64, 64), 64), :] = normed.astype(BF16)
        return carry

    lax.fori_loop(0, tok // 64, norm_rows, 0)
    barrier_wait(3 + n_dp - 1)

    chunks = 4
    step = tok // chunks

    def part(index, i):
        return gath.at[pl.ds(pl.multiple_of(index * tok + i * step, step), step), :]

    sib, cross, diag = flip(h, 1), flip(h, 2), flip(h, 3)
    to_cross = [remote(part(h, i), part(h, i), ag_s.at[i], ag_r.at[i], (d, cross)) for i in range(chunks)]
    to_sib = remote(gath.at[block(h), :], gath.at[block(h), :], ag_s.at[2 * chunks], ag_r.at[2 * chunks], (d, sib))
    onward = [
        remote(part(cross, i), part(cross, i), ag_s.at[chunks + i], ag_r.at[chunks + i], (d, sib)) for i in range(chunks)
    ]
    for copy in to_cross:
        copy.start()
    to_sib.start()
    proj_copies = [
        remote(proj_ref, projf_o.at[h], pj_s.at[k], pj_r.at[k], (d, flip(h, k))) for k in (1, 2, 3)
    ]

    hot_t, flat_row, slot_row = slot_layouts(routes_ref[...], n_dp, cap)
    slot_iota = lax.broadcasted_iota(jnp.int32, (cap, tok), 0)

    def dispatch(e, carry):
        hot = (flat_row == slot_iota + e * cap).astype(F32).astype(BF16)
        disp[pl.ds(pl.multiple_of(e * cap, cap), cap), :] = dot(hot, cot_ref[...]).astype(BF16)
        return carry

    lax.fori_loop(0, n_dp, dispatch, 0)

    def slots(index):
        return pl.ds(pl.multiple_of(index * cap, cap), cap)

    cot_copies = [
        remote(disp.at[slots(flip(d, r)), :], cots_o.at[pl.ds(r * cap, cap), :], ct_s.at[r], ct_r.at[r], (flip(d, r), h))
        for r in range(1, n_dp)
    ]
    for copy in cot_copies:
        copy.start()
    cot_own = pltpu.make_async_copy(disp.at[slots(d), :], cots_o.at[pl.ds(0, cap), :], ct_s.at[0])
    cot_own.start()

    def project(index):
        def rows_of(i, carry):
            at = pl.ds(pl.multiple_of(index * tok + i * TILE, TILE), TILE)
            rows = gath[at, :]
            for c in range(3):
                out = dot(rows, w_ref[c], ((1,), (1,)))
                for a in range(heads):
                    piece = out[:, a * hd : (a + 1) * hd]
                    if c != 1:
                        piece = piece + qb_ref[a, c // 2 : c // 2 + 1, :]
                    piece = piece.astype(BF16)
                    if c == 0:
                        piece = piece * jnp.asarray(hd ** (-0.5), BF16)
                    qkv[c, a, at, :] = piece
            return carry

        lax.fori_loop(0, tok // TILE, rows_of, 0)

    project(h)
    to_sib.wait_recv()
    project(sib)
    for i in range(chunks):
        to_cross[i].wait_recv()
        onward[i].start()
    for copy in proj_copies:
        copy.start()
    proj_own = pltpu.make_async_copy(proj_ref, projf_o.at[h], loc.at[0])
    proj_own.start()
    project(cross)
    for i in range(chunks):
        onward[i].wait_recv()
    project(diag)
    gath_copy = pltpu.make_async_copy(gath, gath_o, loc.at[1])
    gath_copy.start()
    qkv_copy = pltpu.make_async_copy(qkv, qkv_o, loc.at[2])
    qkv_copy.start()

    ends = [len_ref[0, 0]]
    for i in range(1, len_ref.shape[1] - 1):
        ends.append(ends[-1] + len_ref[0, i])

    per_block = tok // TILE
    size_t = TILE * 3 // 2
    low_tiles = reach - 1

    def p_copy(t, a, size):
        return pltpu.make_async_copy(p_st.at[a, :, pl.ds(0, size)], p_o.at[a, t, :, pl.ds(0, size)], p_sem.at[a])

    def ctx_rows(t):
        return pl.ds(pl.multiple_of(lax.rem(t, per_block) * size_t, size_t), size_t)

    def ctx_send(t):
        owner = lax.div(t, per_block)
        return remote(ctx_s.at[t], ctxf_o.at[h, ctx_rows(t), :], cx_s.at[t], cx_r.at[h, lax.rem(t, per_block)], (d, owner))

    def ctx_keep(t):
        return pltpu.make_async_copy(ctx_s.at[t], ctxf_o.at[h, ctx_rows(t), :], cx_s.at[t])

    def tile_step(t, size, before, unrolled):
        first = (t + 1) * TILE - size
        rows = pl.ds(pl.multiple_of(t * TILE, TILE), TILE)
        win = pl.ds(pl.multiple_of(first, TILE), size)
        row = t * TILE + lax.broadcasted_iota(jnp.int32, (TILE, 1), 0)
        start = jnp.zeros((TILE, 1), jnp.int32)
        for end in ends:
            start = jnp.where(row >= end, end, start)
        col = first + lax.broadcasted_iota(jnp.int32, (TILE, size), 1)
        bias_s[:, :size] = jnp.where((col >= start) & (col <= row), 0.0, NEG_LARGE)

        def attend(a, carry):
            s = dot(qkv[0, a, rows, :], qkv[1, a, win, :], ((1,), (1,))) + bias_s[:, :size]
            top = jnp.max(s, axis=1, keepdims=True)
            e = jnp.exp(s - top)
            total = jnp.sum(e, axis=1, keepdims=True)
            p = (e * (1.0 / total)).astype(BF16)
            if before:
                p_copy(t, a, before).wait()
            p_st[a, :, :size] = p
            p_copy(t, a, size).start()
            out_s[a] = dot(p, qkv[2, a, win, :])
            return carry

        if unrolled:
            for a in range(heads):
                attend(a, 0)
        else:
            lax.fori_loop(0, heads, attend, 0)
        ctx_s[t] = pack([out_s[a] for a in range(heads)]).astype(BF16)

        @pl.when(h != lax.div(t, per_block))
        def _():
            ctx_send(t).start()

        @pl.when(h == lax.div(t, per_block))
        def _():
            ctx_keep(t).start()

    before = 0
    for t in range(low_tiles):
        tile_step(t, (t + 1) * TILE, before, False)
        before = (t + 1) * TILE
    span = reach * TILE
    p_st[:, :, before:] = jnp.zeros((heads, TILE, span - before), BF16)
    for a in range(heads):
        p_copy(low_tiles - 1, a, before).wait()
        p_copy(low_tiles - 1, a, span).start()

    def high_tile(t, carry):
        tile_step(t, span, span, UNROLL_A)
        return carry

    lax.fori_loop(low_tiles, tiles, high_tile, 0)
    ctx_copy = pltpu.make_async_copy(ctx_s, ctx_o, loc.at[3])
    ctx_copy.start()
    for a in range(heads):
        p_copy(tiles - 1, a, span).wait()

    def sent(t, carry):
        @pl.when(h != lax.div(t, per_block))
        def _():
            ctx_send(t).wait_send()

        @pl.when(h == lax.div(t, per_block))
        def _():
            ctx_keep(t).wait()

        return carry

    lax.fori_loop(0, tiles, sent, 0)
    for k in (1, 2, 3):
        peer = flip(h, k)
        for sub in range(per_block):
            remote(
                ctx_s.at[0], ctxf_o.at[peer, pl.ds(sub * (TILE * 3 // 2), TILE * 3 // 2), :], cx_s.at[0], cx_r.at[peer, sub], (d, peer)
            ).wait_recv()
    for copy in to_cross:
        copy.wait_send()
    to_sib.wait_send()
    for copy in onward:
        copy.wait_send()
    for k in (1, 2, 3):
        proj_copies[k - 1].wait_send()
        peer = flip(h, k)
        remote(proj_ref, projf_o.at[peer], pj_s.at[k], pj_r.at[k], (d, peer)).wait_recv()
    for copy in cot_copies:
        copy.wait()
    for copy in (cot_own, proj_own, gath_copy, qkv_copy, ctx_copy):
        copy.wait()


VM = pl.BlockSpec(memory_space=pltpu.VMEM)
SM = pl.BlockSpec(memory_space=pltpu.SMEM)
ANY = pl.BlockSpec(memory_space=pl.ANY)
DMA = pltpu.SemaphoreType.DMA


def stage_a(n_dp, x, g1, b1, w, qb, proj, routes, cot, lengths, cap):
    tok, width = x.shape
    heads, hd = qb.shape[1:]
    w, qb, routes = w.transpose(0, 2, 1), qb.transpose(1, 0, 2), routes.T
    group = 4 * tok
    tiles = group // TILE
    span = (group // 2 // TILE + 1) * TILE
    cols = heads * hd
    sds = jax.ShapeDtypeStruct
    return pl.pallas_call(
        functools.partial(kernel_a, n_dp),
        out_shape=(
            sds((group, width), BF16),
            sds((3, heads, group, hd), BF16),
            sds((heads, tiles, TILE, span), BF16),
            sds((tiles, TILE * 3 // 2, 128), BF16),
            sds((4, tok * 3 // 2, 128), BF16),
            sds((4, cols, width), BF16),
            sds((n_dp * cap, width), BF16),
        ),
        in_specs=[VM] * 8 + [SM],
        out_specs=(ANY,) * 7,
        scratch_shapes=[
            pltpu.VMEM((group, width), BF16),
            pltpu.VMEM((3, heads, group, hd), BF16),
            pltpu.VMEM((heads, TILE, span), BF16),
            pltpu.VMEM((TILE, span), F32),
            pltpu.VMEM((tiles, TILE * 3 // 2, 128), BF16),
            pltpu.VMEM((heads, TILE, hd), F32),
            pltpu.VMEM((n_dp * cap, width), BF16),
            DMA((9,)), DMA((9,)), DMA((4,)), DMA((4,)), DMA((tiles,)), DMA((4, tok // TILE)),
            DMA((n_dp,)), DMA((n_dp,)), DMA((heads,)), DMA((4,)),
        ],
        compiler_params=pltpu.CompilerParams(collective_id=0, has_side_effects=True, vmem_limit_bytes=VMEM_LIMIT),
    )(x, g1, b1, w, qb, proj, routes, cot, lengths)


def far_first(n_dp):
    half = n_dp // 2
    return list(range(half, n_dp)) + [r for r in range(2, half)] + [1]


def gelu_parts(u):
    return 0.5 * lax.erf(u * 0.7071067811865476) + 0.5, jnp.exp(u * u * -0.5) * 0.3989422804014327


def split3(value):
    high = value.astype(BF16)
    rest = value - high.astype(F32)
    middle = rest.astype(BF16)
    return high, middle, (rest - middle.astype(F32)).astype(BF16)


def fold3(stacked):
    count = stacked.shape[0] // 3
    return stacked[:count] + stacked[count : 2 * count] + stacked[2 * count :]


def differ(index, other, count):
    out, bit = 0, 1
    while bit < count:
        one, two = lax.rem(lax.div(index, bit), 2), lax.rem(lax.div(other, bit), 2)
        out = out + bit * (one + two - 2 * one * two)
        bit *= 2
    return out


def row_to_col(row):
    return jnp.broadcast_to(row, (128, row.shape[1])).T[:, :1]


def col_to_rows(col):
    return jnp.broadcast_to(col, (col.shape[0], 128)).T[:8]


def kernel_m(
    n_dp, x_ref, ctxf, projf, pb_ref, g2_ref, b2_ref, rt_ref, routes_ref, cot_ref, cots, up_h, upb_ref, down_h, downb_ref,
    res, gate_o, prod_o, gres_o, gctx_o, upc_o, upo_o, dno_o, dnr_o, sm_o, bg_o, bal_o,
    stat, nhigh, nlow, low_s, gates_s, left_s, fcol, disp, gsend, rows, rowst, grecv, up, down, ghu, hid, gg, gacc, gin, ggs, ginr, ggr, dsend, dacc, drecv, urecv,
    ld, ra_s, ra_r, ga_s, ga_r, rb_s, rb_r, gb_s, gb_r, ds_s, ds_r, us_s, us_r, out_sem,
):
    tok, width = x_ref.shape
    ff = up.shape[1]
    slots = rows.shape[0]
    cap = slots // n_dp
    per = TILE // cap
    groups = slots // TILE
    experts = n_dp
    quarter = ff // 4
    size_t = TILE * 3 // 2
    hd = 64
    d = lax.axis_index("dp")
    h = lax.axis_index("head")
    sib, cross = (d, flip(h, 1)), (d, flip(h, 2))
    loads = [pltpu.make_async_copy(down_h.at[0], down, ld.at[0]), pltpu.make_async_copy(up_h.at[0], up, ld.at[1])]
    for copy in loads:
        copy.start()
    barrier_signal([(d, flip(h, k)) for k in (1, 2, 3)] + [(flip(d, r), h) for r in range(1, n_dp)])

    proj = projf[...].reshape(width, width)
    for i in range(tok // TILE):
        heads = []
        for b in range(4):
            heads += unpack(ctxf[b, i * size_t : (i + 1) * size_t, :])
        at = slice(i * TILE, (i + 1) * TILE)
        res[at, :] = x_ref[at, :].astype(F32) + dot(jnp.concatenate(heads, axis=1), proj) + pb_ref[...][None, :]
    gain, bias = g2_ref[...][None, :], b2_ref[...][None, :]
    chunk = 64

    def norm_rows(i, carry):
        at = pl.ds(pl.multiple_of(i * chunk, chunk), chunk)
        residual = res[at, :]
        average = jnp.mean(residual, axis=-1, keepdims=True)
        centred = residual - average
        inverse = lax.rsqrt(jnp.mean(centred * centred, axis=-1, keepdims=True) + EPSILON)
        stat[0, at, :] = average
        stat[1, at, :] = inverse
        normed = centred * inverse * gain + bias
        high = normed.astype(BF16)
        nhigh[at, :] = high
        nlow[at, :] = (normed - high.astype(F32)).astype(BF16)
        return carry

    lax.fori_loop(0, tok // chunk, norm_rows, 0)

    router3 = jnp.concatenate(split3(rt_ref[...]), axis=0)
    logits = fold3(dot(router3, nhigh[...], ((1,), (1,))) + dot(router3, nlow[...], ((1,), (1,))))
    raised = jnp.exp(logits - jnp.max(logits, axis=0, keepdims=True))
    prob = raised / jnp.sum(raised, axis=0, keepdims=True)
    hot, flat_row, slot_row = slot_layouts(routes_ref[...], experts, cap)
    gate_row = jnp.sum(prob * hot, axis=0, keepdims=True)
    gate_o[...] = row_to_col(gate_row)
    fraction = jnp.mean(hot, axis=1, keepdims=True)
    bal_o[...] = experts * jnp.sum(fraction * jnp.mean(prob, axis=1, keepdims=True), axis=0, keepdims=True)

    expert_row = jnp.sum(hot * lax.broadcasted_iota(jnp.int32, hot.shape, 0).astype(F32), axis=0, keepdims=True)
    other_row = jnp.bitwise_xor(expert_row.astype(jnp.int32), d)
    flat_x = other_row * cap + slot_row
    at_slot = (slot_row == lax.broadcasted_iota(jnp.int32, (128, tok), 0)).astype(F32).astype(BF16)
    other_hot = (other_row == lax.broadcasted_iota(jnp.int32, hot.shape, 0)).astype(F32)
    gates3 = jnp.concatenate([other_hot * part.astype(F32) for part in split3(gate_row)], axis=0).astype(BF16)
    gates = fold3(dot(gates3, at_slot, ((1,), (1,))))
    barrier_wait(3 + n_dp - 1)
    order = far_first(n_dp)

    def slot_block(r):
        return pl.ds(pl.multiple_of(r * cap, cap), cap)

    def send_rows(r):
        at = slot_block(r)
        return remote(disp.at[at, :], rows.at[at, :], ra_s.at[r], ra_r.at[r], (differ(d, r, n_dp), h))

    def send_gate(r):
        return remote(gsend.at[r], grecv.at[r], ga_s.at[r], ga_r.at[r], (differ(d, r, n_dp), h))

    slot_iota = lax.broadcasted_iota(jnp.int32, (cap, tok), 0)

    gates_s[...] = gates

    def fill(i, carry):
        r = lax.rem(i + n_dp // 2, n_dp)
        hits = (flat_x == slot_iota + r * cap).astype(F32).astype(BF16)
        gsend[r] = jnp.broadcast_to(gates_s[pl.ds(r, 1), :], (8, 128))
        block = dot(hits, nhigh[...]).astype(BF16)

        @pl.when(r != 0)
        def _():
            disp[slot_block(r), :] = block
            send_rows(r).start()
            send_gate(r).start()

        @pl.when(r == 0)
        def _():
            rows[:cap, :] = block
            grecv[0] = gsend[0]

        return carry

    lax.fori_loop(0, n_dp, fill, 0)

    loads[0].wait()

    def hidden_grad(i, carry):
        at = pl.ds(pl.multiple_of(lax.div(i, 4) * TILE, TILE), TILE)
        cols = pl.ds(pl.multiple_of(lax.rem(i, 4) * quarter, quarter), quarter)
        ghu[at, cols] = dot(cots[at, :], down[cols, :], ((1,), (1,))).astype(BF16)
        return carry

    lax.fori_loop(0, 4 * groups, hidden_grad, 0)
    loads[1].wait()

    step = quarter

    def send_back(r):
        at = slot_block(r)
        return remote(gin.at[at, :], ginr.at[at, :], rb_s.at[r], rb_r.at[r], (differ(d, r, n_dp), h))

    def send_gg(r):
        return remote(ggs.at[lax.div(r, per)], ggr.at[r], gb_s.at[r], gb_r.at[r], (differ(d, r, n_dp), h))

    def group_step(g, carry):
        for i in range(per):
            r = g * per + i

            @pl.when(r != 0)
            def _():
                send_rows(r).wait_recv()
                send_gate(r).wait_recv()

        at = pl.ds(pl.multiple_of(g * TILE, TILE), TILE)
        gate = jnp.concatenate([grecv[g * per + i].T[:cap, :1] for i in range(per)], axis=0)
        gacc[...] = jnp.zeros_like(gacc)
        gg[...] = jnp.zeros_like(gg)

        def expert(f, carry):
            cols = pl.ds(pl.multiple_of(f * step, step), step)
            u = dot(rows[at, :], up[:, cols]) + upb_ref[:, cols]
            share, density = gelu_parts(u)
            low = (u * share).astype(BF16)
            back = ghu[at, cols].astype(F32)
            hid[at, cols] = low
            meet = low.astype(F32) * back
            folded = meet[:, :128]
            for j in range(1, step // 128):
                folded += meet[:, j * 128 : (j + 1) * 128]
            gg[...] += folded
            pre = (gate * back * (share + u * density)).astype(BF16)
            ghu[at, cols] = pre
            gacc[...] += dot(pre, up[:, cols], ((1,), (1,)))
            return carry

        lax.fori_loop(0, ff // step, expert, 0)
        gin[at, :] = gacc[...].astype(BF16)
        cot_g = cots[at, :].astype(F32)
        gg_col = jnp.sum(gg[...], axis=1, keepdims=True) + jnp.sum(cot_g * downb_ref[...], axis=1, keepdims=True)
        ggs[g] = col_to_rows(gg_col)
        for i in range(per):
            r = g * per + i

            @pl.when(r != 0)
            def _():
                send_back(r).start()
                send_gg(r).start()

        cots[at, :] = (gate * cot_g).astype(BF16)
        rowst[:, at] = flip_t(rows[at, :])
        return carry

    lax.fori_loop(0, groups, group_step, 0)
    ginr[:cap, :] = gin[:cap, :]
    ggr[0] = ggs[0]

    third = quarter // 3

    def block_cols(index):
        return pl.ds(pl.multiple_of(index * quarter, quarter), quarter)

    def down_block(index, ref):
        def body(i, carry):
            cols = pl.ds(pl.multiple_of(index * quarter + i * third, third), third)
            ref[pl.ds(pl.multiple_of(i * third, third), third), :] = dot(hid[:, cols], cots[...], ((0,), (0,))).astype(BF16)
            return carry

        lax.fori_loop(0, 3, body, 0)

    def up_block(index, ref):
        part = width // 3

        def body(i, carry):
            at = pl.ds(pl.multiple_of(i * part, part), part)
            ref[at, :] = dot(rowst[at, :], ghu[:, block_cols(index)]).astype(BF16)
            return carry

        lax.fori_loop(0, 3, body, 0)

    def add_into(ref, other):
        def body(i, carry):
            at = pl.ds(pl.multiple_of(i * 64, 64), 64)
            ref[at, :] = (ref[at, :].astype(F32) + other[at, :].astype(F32)).astype(BF16)
            return carry

        lax.fori_loop(0, ref.shape[0] // 64, body, 0)

    down_sib = [remote(dsend.at[i], drecv.at[i], ds_s.at[i], ds_r.at[i], sib) for i in range(2)]
    down_cross = remote(dacc, dnr_o, ds_s.at[2], ds_r.at[2], cross)
    up_sib = [remote(dsend.at[i], urecv.at[i], us_s.at[i], us_r.at[i], sib) for i in range(2)]
    down_block(flip(h, 3), dsend.at[1])
    down_sib[1].start()
    down_block(flip(h, 2), dacc)
    down_sib[1].wait_recv()
    add_into(dacc, drecv.at[1])
    down_cross.start()
    down_block(flip(h, 1), dsend.at[0])
    down_sib[0].start()
    for r in order:
        send_rows(r).wait_send()

    def produce(i, carry):
        at = pl.ds(pl.multiple_of(i * TILE, TILE), TILE)
        disp[at, :] = (dot(hid[at, :], down[...]) + downb_ref[...]).astype(BF16)
        return carry

    lax.fori_loop(0, groups, produce, 0)
    prod_copy = pltpu.make_async_copy(disp, prod_o, out_sem.at[0])
    prod_copy.start()
    for copy in down_sib:
        copy.wait_send()
    up_block(flip(h, 3), dsend.at[1])
    up_sib[1].start()
    up_block(flip(h, 1), dsend.at[0])
    up_sib[0].start()
    up_block(flip(h, 2), upc_o)
    up_block(h, upo_o)
    down_block(h, dno_o)
    ones = jnp.ones((8, slots), BF16)
    up_bias = dot(ones, ghu[...])
    down_bias = dot(ones, cots[...])
    short = width // 4
    for b in range(4):
        bg_o[b, 0:1, :] = up_bias[:1, b * quarter : (b + 1) * quarter]
        bg_o[b, 1:2, :short] = down_bias[:1, b * short : (b + 1) * short]
    up_sib[1].wait_recv()
    add_into(upc_o, urecv.at[1])
    up_sib[0].wait_recv()
    add_into(upo_o, urecv.at[0])
    down_sib[0].wait_recv()
    add_into(dno_o, drecv.at[0])

    flat_col = row_to_col(flat_x.astype(F32)).astype(jnp.int32)
    for r in order:
        send_gg(r).wait_recv()
    slot_gg = [ggr[r][:1, (r % per) * cap : (r % per) * cap + cap] for r in range(n_dp)]
    slot_gg = jnp.concatenate(slot_gg, axis=0)
    grad_gate = jnp.sum(
        fold3(dot(jnp.concatenate(split3(slot_gg), axis=0), at_slot[:cap])) * other_hot, axis=0, keepdims=True
    )
    grad_prob = hot * grad_gate + (BAL_COEF * experts / tok) * fraction
    grad_logits = prob * (grad_prob - jnp.sum(prob * grad_prob, axis=0, keepdims=True))
    high, middle, low = split3(grad_logits)
    grads3 = jnp.concatenate([high, middle, low], axis=0)
    r_high, r_middle, r_low = split3(rt_ref[...])
    inner = 6 * experts
    padded = -(-inner // 128) * 128
    left = [v.astype(F32) for v in (high, high, high, middle, middle, low)]
    left = jnp.concatenate(left + [jnp.zeros((padded - inner, tok), F32)], axis=0).T.astype(BF16)
    right = jnp.concatenate([r_high, r_middle, r_low, r_high, r_middle, r_high, jnp.zeros((padded - inner, width), BF16)], axis=0)
    sm_o[...] = jnp.zeros_like(sm_o)
    sm_o[8 : 8 + experts, :] = fold3(dot(grads3, nhigh[...]) + dot(grads3, nlow[...]))
    for r in order:
        send_back(r).wait_recv()
    left_s[...] = left
    fcol[...] = flat_col
    part = 128

    def finish(i, carry):
        gain_sum, bias_sum, res_sum = carry
        at = pl.ds(pl.multiple_of(i * part, part), part)
        pick = (fcol[at, :] == lax.broadcasted_iota(jnp.int32, (part, slots), 1)).astype(F32).astype(BF16)
        grad_normed = dot(pick, ginr[...]) + dot(left_s[at, :], right)
        inverse = stat[1, at, :]
        scaled = (res[at, :] - stat[0, at, :]) * inverse
        grad_res = cot_ref[at, :].astype(F32) + norm_backward(grad_normed, scaled, inverse, gain)
        gres_o[at, :] = grad_res
        low_s[at, :] = grad_res.astype(BF16)
        return (
            gain_sum + jnp.sum(grad_normed * scaled, axis=0, keepdims=True),
            bias_sum + jnp.sum(grad_normed, axis=0, keepdims=True),
            res_sum + jnp.sum(grad_res, axis=0, keepdims=True),
        )

    gain_sum, bias_sum, res_sum = lax.fori_loop(0, tok // part, finish, (jnp.zeros((1, width), F32),) * 3)

    def turn_back(i, carry):
        back = dot(low_s[pl.ds(pl.multiple_of(i * TILE, TILE), TILE), :], proj, ((1,), (1,)))
        for b in range(4):
            outs = [back[:, (3 * b + a) * hd : (3 * b + a + 1) * hd] for a in range(3)]
            gctx_o[b, pl.ds(pl.multiple_of(i * size_t, size_t), size_t), :] = pack(outs).astype(BF16)
        return carry

    lax.fori_loop(0, tok // TILE, turn_back, 0)
    sm_o[0:1, :] = gain_sum
    sm_o[1:2, :] = bias_sum
    sm_o[2:3, :] = res_sum
    down_cross.wait()
    for copy in up_sib:
        copy.wait_send()
    for r in order:
        send_gate(r).wait_send()
        send_back(r).wait_send()
        send_gg(r).wait_send()
    prod_copy.wait()


def stage_m(n_dp, x, ctxf, projf, pb, g2, b2, router, routes, cot, cots, up, upb, down, downb):
    tok, width = x.shape
    slots = cots.shape[0]
    ff = up.shape[2]
    groups = slots // TILE
    quarter = ff // 4
    sds = jax.ShapeDtypeStruct
    vm = pltpu.VMEM
    return pl.pallas_call(
        functools.partial(kernel_m, n_dp),
        out_shape=(
            sds((tok, width), F32),
            sds((tok, 1), F32),
            sds((slots, width), BF16),
            sds((tok, width), F32),
            sds(ctxf.shape, BF16),
            sds((width, quarter), BF16),
            sds((width, quarter), BF16),
            sds((quarter, width), BF16),
            sds((quarter, width), BF16),
            sds((8 + n_dp, width), F32),
            sds((4, 8, quarter), F32),
            sds((1, 1), F32),
        ),
        in_specs=[VM] * 10 + [ANY, VM, ANY, VM],
        out_specs=(VM, VM, ANY, VM, VM, VM, VM, VM, ANY, VM, VM, VM),
        scratch_shapes=[
            vm((2, tok, 1), F32),
            vm((tok, width), BF16),
            vm((tok, width), BF16),
            vm((tok, width), BF16),
            vm((n_dp, 128), F32),
            vm((tok, -(-6 * n_dp // 128) * 128), BF16),
            vm((tok, 1), jnp.int32),
            vm((slots, width), BF16),
            vm((n_dp, 8, 128), F32),
            vm((slots, width), BF16),
            vm((width, slots), BF16),
            vm((n_dp, 8, 128), F32),
            vm((width, ff), BF16),
            vm((ff, width), BF16),
            vm((slots, ff), BF16),
            vm((slots, ff), BF16),
            vm((TILE, 128), F32),
            vm((TILE, width), F32),
            vm((slots, width), BF16),
            vm((groups, 8, TILE), F32),
            vm((slots, width), BF16),
            vm((n_dp, 8, TILE), F32),
            vm((2, quarter, width), BF16),
            vm((quarter, width), BF16),
            vm((2, quarter, width), BF16),
            vm((2, width, quarter), BF16),
            DMA((2,)), DMA((n_dp,)), DMA((n_dp,)), DMA((n_dp,)), DMA((n_dp,)), DMA((n_dp,)), DMA((n_dp,)),
            DMA((n_dp,)), DMA((n_dp,)), DMA((3,)), DMA((3,)), DMA((2,)), DMA((2,)), DMA((1,)),
        ],
        compiler_params=pltpu.CompilerParams(collective_id=1, has_side_effects=True, vmem_limit_bytes=VMEM_LIMIT),
    )(x, ctxf, projf, pb, g2, b2, router.T, routes.T, cot, cots, up, upb, down, downb)


def pack(outs):
    half = outs[2].shape[0] // 2
    return jnp.concatenate(
        [jnp.concatenate(outs[:2], axis=1), jnp.concatenate([outs[2][:half], outs[2][half:]], axis=1)], axis=0
    )


def unpack(tile):
    rows = tile.shape[0] * 2 // 3
    third = jnp.concatenate([tile[rows:, :64], tile[rows:, 64:]], axis=0)
    return [tile[:rows, :64], tile[:rows, 64:], third]


def unpack_t(tile):
    rows = tile.shape[1] * 2 // 3
    third = jnp.concatenate([tile[:64, rows:], tile[64:, rows:]], axis=1)
    return [tile[:64, :rows], tile[64:, :rows], third]


def flip_t(value):
    return value.astype(F32).T.astype(BF16)


def kernel_b(
    n_dp, gctx, qkv_h, p_h, ctx, ctxf, gath_h, w_ref, x_ref, g1_ref, b1_ref, gres, res, gate_ref, routes_ref, prod_h, upc_h, sm_ref, bg_ref,
    mixed_o, igrad_o, upr_o, comb_o, qb_o, sums_o, ends_o, bgs_o,
    gcr, qkv, p_v, gath, prodr, g_s, gt_s, qt_s, delta_s, dq_s, own_s, fcol, dkt, dvt, grads, gradst, gsend, gacc, grecv, comb, combx, comba, combr, pg, pgr, low_s,
    qb, qbr, smr, smd, smt, en, enr, ent, enq, bgr,
    ld, p_sem, gc_s, gc_r, pr_s, pr_r, uc_s, uc_r, gn_s, gn_r, gx_s, gx_r, qx_s, qx_r, qg_s, qg_r, pg_s, pg_r, qb_s, qb_r,
    sh_s, sh_r, sd_s, sd_r, eh_s, eh_r, ed_s, ed_r, bg_s, bg_r,
):
    tok, width = x_ref.shape
    heads, group, hd = qkv.shape[1:]
    cols = heads * hd
    tiles = group // TILE
    reach = group // 2 // TILE + 1
    per_block = tok // TILE
    slots = prod_h.shape[0]
    cap = slots // n_dp
    share = width // n_dp
    size_t = TILE * 3 // 2
    d = lax.axis_index("dp")
    h = lax.axis_index("head")
    sib, cross = (d, flip(h, 1)), (d, flip(h, 2))
    order = far_first(n_dp)

    def at_head(k):
        return (d, flip(h, k))

    def at_dp(r):
        return (flip(d, r), h)

    def p_load(t, size):
        return pltpu.make_async_copy(p_h.at[:, t, :, pl.ds(0, size)], p_v.at[t, :, :, pl.ds(0, size)], p_sem.at[t])

    barrier_signal([at_head(k) for k in (1, 2, 3)] + [at_dp(r) for r in range(1, n_dp)])
    load_qkv = pltpu.make_async_copy(qkv_h, qkv, ld.at[0])
    load_qkv.start()
    for t in range(tiles):
        p_load(t, min(t + 1, reach) * TILE).start()
    load_gath = pltpu.make_async_copy(gath_h, gath, ld.at[1])
    load_gath.start()
    dkt[...] = jnp.zeros_like(dkt)
    dvt[...] = jnp.zeros_like(dvt)
    barrier_wait(3 + n_dp - 1)

    def send_ctx(k):
        return remote(gctx.at[flip(h, k)], gcr.at[h], gc_s.at[k], gc_r.at[k], at_head(k))

    for k in (2, 3, 1):
        send_ctx(k).start()

    def send_prod(r):
        rows = pl.ds(r * cap, cap)
        return remote(prod_h.at[rows, :], prodr.at[rows, :], pr_s.at[r], pr_r.at[r], at_dp(r))

    for r in order:
        send_prod(r).start()
    prod_own = pltpu.make_async_copy(prod_h.at[pl.ds(0, cap), :], prodr.at[pl.ds(0, cap), :], pr_s.at[0])
    prod_own.start()
    gcr[h] = gctx[h]

    sm_head = [remote(sm_ref, smr.at[k], sh_s.at[k], sh_r.at[k], at_head(k)) for k in (1, 2, 3)]
    bg_head = [remote(bg_ref.at[flip(h, k)], bgr.at[k], bg_s.at[k], bg_r.at[k], at_head(k)) for k in (1, 2, 3)]
    up_half = width // 2
    up_cross = [
        remote(upc_h.at[pl.ds(i * up_half, up_half), :], upr_o.at[pl.ds(i * up_half, up_half), :], uc_s.at[i], uc_r.at[i], cross)
        for i in range(2)
    ]

    low_t = gres[...].T.astype(BF16)

    low_s[...] = low_t

    def proj_block(i, carry):
        index = differ(h, 3 - i, 4)
        total = []
        for j in range(per_block):
            outs = unpack(ctxf[index, j * size_t : (j + 1) * size_t, :])
            total.append(jnp.concatenate(outs, axis=1))
        out = dot(low_s[...], jnp.concatenate(total, axis=0))
        pg[3 - i] = pack([out[:, a * hd : (a + 1) * hd] for a in range(heads)]).astype(BF16)
        return carry

    lax.fori_loop(0, 4, proj_block, 0)
    pg_sib = [remote(pg.at[1 + 2 * i], pgr.at[i], pg_s.at[i], pg_r.at[i], sib) for i in range(2)]
    pg_sib[1].start()
    pg_sib[0].start()
    pg_cross = remote(pg.at[2], pgr.at[2], pg_s.at[2], pg_r.at[2], cross)
    pg_sib[1].wait_recv()
    pg[2] = (pg[2].astype(F32) + pgr[1].astype(F32)).astype(BF16)
    pg_cross.start()
    for copy in sm_head + bg_head:
        copy.start()
    load_qkv.wait()

    def wait_block(b):
        for k in (1, 2, 3):

            @pl.when(flip(h, k) == b)
            def _():
                remote(gctx.at[0], gcr.at[b], gc_s.at[k], gc_r.at[k], at_head(k)).wait_recv()

    def attention(t, size, unrolled):
        b, sub = lax.div(t, per_block), lax.rem(t, per_block)

        @pl.when(sub == 0)
        def _():
            wait_block(b)

        p_load(t, size).wait()
        rows = pl.ds(pl.multiple_of(t * TILE, TILE), TILE)
        win = pl.ds(pl.multiple_of((t + 1) * TILE - size, TILE), size)
        grad = gcr[b, pl.ds(pl.multiple_of(sub * size_t, size_t), size_t), :]
        meets = unpack(grad.astype(F32) * ctx[t].astype(F32))
        gs, gts = unpack(grad), unpack_t(flip_t(grad))
        qts = unpack_t(flip_t(pack([qkv[0, a, rows, :] for a in range(heads)])))
        for a in range(heads):
            delta_s[a] = jnp.sum(meets[a], axis=1, keepdims=True)
            g_s[a], gt_s[a], qt_s[a] = gs[a], gts[a], qts[a]

        def head(a, carry):
            p = p_v[t, a, :, :size]
            ds = (p.astype(F32) * (dot(g_s[a], qkv[2, a, win, :], ((1,), (1,))) - delta_s[a])).astype(BF16)
            dq_s[a] = dot(ds, qkv[1, a, win, :]) * (hd ** (-0.5))
            at = pl.ds(pl.multiple_of(a * hd, hd), hd)
            dkt[at, win] += dot(qt_s[a], ds)
            dvt[at, win] += dot(gt_s[a], p)
            return carry

        if unrolled:
            for a in range(heads):
                head(a, 0)
        else:
            lax.fori_loop(0, heads, head, 0)
        dq = jnp.concatenate([dq_s[a] for a in range(heads)], axis=1)
        grads[rows, :cols] = dq.astype(BF16)
        gradst[:cols, rows] = dq.T.astype(BF16)

    half = tiles // 2

    def both_halves(i, carry):
        @pl.when(i == 1)
        def _():
            up_cross[0].start()

        turn = lax.rem(i + lax.div(h, 2), 2)

        @pl.when(turn == 0)
        def _():
            for t in range(half):
                attention(t, (t + 1) * TILE, False)

        @pl.when(turn == 1)
        def _():
            def high_tile(t, inner):
                attention(t, reach * TILE, UNROLL_B)
                return inner

            lax.fori_loop(half, tiles, high_tile, 0)

        return carry

    lax.fori_loop(0, 2, both_halves, 0)

    def settle(t, carry):
        at = pl.ds(pl.multiple_of(t * TILE, TILE), TILE)
        both = jnp.concatenate([dkt[:, at], dvt[:, at]], axis=0)
        gradst[cols:, at] = both.astype(BF16)
        grads[at, cols:] = both.T.astype(BF16)
        return carry

    lax.fori_loop(0, tiles, settle, 0)

    pieces = 2
    piece = tok // pieces

    def normed_piece(index, i):
        at = pl.ds(pl.multiple_of(index * tok + i * piece, piece), piece)
        total = dot(grads[at, :cols], w_ref[0])
        for c in range(1, 3):
            total += dot(grads[at, c * cols : (c + 1) * cols], w_ref[c])
        return total

    def part(i):
        return pl.ds(pl.multiple_of(i * piece, piece), piece)

    def gn_sib(j, i):
        return remote(gsend.at[j, part(i), :], grecv.at[j, part(i), :], gn_s.at[j, i], gn_r.at[j, i], sib)

    def gn_cross(i):
        return remote(gacc.at[part(i), :], grecv.at[2, part(i), :], gx_s.at[i], gx_r.at[i], cross)

    def across(i, carry):
        gsend[1, part(i), :] = normed_piece(flip(h, 3), i).astype(BF16)
        gn_sib(1, i).start()
        mine = normed_piece(flip(h, 2), i)
        gn_sib(1, i).wait_recv()
        gacc[part(i), :] = (mine + grecv[1, part(i), :].astype(F32)).astype(BF16)
        gn_cross(i).start()
        return carry

    lax.fori_loop(0, pieces, across, 0)

    def beside(i, carry):
        gsend[0, part(i), :] = normed_piece(flip(h, 1), i).astype(BF16)
        gn_sib(0, i).start()
        own_s[part(i), :] = normed_piece(h, i)
        return carry

    lax.fori_loop(0, pieces, beside, 0)

    pg_sib[0].wait_recv()
    pg_cross.wait_recv()
    done = unpack(pg[0].astype(F32) + pgr[0].astype(F32) + pgr[2].astype(F32))
    comb[:, 3 * cols :] = jnp.concatenate(done, axis=1).astype(BF16)
    load_gath.wait()
    for c in range(3):
        comb[:, c * cols : (c + 1) * cols] = dot(gradst[c * cols : (c + 1) * cols, :], gath[...]).T.astype(BF16)
    ones = jnp.ones((8, group), BF16)
    qb[...] = jnp.concatenate([dot(ones, grads[:, :cols])[:1], dot(ones, grads[:, 2 * cols :])[:1]], axis=1)

    pairs = n_dp // 2
    side, place = lax.rem(d, 2), lax.div(d, 2)

    def comb_rows(index):
        return pl.ds(pl.multiple_of(index * share, share), share)

    def send_side(j):
        return remote(comb.at[comb_rows(2 * j + 1 - side), :], combx.at[j], qx_s.at[j], qx_r.at[j], at_dp(1))

    def send_qg(r):
        return remote(comba.at[flip(place, r)], combr.at[r], qg_s.at[r], qg_r.at[r], at_dp(2 * r))

    def send_qb(r):
        return remote(qb, qbr.at[r], qb_s.at[r], qb_r.at[r], at_dp(r))

    pair_order = list(range(pairs // 2, pairs)) + list(range(1, pairs // 2))
    for j in range(pairs):
        send_side(j).start()
    for r in order:
        send_qb(r).start()
    for copy in sm_head:
        copy.wait_recv()
    total = sm_ref[...] + smr[1] + smr[2] + smr[3]
    for e in range(n_dp):
        smt[e] = (pltpu.roll(total, width - e * share, 1) if e else total)[:, :128]

    def send_sm(r):
        return remote(smt.at[flip(d, r)], smd.at[r], sd_s.at[r], sd_r.at[r], at_dp(r))

    for r in order:
        send_sm(r).start()
    for j in range(pairs):
        send_side(j).wait_recv()
        comba[j] = (comb[comb_rows(2 * j + side), :].astype(F32) + combx[j].astype(F32)).astype(BF16)
    for r in pair_order:
        send_qg(r).start()

    hot, flat_row, slot_row = slot_layouts(routes_ref[...], n_dp, cap)
    expert_row = jnp.sum(hot * lax.broadcasted_iota(jnp.int32, hot.shape, 0).astype(F32), axis=0, keepdims=True)
    flat_x = jnp.bitwise_xor(expert_row.astype(jnp.int32), d) * cap + slot_row
    flat_col = row_to_col(flat_x.astype(F32)).astype(jnp.int32)
    for r in order:
        send_prod(r).wait_recv()
    prod_own.wait()
    fcol[...] = flat_col

    def mix(i, carry):
        at = pl.ds(pl.multiple_of(i * 128, 128), 128)
        pick = (fcol[at, :] == lax.broadcasted_iota(jnp.int32, (128, slots), 1)).astype(F32).astype(BF16)
        mixed_o[at, :] = (res[at, :] + gate_ref[at, :] * dot(pick, prodr[...])).astype(BF16)
        return carry

    lax.fori_loop(0, tok // 128, mix, 0)
    gain, bias = g1_ref[...][None, :], b1_ref[...][None, :]

    def norm_back(i, carry):
        at = pl.ds(pl.multiple_of(i * 64, 64), 64)
        own = own_s[at, :] + grecv[0, at, :].astype(F32) + grecv[2, at, :].astype(F32)
        _, scaled, inverse = normalize(x_ref[at, :].astype(F32), gain, bias)
        igrad_o[at, :] = gres[at, :] + norm_backward(own, scaled, inverse, gain)
        return (carry[0] + jnp.sum(own * scaled, axis=0, keepdims=True), carry[1] + jnp.sum(own, axis=0, keepdims=True))

    sums = (jnp.zeros((1, width), F32),) * 2
    for i in range(pieces):
        gn_sib(0, i).wait_recv()
        gn_cross(i).wait_recv()
        sums = lax.fori_loop(i * (piece // 64), (i + 1) * (piece // 64), norm_back, sums)
    gain_sum, bias_sum = sums
    en[0:1, :] = gain_sum
    en[1:2, :] = bias_sum
    en_head = [remote(en, enr.at[k], eh_s.at[k], eh_r.at[k], at_head(k)) for k in (1, 2, 3)]
    for copy in en_head:
        copy.start()
    up_cross[1].start()
    for copy in en_head:
        copy.wait_recv()
    ent[...] = en[...] + enr[1] + enr[2] + enr[3]
    en_dp = [remote(ent, enq.at[r], ed_s.at[r], ed_r.at[r], at_dp(r)) for r in range(1, n_dp)]
    for copy in en_dp:
        copy.start()

    for r in pair_order:
        send_qg(r).wait_recv()
    for r in order:
        send_qb(r).wait_recv()
        send_sm(r).wait_recv()
    total = comb[comb_rows(d), :].astype(F32) + combx[place].astype(F32)
    for r in range(1, pairs):
        total += combr[r].astype(F32)
    comb_o[...] = total
    sums = qb[...]
    for r in range(1, n_dp):
        sums += qbr[r]
    qb_o[...] = sums
    total = smt[d]
    for r in range(1, n_dp):
        total += smd[r]
    sums_o[...] = total
    for copy in bg_head:
        copy.wait_recv()
    bgs_o[...] = bg_ref[h] + bgr[1] + bgr[2] + bgr[3]
    for copy in en_dp:
        copy.wait_recv()
    total = ent[...]
    for r in range(1, n_dp):
        total += enq[r]
    ends_o[...] = total

    for k in (1, 2, 3):
        send_ctx(k).wait_send()
    for r in order:
        send_prod(r).wait_send()
        send_qb(r).wait_send()
        send_sm(r).wait_send()
    for r in pair_order:
        send_qg(r).wait_send()
    for j in range(pairs):
        send_side(j).wait_send()
    for copy in up_cross:
        copy.wait()
    pg_cross.wait_send()
    for copy in pg_sib + [gn_cross(i) for i in range(pieces)] + [gn_sib(j, i) for j in range(2) for i in range(pieces)] + sm_head + bg_head + en_head + en_dp:
        copy.wait_send()


def stage_b(n_dp, gctx, qkv, probs, ctx, ctxf, gath, w, x, g1, b1, gres, res, gate, routes, prod, upc, sm, bg):
    tok, width = x.shape
    _, heads, group, hd = qkv.shape
    cols = heads * hd
    span = probs.shape[3]
    share = width // n_dp
    sds = jax.ShapeDtypeStruct
    vm = pltpu.VMEM
    packed = width * 3 // 2
    return pl.pallas_call(
        functools.partial(kernel_b, n_dp),
        out_shape=(
            sds((tok, width), BF16),
            sds((tok, width), F32),
            sds(upc.shape, BF16),
            sds((share, width), F32),
            sds((1, 2 * cols), F32),
            sds((sm.shape[0], 128), F32),
            sds((2, width), F32),
            sds(bg.shape[1:], F32),
        ),
        in_specs=[VM, ANY, ANY, VM, VM, ANY] + [VM] * 8 + [ANY, ANY, VM, VM],
        out_specs=(VM, VM, ANY) + (VM,) * 5,
        scratch_shapes=[
            vm(gctx.shape, BF16), vm((3, heads, group, hd), BF16), vm((group // TILE, heads, TILE, span), BF16), vm((group, width), BF16),
            vm(prod.shape, BF16),
            vm((heads, TILE, hd), BF16), vm((heads, hd, TILE), BF16), vm((heads, hd, TILE), BF16), vm((heads, TILE, 1), F32),
            vm((heads, TILE, hd), F32), vm((tok, width), F32), vm((tok, 1), jnp.int32), vm((cols, group), F32), vm((cols, group), F32), vm((group, 3 * cols), BF16), vm((3 * cols, group), BF16),
            vm((2, tok, width), BF16), vm((tok, width), BF16), vm((3, tok, width), BF16),
            vm((width, 4 * cols), BF16), vm((n_dp // 2, share, 4 * cols), BF16), vm((n_dp // 2, share, 4 * cols), BF16),
            vm((n_dp // 2, share, 4 * cols), BF16),
            vm((4, packed, 128), BF16), vm((3, packed, 128), BF16), vm((width, tok), BF16),
            vm((1, 2 * cols), F32), vm((n_dp, 1, 2 * cols), F32),
            vm((4,) + sm.shape, F32), vm((n_dp, sm.shape[0], 128), F32), vm((n_dp, sm.shape[0], 128), F32),
            vm((2, width), F32), vm((4, 2, width), F32), vm((2, width), F32), vm((n_dp, 2, width), F32),
            vm((4,) + bg.shape[1:], F32),
            DMA((2,)), DMA((group // TILE,)), DMA((4,)), DMA((4,)), DMA((n_dp,)), DMA((n_dp,)), DMA((2,)), DMA((2,)), DMA((2, 2)), DMA((2, 2)),
            DMA((2,)), DMA((2,)), DMA((n_dp // 2,)), DMA((n_dp // 2,)), DMA((n_dp // 2,)), DMA((n_dp // 2,)), DMA((3,)), DMA((3,)),
            DMA((n_dp,)), DMA((n_dp,)),
            DMA((4,)), DMA((4,)), DMA((n_dp,)), DMA((n_dp,)), DMA((4,)), DMA((4,)), DMA((n_dp,)), DMA((n_dp,)), DMA((4,)), DMA((4,)),
        ],
        compiler_params=pltpu.CompilerParams(collective_id=2, has_side_effects=True, vmem_limit_bytes=VMEM_LIMIT),
    )(gctx, qkv, probs, ctx, ctxf, gath, w.transpose(0, 2, 1), x, g1, b1, gres, res, gate, routes.T, prod, upc, sm, bg)


def kernel_f(
    n_dp, mixed, igrad, upo, upr, dno, dnr, comb, qb, sums, ends, bgs, bal,
    mixed_o, bal_o, igrad_o, g1_o, b1_o, qkv_o, qkvb_o, proj_o, pb_o, g2_o, b2_o, router_o, up_o, upb_o, down_o, downb_o,
):
    mixed_o[...] = mixed[...]
    igrad_o[...] = igrad[...]
    up_o[0] = upo[...].astype(F32) + upr[...].astype(F32)
    down_o[0] = dno[...].astype(F32) + dnr[...].astype(F32)

    @pl.when(pl.program_id(0) == 0)
    def _():
        d = lax.axis_index("dp")
        device = d * 4 + lax.axis_index("head")
        width = ends.shape[1]
        part = g1_o.shape[0]
        cols = qkv_o.shape[2]
        hd = cols // 3
        share = qkvb_o.shape[2]
        bal_o[...] = bal[0]
        shift = lax.rem(width - device * part, width)
        mine = pltpu.roll(sums[...], lax.rem(128 - lax.axis_index("head") * part, 128), 1)[:, :part]
        tail = pltpu.roll(jnp.concatenate([ends[...], jnp.zeros((6, width), F32)], axis=0), shift, 1)[:, :part]
        g1_o[...] = tail[0]
        b1_o[...] = tail[1]
        g2_o[...] = mine[0]
        b2_o[...] = mine[1]
        pb_o[...] = mine[2]
        router_o[...] = mine[8 : 8 + n_dp]
        for c in range(3):
            qkv_o[c] = comb[:, c * cols : (c + 1) * cols]
        proj_o[...] = comb[:, 3 * cols :].T
        turned = pltpu.roll(jnp.broadcast_to(qb[...], (8, 2 * cols)), lax.rem(2 * cols - d * share, 2 * cols), 1)
        for a in range(3):
            for c in range(2):
                at = c * cols + a * hd
                qkvb_o[a, c : c + 1, :] = turned[:1, at : at + share]
        upb_o[...] = bgs[0:1, :]
        downb_o[...] = bgs[1:2, : downb_o.shape[1]]


def stage_f(n_dp, mixed, igrad, upo, upr, dno, dnr, comb, qb, sums, ends, bgs, bal):
    tok, width = mixed.shape
    cols = qb.shape[1] // 2
    part = width // (4 * n_dp)
    share = width // n_dp
    steps = 4
    sds = jax.ShapeDtypeStruct

    def rows(shape):
        if len(shape) == 3:
            return pl.BlockSpec((1, shape[1] // steps, shape[2]), lambda i: (0, i, 0))
        return pl.BlockSpec((shape[0] // steps, shape[1]), lambda i: (i, 0))

    def whole(shape):
        return pl.BlockSpec(shape, lambda i: (0,) * len(shape))

    args = (mixed, igrad, upo, upr, dno, dnr, comb, qb, sums, ends, bgs, bal)
    outs = (
        sds((tok, width), BF16), sds((1,), F32), sds((tok, width), F32), sds((part,), F32), sds((part,), F32),
        sds((3, share, cols), F32), sds((3, 2, cols // 3 // n_dp), F32), sds((cols, share), F32), sds((part,), F32), sds((part,), F32),
        sds((part,), F32), sds((n_dp, part), F32), sds((1,) + upo.shape, F32), sds((1, upo.shape[1]), F32),
        sds((1,) + dno.shape, F32), sds((1, width // 4), F32),
    )
    return pl.pallas_call(
        functools.partial(kernel_f, n_dp),
        out_shape=outs,
        grid=(steps,),
        in_specs=[rows(a.shape) for a in args[:6]] + [whole(a.shape) for a in args[6:]],
        out_specs=tuple(rows(o.shape) if i in (0, 2, 12, 14) else whole(o.shape) for i, o in enumerate(outs)),
        compiler_params=pltpu.CompilerParams(vmem_limit_bytes=VMEM_LIMIT),
    )(*args)


def local(
    block_input, norm1_gain, norm1_bias, qkv_weight, qkv_bias, proj_weight, proj_bias, norm2_gain, norm2_bias, router_weight,
    up_weight, up_bias, down_weight, down_bias, routes, lengths, cotangent,
):
    tok, width = block_input.shape
    experts = router_weight.shape[1]
    cap = 2 * tok // experts
    gath, qkv, probs, ctx, ctxf, projf, cots = stage_a(
        experts, block_input, norm1_gain, norm1_bias, qkv_weight, qkv_bias, proj_weight, routes, cotangent, lengths, cap
    )
    res, gate, prod, gres, gctx, upc, upo, dno, dnr, sm, bg, balance = stage_m(
        experts, block_input, ctxf, projf, proj_bias, norm2_gain, norm2_bias, router_weight, routes, cotangent, cots,
        up_weight, up_bias, down_weight, down_bias,
    )
    mixed, igrad, upr, comb, qb, sums, ends, bgs = stage_b(
        experts, gctx, qkv, probs, ctx, ctxf, gath, qkv_weight, block_input, norm1_gain, norm1_bias, gres, res, gate, routes, prod,
        upc, sm, bg,
    )
    outs = list(stage_f(experts, mixed, igrad, upo, upr, dno, dnr, comb, qb, sums, ends, bgs, balance))
    outs[6] = outs[6].transpose(1, 0, 2)
    outs[11] = outs[11].T
    return tuple(outs)


def solution(mesh):
    placed = (
        P(("dp", "head"), None), P(), P(), P(None, None, "head"), P(None, "head", None), P("head", None), P(), P(), P(), P(),
        P("dp", None, None), P("dp", None), P("dp", None, None), P("dp", None), P(("dp", "head"), None), P("dp", None),
        P(("dp", "head"), None),
    )
    tokens = P(("dp", "head"))
    return jax.shard_map(
        local,
        mesh=mesh,
        in_specs=placed,
        out_specs=(
            P(("dp", "head"), None), tokens, P(("dp", "head"), None), tokens, tokens, P(None, "dp", "head"), P(None, "head", "dp"),
            P("head", "dp"), tokens, tokens, tokens, P(("dp", "head"), None), P("dp", None, "head"), P("dp", "head"),
            P("dp", "head", None), P("dp", "head"),
        ),
        check_vma=False,
    )
```

```python
import functools
import jax
import jax.numpy as jnp
from jax import lax
from jax.experimental import pallas as pl
from jax.experimental.pallas import tpu as pltpu
from jax.sharding import PartitionSpec as P

EPSILON = 1e-05
BAL_COEF = 0.01
HIGHEST = lax.Precision.HIGHEST
NEG_LARGE = -1e30
MESH = pl.DeviceIdType.MESH
F32 = jnp.float32
BF16 = jnp.bfloat16
TILE = 256
VMEM_LIMIT = 61 << 20
UNROLL_A = True
UNROLL_B = True


def flip(index, bits):
    out, bit = index, 1
    while bit <= bits:
        if bits & bit:
            out = out + bit - 2 * bit * lax.rem(lax.div(index, bit), 2)
        bit *= 2
    return out


def remote(src, dst, send_sem, recv_sem, device):
    return pltpu.make_async_remote_copy(
        src_ref=src, dst_ref=dst, send_sem=send_sem, recv_sem=recv_sem, device_id=device, device_id_type=MESH
    )


def dot(left, right, dims=((1,), (0,)), precision=None):
    return lax.dot_general(left, right, (dims, ((), ())), precision=precision, preferred_element_type=F32)


def normalize(values, gain, bias):
    average = jnp.mean(values, axis=-1, keepdims=True)
    centred = values - average
    variance = jnp.mean(centred * centred, axis=-1, keepdims=True)
    inverse = lax.rsqrt(variance + EPSILON)
    scaled = centred * inverse
    return (scaled * gain + bias, scaled, inverse)


def norm_backward(grad_normed, scaled, inverse, gain):
    grad_scaled = grad_normed * gain
    first_mean = jnp.mean(grad_scaled, axis=-1, keepdims=True)
    second_mean = jnp.mean(grad_scaled * scaled, axis=-1, keepdims=True)
    return inverse * (grad_scaled - first_mean - scaled * second_mean)


def slot_layouts(routes, experts, cap):
    rows = routes.shape[1]
    count = max(8, experts)
    expert = lax.broadcasted_iota(jnp.int32, (count, rows), 0)
    hot = (routes == expert).astype(F32)
    upto = lax.broadcasted_iota(jnp.int32, (rows, rows), 0) <= lax.broadcasted_iota(jnp.int32, (rows, rows), 1)
    rank = dot(hot.astype(BF16), upto.astype(F32).astype(BF16))
    slot_row = jnp.sum((rank - 1.0) * hot, axis=0, keepdims=True)
    flat_row = jnp.sum((rank - 1.0 + cap * expert.astype(F32)) * hot, axis=0, keepdims=True)
    return hot, flat_row.astype(jnp.int32), slot_row.astype(jnp.int32)


def barrier_signal(peers):
    barrier = pltpu.get_barrier_semaphore()
    for peer in peers:
        pl.semaphore_signal(barrier, inc=1, device_id=peer, device_id_type=MESH)


def barrier_wait(count):
    pl.semaphore_wait(pltpu.get_barrier_semaphore(), count)


def kernel_a(
    n_dp, x_ref, g1_ref, b1_ref, w_ref, qb_ref, proj_ref, routes_ref, cot_ref, len_ref,
    gath_o, qkv_o, p_o, ctx_o, ctxf_o, projf_o, cots_o,
    gath, qkv, p_st, bias_s, ctx_s, out_s, disp,
    ag_s, ag_r, pj_s, pj_r, cx_s, cx_r, ct_s, ct_r, p_sem, loc,
):
    tok, width = x_ref.shape
    heads = qb_ref.shape[0]
    hd = qb_ref.shape[2]
    group = 4 * tok
    tiles = group // TILE
    reach = group // 2 // TILE + 1
    cap = cots_o.shape[0] // n_dp
    d = lax.axis_index("dp")
    h = lax.axis_index("head")
    barrier_signal([(d, flip(h, k)) for k in (1, 2, 3)] + [(flip(d, r), h) for r in range(1, n_dp)])

    def block(index):
        return pl.ds(pl.multiple_of(index * tok, tok), tok)

    gain, bias = g1_ref[...][None, :], b1_ref[...][None, :]

    def norm_rows(i, carry):
        normed, _, _ = normalize(x_ref[pl.ds(pl.multiple_of(i * 64, 64), 64), :].astype(F32), gain, bias)
        gath[pl.ds(pl.multiple_of(h * tok + i * 64, 64), 64), :] = normed.astype(BF16)
        return carry

    lax.fori_loop(0, tok // 64, norm_rows, 0)
    barrier_wait(3 + n_dp - 1)

    chunks = 4
    step = tok // chunks

    def part(index, i):
        return gath.at[pl.ds(pl.multiple_of(index * tok + i * step, step), step), :]

    sib, cross, diag = flip(h, 1), flip(h, 2), flip(h, 3)
    to_cross = [remote(part(h, i), part(h, i), ag_s.at[i], ag_r.at[i], (d, cross)) for i in range(chunks)]
    to_sib = remote(gath.at[block(h), :], gath.at[block(h), :], ag_s.at[2 * chunks], ag_r.at[2 * chunks], (d, sib))
    onward = [
        remote(part(cross, i), part(cross, i), ag_s.at[chunks + i], ag_r.at[chunks + i], (d, sib)) for i in range(chunks)
    ]
    for copy in to_cross:
        copy.start()
    to_sib.start()
    proj_copies = [
        remote(proj_ref, projf_o.at[h], pj_s.at[k], pj_r.at[k], (d, flip(h, k))) for k in (1, 2, 3)
    ]

    hot_t, flat_row, slot_row = slot_layouts(routes_ref[...], n_dp, cap)
    slot_iota = lax.broadcasted_iota(jnp.int32, (cap, tok), 0)

    def dispatch(e, carry):
        hot = (flat_row == slot_iota + e * cap).astype(F32).astype(BF16)
        disp[pl.ds(pl.multiple_of(e * cap, cap), cap), :] = dot(hot, cot_ref[...]).astype(BF16)
        return carry

    lax.fori_loop(0, n_dp, dispatch, 0)

    def slots(index):
        return pl.ds(pl.multiple_of(index * cap, cap), cap)

    cot_copies = [
        remote(disp.at[slots(flip(d, r)), :], cots_o.at[pl.ds(r * cap, cap), :], ct_s.at[r], ct_r.at[r], (flip(d, r), h))
        for r in range(1, n_dp)
    ]
    for copy in cot_copies:
        copy.start()
    cot_own = pltpu.make_async_copy(disp.at[slots(d), :], cots_o.at[pl.ds(0, cap), :], ct_s.at[0])
    cot_own.start()

    def project(index):
        def rows_of(i, carry):
            at = pl.ds(pl.multiple_of(index * tok + i * TILE, TILE), TILE)
            rows = gath[at, :]
            for c in range(3):
                out = dot(rows, w_ref[c], ((1,), (1,)))
                for a in range(heads):
                    piece = out[:, a * hd : (a + 1) * hd]
                    if c != 1:
                        piece = piece + qb_ref[a, c // 2 : c // 2 + 1, :]
                    piece = piece.astype(BF16)
                    if c == 0:
                        piece = piece * jnp.asarray(hd ** (-0.5), BF16)
                    qkv[c, a, at, :] = piece
            return carry

        lax.fori_loop(0, tok // TILE, rows_of, 0)

    project(h)
    to_sib.wait_recv()
    project(sib)
    for i in range(chunks):
        to_cross[i].wait_recv()
        onward[i].start()
    for copy in proj_copies:
        copy.start()
    proj_own = pltpu.make_async_copy(proj_ref, projf_o.at[h], loc.at[0])
    proj_own.start()
    project(cross)
    for i in range(chunks):
        onward[i].wait_recv()
    project(diag)
    gath_copy = pltpu.make_async_copy(gath, gath_o, loc.at[1])
    gath_copy.start()
    qkv_copy = pltpu.make_async_copy(qkv, qkv_o, loc.at[2])
    qkv_copy.start()

    ends = [len_ref[0, 0]]
    for i in range(1, len_ref.shape[1] - 1):
        ends.append(ends[-1] + len_ref[0, i])

    per_block = tok // TILE
    size_t = TILE * 3 // 2
    low_tiles = reach - 1

    def p_copy(t, a, size):
        return pltpu.make_async_copy(p_st.at[a, :, pl.ds(0, size)], p_o.at[a, t, :, pl.ds(0, size)], p_sem.at[a])

    def ctx_rows(t):
        return pl.ds(pl.multiple_of(lax.rem(t, per_block) * size_t, size_t), size_t)

    def ctx_send(t):
        owner = lax.div(t, per_block)
        return remote(ctx_s.at[t], ctxf_o.at[h, ctx_rows(t), :], cx_s.at[t], cx_r.at[h, lax.rem(t, per_block)], (d, owner))

    def ctx_keep(t):
        return pltpu.make_async_copy(ctx_s.at[t], ctxf_o.at[h, ctx_rows(t), :], cx_s.at[t])

    def tile_step(t, size, before, unrolled):
        first = (t + 1) * TILE - size
        rows = pl.ds(pl.multiple_of(t * TILE, TILE), TILE)
        win = pl.ds(pl.multiple_of(first, TILE), size)
        row = t * TILE + lax.broadcasted_iota(jnp.int32, (TILE, 1), 0)
        start = jnp.zeros((TILE, 1), jnp.int32)
        for end in ends:
            start = jnp.where(row >= end, end, start)
        col = first + lax.broadcasted_iota(jnp.int32, (TILE, size), 1)
        bias_s[:, :size] = jnp.where((col >= start) & (col <= row), 0.0, NEG_LARGE)

        def attend(a, carry):
            s = dot(qkv[0, a, rows, :], qkv[1, a, win, :], ((1,), (1,))) + bias_s[:, :size]
            top = jnp.max(s, axis=1, keepdims=True)
            e = jnp.exp(s - top)
            total = jnp.sum(e, axis=1, keepdims=True)
            p = (e * (1.0 / total)).astype(BF16)
            if before:
                p_copy(t, a, before).wait()
            p_st[a, :, :size] = p
            p_copy(t, a, size).start()
            out_s[a] = dot(p, qkv[2, a, win, :])
            return carry

        if unrolled:
            for a in range(heads):
                attend(a, 0)
        else:
            lax.fori_loop(0, heads, attend, 0)
        ctx_s[t] = pack([out_s[a] for a in range(heads)]).astype(BF16)

        @pl.when(h != lax.div(t, per_block))
        def _():
            ctx_send(t).start()

        @pl.when(h == lax.div(t, per_block))
        def _():
            ctx_keep(t).start()

    before = 0
    for t in range(low_tiles):
        tile_step(t, (t + 1) * TILE, before, False)
        before = (t + 1) * TILE
    span = reach * TILE
    p_st[:, :, before:] = jnp.zeros((heads, TILE, span - before), BF16)
    for a in range(heads):
        p_copy(low_tiles - 1, a, before).wait()
        p_copy(low_tiles - 1, a, span).start()

    def high_tile(t, carry):
        tile_step(t, span, span, UNROLL_A)
        return carry

    lax.fori_loop(low_tiles, tiles, high_tile, 0)
    ctx_copy = pltpu.make_async_copy(ctx_s, ctx_o, loc.at[3])
    ctx_copy.start()
    for a in range(heads):
        p_copy(tiles - 1, a, span).wait()

    def sent(t, carry):
        @pl.when(h != lax.div(t, per_block))
        def _():
            ctx_send(t).wait_send()

        @pl.when(h == lax.div(t, per_block))
        def _():
            ctx_keep(t).wait()

        return carry

    lax.fori_loop(0, tiles, sent, 0)
    for k in (1, 2, 3):
        peer = flip(h, k)
        for sub in range(per_block):
            remote(
                ctx_s.at[0], ctxf_o.at[peer, pl.ds(sub * (TILE * 3 // 2), TILE * 3 // 2), :], cx_s.at[0], cx_r.at[peer, sub], (d, peer)
            ).wait_recv()
    for copy in to_cross:
        copy.wait_send()
    to_sib.wait_send()
    for copy in onward:
        copy.wait_send()
    for k in (1, 2, 3):
        proj_copies[k - 1].wait_send()
        peer = flip(h, k)
        remote(proj_ref, projf_o.at[peer], pj_s.at[k], pj_r.at[k], (d, peer)).wait_recv()
    for copy in cot_copies:
        copy.wait()
    for copy in (cot_own, proj_own, gath_copy, qkv_copy, ctx_copy):
        copy.wait()


VM = pl.BlockSpec(memory_space=pltpu.VMEM)
SM = pl.BlockSpec(memory_space=pltpu.SMEM)
ANY = pl.BlockSpec(memory_space=pl.ANY)
DMA = pltpu.SemaphoreType.DMA


def stage_a(n_dp, x, g1, b1, w, qb, proj, routes, cot, lengths, cap):
    tok, width = x.shape
    heads, hd = qb.shape[1:]
    w, qb, routes = w.transpose(0, 2, 1), qb.transpose(1, 0, 2), routes.T
    group = 4 * tok
    tiles = group // TILE
    span = (group // 2 // TILE + 1) * TILE
    cols = heads * hd
    sds = jax.ShapeDtypeStruct
    return pl.pallas_call(
        functools.partial(kernel_a, n_dp),
        out_shape=(
            sds((group, width), BF16),
            sds((3, heads, group, hd), BF16),
            sds((heads, tiles, TILE, span), BF16),
            sds((tiles, TILE * 3 // 2, 128), BF16),
            sds((4, tok * 3 // 2, 128), BF16),
            sds((4, cols, width), BF16),
            sds((n_dp * cap, width), BF16),
        ),
        in_specs=[VM] * 8 + [SM],
        out_specs=(ANY,) * 7,
        scratch_shapes=[
            pltpu.VMEM((group, width), BF16),
            pltpu.VMEM((3, heads, group, hd), BF16),
            pltpu.VMEM((heads, TILE, span), BF16),
            pltpu.VMEM((TILE, span), F32),
            pltpu.VMEM((tiles, TILE * 3 // 2, 128), BF16),
            pltpu.VMEM((heads, TILE, hd), F32),
            pltpu.VMEM((n_dp * cap, width), BF16),
            DMA((9,)), DMA((9,)), DMA((4,)), DMA((4,)), DMA((tiles,)), DMA((4, tok // TILE)),
            DMA((n_dp,)), DMA((n_dp,)), DMA((heads,)), DMA((4,)),
        ],
        compiler_params=pltpu.CompilerParams(collective_id=0, has_side_effects=True, vmem_limit_bytes=VMEM_LIMIT),
    )(x, g1, b1, w, qb, proj, routes, cot, lengths)


def far_first(n_dp):
    half = n_dp // 2
    return list(range(half, n_dp)) + [r for r in range(2, half)] + [1]


def gelu_parts(u):
    return 0.5 * lax.erf(u * 0.7071067811865476) + 0.5, jnp.exp(u * u * -0.5) * 0.3989422804014327


def split3(value):
    high = value.astype(BF16)
    rest = value - high.astype(F32)
    middle = rest.astype(BF16)
    return high, middle, (rest - middle.astype(F32)).astype(BF16)


def fold3(stacked):
    count = stacked.shape[0] // 3
    return stacked[:count] + stacked[count : 2 * count] + stacked[2 * count :]


def differ(index, other, count):
    out, bit = 0, 1
    while bit < count:
        one, two = lax.rem(lax.div(index, bit), 2), lax.rem(lax.div(other, bit), 2)
        out = out + bit * (one + two - 2 * one * two)
        bit *= 2
    return out


def row_to_col(row):
    return jnp.broadcast_to(row, (128, row.shape[1])).T[:, :1]


def col_to_rows(col):
    return jnp.broadcast_to(col, (col.shape[0], 128)).T[:8]


def kernel_m(
    n_dp, x_ref, ctxf, projf, pb_ref, g2_ref, b2_ref, rt_ref, routes_ref, cot_ref, cots, up_h, upb_ref, down_h, downb_ref,
    res_o, gate_o, prod_o, gres_o, gctx_o, upc_h, upo_h, dno_h, dnr_o, sm_o, bg_o, bal_o,
    res, upc_o, upo_o, dno_o, stat, nhigh, nlow, low_s, gates_s, left_s, fcol, disp, gsend, rows, rowst, grecv, up, down, ghu, hid, gg, gacc, gin, ggs, ginr, ggr, dsend, dacc, drecv, urecv,
    ld, ra_s, ra_r, ga_s, ga_r, rb_s, rb_r, gb_s, gb_r, ds_s, ds_r, us_s, us_r, out_sem,
):
    tok, width = x_ref.shape
    ff = up.shape[1]
    slots = rows.shape[0]
    cap = slots // n_dp
    per = TILE // cap
    groups = slots // TILE
    experts = n_dp
    quarter = ff // 4
    size_t = TILE * 3 // 2
    hd = 64
    d = lax.axis_index("dp")
    h = lax.axis_index("head")
    sib, cross = (d, flip(h, 1)), (d, flip(h, 2))
    loads = [pltpu.make_async_copy(down_h.at[0], down, ld.at[0]), pltpu.make_async_copy(up_h.at[0], up, ld.at[1])]
    for copy in loads:
        copy.start()
    barrier_signal([(d, flip(h, k)) for k in (1, 2, 3)] + [(flip(d, r), h) for r in range(1, n_dp)])

    proj = projf[...].reshape(width, width)
    for i in range(tok // TILE):
        heads = []
        for b in range(4):
            heads += unpack(ctxf[b, i * size_t : (i + 1) * size_t, :])
        at = slice(i * TILE, (i + 1) * TILE)
        res[at, :] = x_ref[at, :].astype(F32) + dot(jnp.concatenate(heads, axis=1), proj) + pb_ref[...][None, :]
    gain, bias = g2_ref[...][None, :], b2_ref[...][None, :]
    chunk = 64

    def norm_rows(i, carry):
        at = pl.ds(pl.multiple_of(i * chunk, chunk), chunk)
        residual = res[at, :]
        average = jnp.mean(residual, axis=-1, keepdims=True)
        centred = residual - average
        inverse = lax.rsqrt(jnp.mean(centred * centred, axis=-1, keepdims=True) + EPSILON)
        stat[0, at, :] = average
        stat[1, at, :] = inverse
        normed = centred * inverse * gain + bias
        high = normed.astype(BF16)
        nhigh[at, :] = high
        nlow[at, :] = (normed - high.astype(F32)).astype(BF16)
        return carry

    lax.fori_loop(0, tok // chunk, norm_rows, 0)

    router3 = jnp.concatenate(split3(rt_ref[...]), axis=0)
    logits = fold3(dot(router3, nhigh[...], ((1,), (1,))) + dot(router3, nlow[...], ((1,), (1,))))
    raised = jnp.exp(logits - jnp.max(logits, axis=0, keepdims=True))
    prob = raised / jnp.sum(raised, axis=0, keepdims=True)
    hot, flat_row, slot_row = slot_layouts(routes_ref[...], experts, cap)
    gate_row = jnp.sum(prob * hot, axis=0, keepdims=True)
    gate_o[...] = row_to_col(gate_row)
    fraction = jnp.mean(hot, axis=1, keepdims=True)
    bal_o[...] = experts * jnp.sum(fraction * jnp.mean(prob, axis=1, keepdims=True), axis=0, keepdims=True)

    expert_row = jnp.sum(hot * lax.broadcasted_iota(jnp.int32, hot.shape, 0).astype(F32), axis=0, keepdims=True)
    other_row = jnp.bitwise_xor(expert_row.astype(jnp.int32), d)
    flat_x = other_row * cap + slot_row
    at_slot = (slot_row == lax.broadcasted_iota(jnp.int32, (128, tok), 0)).astype(F32).astype(BF16)
    other_hot = (other_row == lax.broadcasted_iota(jnp.int32, hot.shape, 0)).astype(F32)
    gates3 = jnp.concatenate([other_hot * part.astype(F32) for part in split3(gate_row)], axis=0).astype(BF16)
    gates = fold3(dot(gates3, at_slot, ((1,), (1,))))
    barrier_wait(3 + n_dp - 1)
    order = far_first(n_dp)

    def slot_block(r):
        return pl.ds(pl.multiple_of(r * cap, cap), cap)

    def send_rows(r):
        at = slot_block(r)
        return remote(disp.at[at, :], rows.at[at, :], ra_s.at[r], ra_r.at[r], (differ(d, r, n_dp), h))

    def send_gate(r):
        return remote(gsend.at[r], grecv.at[r], ga_s.at[r], ga_r.at[r], (differ(d, r, n_dp), h))

    slot_iota = lax.broadcasted_iota(jnp.int32, (cap, tok), 0)

    gates_s[...] = gates

    def fill(i, carry):
        r = lax.rem(i + n_dp // 2, n_dp)
        hits = (flat_x == slot_iota + r * cap).astype(F32).astype(BF16)
        gsend[r] = jnp.broadcast_to(gates_s[pl.ds(r, 1), :], (8, 128))
        block = dot(hits, nhigh[...]).astype(BF16)

        @pl.when(r != 0)
        def _():
            disp[slot_block(r), :] = block
            send_rows(r).start()
            send_gate(r).start()

        @pl.when(r == 0)
        def _():
            rows[:cap, :] = block
            grecv[0] = gsend[0]

        return carry

    lax.fori_loop(0, n_dp, fill, 0)

    loads[0].wait()

    def hidden_grad(i, carry):
        at = pl.ds(pl.multiple_of(lax.div(i, 4) * TILE, TILE), TILE)
        cols = pl.ds(pl.multiple_of(lax.rem(i, 4) * quarter, quarter), quarter)
        ghu[at, cols] = dot(cots[at, :], down[cols, :], ((1,), (1,))).astype(BF16)
        return carry

    lax.fori_loop(0, 4 * groups, hidden_grad, 0)
    loads[1].wait()

    step = quarter

    def send_back(r):
        at = slot_block(r)
        return remote(gin.at[at, :], ginr.at[at, :], rb_s.at[r], rb_r.at[r], (differ(d, r, n_dp), h))

    def send_gg(r):
        return remote(ggs.at[lax.div(r, per)], ggr.at[r], gb_s.at[r], gb_r.at[r], (differ(d, r, n_dp), h))

    def group_step(g, carry):
        for i in range(per):
            r = g * per + i

            @pl.when(r != 0)
            def _():
                send_rows(r).wait_recv()
                send_gate(r).wait_recv()

        at = pl.ds(pl.multiple_of(g * TILE, TILE), TILE)
        gate = jnp.concatenate([grecv[g * per + i].T[:cap, :1] for i in range(per)], axis=0)
        gacc[...] = jnp.zeros_like(gacc)
        gg[...] = jnp.zeros_like(gg)

        def expert(f, carry):
            cols = pl.ds(pl.multiple_of(f * step, step), step)
            u = dot(rows[at, :], up[:, cols]) + upb_ref[:, cols]
            share, density = gelu_parts(u)
            low = (u * share).astype(BF16)
            back = ghu[at, cols].astype(F32)
            hid[at, cols] = low
            meet = low.astype(F32) * back
            folded = meet[:, :128]
            for j in range(1, step // 128):
                folded += meet[:, j * 128 : (j + 1) * 128]
            gg[...] += folded
            pre = (gate * back * (share + u * density)).astype(BF16)
            ghu[at, cols] = pre
            gacc[...] += dot(pre, up[:, cols], ((1,), (1,)))
            return carry

        lax.fori_loop(0, ff // step, expert, 0)
        gin[at, :] = gacc[...].astype(BF16)
        cot_g = cots[at, :].astype(F32)
        gg_col = jnp.sum(gg[...], axis=1, keepdims=True) + jnp.sum(cot_g * downb_ref[...], axis=1, keepdims=True)
        ggs[g] = col_to_rows(gg_col)
        for i in range(per):
            r = g * per + i

            @pl.when(r != 0)
            def _():
                send_back(r).start()
                send_gg(r).start()

        cots[at, :] = (gate * cot_g).astype(BF16)
        rowst[:, at] = flip_t(rows[at, :])
        return carry

    lax.fori_loop(0, groups, group_step, 0)
    ginr[:cap, :] = gin[:cap, :]
    ggr[0] = ggs[0]

    third = quarter // 3

    def block_cols(index):
        return pl.ds(pl.multiple_of(index * quarter, quarter), quarter)

    def down_block(index, ref):
        def body(i, carry):
            cols = pl.ds(pl.multiple_of(index * quarter + i * third, third), third)
            ref[pl.ds(pl.multiple_of(i * third, third), third), :] = dot(hid[:, cols], cots[...], ((0,), (0,))).astype(BF16)
            return carry

        lax.fori_loop(0, 3, body, 0)

    def up_block(index, ref):
        part = width // 3

        def body(i, carry):
            at = pl.ds(pl.multiple_of(i * part, part), part)
            ref[at, :] = dot(rowst[at, :], ghu[:, block_cols(index)]).astype(BF16)
            return carry

        lax.fori_loop(0, 3, body, 0)

    def add_into(ref, other):
        def body(i, carry):
            at = pl.ds(pl.multiple_of(i * 64, 64), 64)
            ref[at, :] = (ref[at, :].astype(F32) + other[at, :].astype(F32)).astype(BF16)
            return carry

        lax.fori_loop(0, ref.shape[0] // 64, body, 0)

    down_sib = [remote(dsend.at[i], drecv.at[i], ds_s.at[i], ds_r.at[i], sib) for i in range(2)]
    down_cross = remote(dacc, dnr_o, ds_s.at[2], ds_r.at[2], cross)
    up_sib = [remote(dsend.at[i], urecv.at[i], us_s.at[i], us_r.at[i], sib) for i in range(2)]
    down_block(flip(h, 3), dsend.at[1])
    down_sib[1].start()
    down_block(flip(h, 2), dacc)
    down_sib[1].wait_recv()
    add_into(dacc, drecv.at[1])
    down_cross.start()
    down_block(flip(h, 1), dsend.at[0])
    down_sib[0].start()
    for r in order:
        send_rows(r).wait_send()

    def produce(i, carry):
        at = pl.ds(pl.multiple_of(i * TILE, TILE), TILE)
        disp[at, :] = (dot(hid[at, :], down[...]) + downb_ref[...]).astype(BF16)
        return carry

    lax.fori_loop(0, groups, produce, 0)
    prod_copy = pltpu.make_async_copy(disp, prod_o, out_sem.at[0])
    prod_copy.start()
    outs = [
        pltpu.make_async_copy(a, b, out_sem.at[1 + i])
        for i, (a, b) in enumerate(((res, res_o), (upc_o, upc_h), (upo_o, upo_h), (dno_o, dno_h)))
    ]
    outs[0].start()
    for copy in down_sib:
        copy.wait_send()
    up_block(flip(h, 3), dsend.at[1])
    up_sib[1].start()
    up_block(flip(h, 1), dsend.at[0])
    up_sib[0].start()
    up_block(flip(h, 2), upc_o)
    up_block(h, upo_o)
    down_block(h, dno_o)
    ones = jnp.ones((8, slots), BF16)
    up_bias = dot(ones, ghu[...])
    down_bias = dot(ones, cots[...])
    short = width // 4
    for b in range(4):
        bg_o[b, 0:1, :] = up_bias[:1, b * quarter : (b + 1) * quarter]
        bg_o[b, 1:2, :short] = down_bias[:1, b * short : (b + 1) * short]
    up_sib[1].wait_recv()
    add_into(upc_o, urecv.at[1])
    outs[1].start()
    up_sib[0].wait_recv()
    add_into(upo_o, urecv.at[0])
    outs[2].start()
    down_sib[0].wait_recv()
    add_into(dno_o, drecv.at[0])
    outs[3].start()

    flat_col = row_to_col(flat_x.astype(F32)).astype(jnp.int32)
    for r in order:
        send_gg(r).wait_recv()
    slot_gg = [ggr[r][:1, (r % per) * cap : (r % per) * cap + cap] for r in range(n_dp)]
    slot_gg = jnp.concatenate(slot_gg, axis=0)
    grad_gate = jnp.sum(
        fold3(dot(jnp.concatenate(split3(slot_gg), axis=0), at_slot[:cap])) * other_hot, axis=0, keepdims=True
    )
    grad_prob = hot * grad_gate + (BAL_COEF * experts / tok) * fraction
    grad_logits = prob * (grad_prob - jnp.sum(prob * grad_prob, axis=0, keepdims=True))
    high, middle, low = split3(grad_logits)
    grads3 = jnp.concatenate([high, middle, low], axis=0)
    r_high, r_middle, r_low = split3(rt_ref[...])
    inner = 6 * experts
    padded = -(-inner // 128) * 128
    left = [v.astype(F32) for v in (high, high, high, middle, middle, low)]
    left = jnp.concatenate(left + [jnp.zeros((padded - inner, tok), F32)], axis=0).T.astype(BF16)
    right = jnp.concatenate([r_high, r_middle, r_low, r_high, r_middle, r_high, jnp.zeros((padded - inner, width), BF16)], axis=0)
    sm_o[...] = jnp.zeros_like(sm_o)
    sm_o[8 : 8 + experts, :] = fold3(dot(grads3, nhigh[...]) + dot(grads3, nlow[...]))
    for r in order:
        send_back(r).wait_recv()
    left_s[...] = left
    fcol[...] = flat_col
    part = 128

    def finish(i, carry):
        gain_sum, bias_sum, res_sum = carry
        at = pl.ds(pl.multiple_of(i * part, part), part)
        pick = (fcol[at, :] == lax.broadcasted_iota(jnp.int32, (part, slots), 1)).astype(F32).astype(BF16)
        grad_normed = dot(pick, ginr[...]) + dot(left_s[at, :], right)
        inverse = stat[1, at, :]
        scaled = (res[at, :] - stat[0, at, :]) * inverse
        grad_res = cot_ref[at, :].astype(F32) + norm_backward(grad_normed, scaled, inverse, gain)
        gres_o[at, :] = grad_res
        low_s[at, :] = grad_res.astype(BF16)
        return (
            gain_sum + jnp.sum(grad_normed * scaled, axis=0, keepdims=True),
            bias_sum + jnp.sum(grad_normed, axis=0, keepdims=True),
            res_sum + jnp.sum(grad_res, axis=0, keepdims=True),
        )

    gain_sum, bias_sum, res_sum = lax.fori_loop(0, tok // part, finish, (jnp.zeros((1, width), F32),) * 3)

    def turn_back(i, carry):
        back = dot(low_s[pl.ds(pl.multiple_of(i * TILE, TILE), TILE), :], proj, ((1,), (1,)))
        for b in range(4):
            heads = [back[:, (3 * b + a) * hd : (3 * b + a + 1) * hd] for a in range(3)]
            gctx_o[b, pl.ds(pl.multiple_of(i * size_t, size_t), size_t), :] = pack(heads).astype(BF16)
        return carry

    lax.fori_loop(0, tok // TILE, turn_back, 0)
    sm_o[0:1, :] = gain_sum
    sm_o[1:2, :] = bias_sum
    sm_o[2:3, :] = res_sum
    down_cross.wait()
    for copy in up_sib:
        copy.wait_send()
    for r in order:
        send_gate(r).wait_send()
        send_back(r).wait_send()
        send_gg(r).wait_send()
    prod_copy.wait()
    for copy in outs:
        copy.wait()


def stage_m(n_dp, x, ctxf, projf, pb, g2, b2, router, routes, cot, cots, up, upb, down, downb):
    tok, width = x.shape
    slots = cots.shape[0]
    ff = up.shape[2]
    groups = slots // TILE
    quarter = ff // 4
    sds = jax.ShapeDtypeStruct
    vm = pltpu.VMEM
    return pl.pallas_call(
        functools.partial(kernel_m, n_dp),
        out_shape=(
            sds((tok, width), F32),
            sds((tok, 1), F32),
            sds((slots, width), BF16),
            sds((tok, width), F32),
            sds(ctxf.shape, BF16),
            sds((width, quarter), BF16),
            sds((width, quarter), BF16),
            sds((quarter, width), BF16),
            sds((quarter, width), BF16),
            sds((8 + n_dp, width), F32),
            sds((4, 2, quarter), F32),
            sds((1, 1), F32),
        ),
        in_specs=[VM] * 10 + [ANY, VM, ANY, VM],
        out_specs=(ANY, VM, ANY, VM, VM, ANY, ANY, ANY, ANY, VM, VM, VM),
        scratch_shapes=[
            vm((tok, width), F32), vm((width, quarter), BF16), vm((width, quarter), BF16), vm((quarter, width), BF16),
            vm((2, tok, 1), F32),
            vm((tok, width), BF16),
            vm((tok, width), BF16),
            vm((tok, width), BF16),
            vm((n_dp, 128), F32),
            vm((tok, -(-6 * n_dp // 128) * 128), BF16),
            vm((tok, 1), jnp.int32),
            vm((slots, width), BF16),
            vm((n_dp, 8, 128), F32),
            vm((slots, width), BF16),
            vm((width, slots), BF16),
            vm((n_dp, 8, 128), F32),
            vm((width, ff), BF16),
            vm((ff, width), BF16),
            vm((slots, ff), BF16),
            vm((slots, ff), BF16),
            vm((TILE, 128), F32),
            vm((TILE, width), F32),
            vm((slots, width), BF16),
            vm((groups, 8, TILE), F32),
            vm((slots, width), BF16),
            vm((n_dp, 8, TILE), F32),
            vm((2, quarter, width), BF16),
            vm((quarter, width), BF16),
            vm((2, quarter, width), BF16),
            vm((2, width, quarter), BF16),
            DMA((2,)), DMA((n_dp,)), DMA((n_dp,)), DMA((n_dp,)), DMA((n_dp,)), DMA((n_dp,)), DMA((n_dp,)),
            DMA((n_dp,)), DMA((n_dp,)), DMA((3,)), DMA((3,)), DMA((2,)), DMA((2,)), DMA((5,)),
        ],
        compiler_params=pltpu.CompilerParams(collective_id=1, has_side_effects=True, vmem_limit_bytes=VMEM_LIMIT),
    )(x, ctxf, projf, pb, g2, b2, router.T, routes.T, cot, cots, up, upb, down, downb)


def pack(outs):
    half = outs[2].shape[0] // 2
    return jnp.concatenate(
        [jnp.concatenate(outs[:2], axis=1), jnp.concatenate([outs[2][:half], outs[2][half:]], axis=1)], axis=0
    )


def unpack(tile):
    rows = tile.shape[0] * 2 // 3
    third = jnp.concatenate([tile[rows:, :64], tile[rows:, 64:]], axis=0)
    return [tile[:rows, :64], tile[:rows, 64:], third]


def unpack_t(tile):
    rows = tile.shape[1] * 2 // 3
    third = jnp.concatenate([tile[:64, rows:], tile[64:, rows:]], axis=1)
    return [tile[:64, :rows], tile[64:, :rows], third]


def flip_t(value):
    return value.astype(F32).T.astype(BF16)


def kernel_b(
    n_dp, gctx, qkv_h, p_h, ctx, ctxf, gath_h, w_h, x_h, g1_ref, b1_ref, gres, res_h, gate_ref, routes_ref, prod_h, upc_h, sm_ref, bg_ref,
    mixed_o, igrad_o, upr_o, comb_o, qb_o, sums_o, ends_o, bgs_o,
    w_ref, x_ref, res, gcr, qkv, p_v, gath, prodr, g_s, gt_s, qt_s, delta_s, dq_s, own_s, fcol, dkt, dvt, grads, gradst, gsend, gacc, grecv, comb, combx, comba, combr, ctxa, pgall, pgx, pga, pgz, pgh, pghr, low_s,
    qb, qbr, smr, smd, smt, smh, en, enr, ent, enq, bgr,
    ld, p_sem, gc_s, gc_r, pr_s, pr_r, uc_s, uc_r, gn_s, gn_r, gx_s, gx_r, qx_s, qx_r, qg_s, qg_r, px_s, px_r, pz_s, pz_r, ph_s, ph_r, qb_s, qb_r,
    sh_s, sh_r, sd_s, sd_r, eh_s, eh_r, ed_s, ed_r, bg_s, bg_r,
):
    tok, width = x_ref.shape
    heads, group, hd = qkv.shape[1:]
    cols = heads * hd
    tiles = group // TILE
    reach = group // 2 // TILE + 1
    per_block = tok // TILE
    slots = prod_h.shape[0]
    cap = slots // n_dp
    share = width // n_dp
    size_t = TILE * 3 // 2
    d = lax.axis_index("dp")
    h = lax.axis_index("head")
    sib, cross = (d, flip(h, 1)), (d, flip(h, 2))
    order = far_first(n_dp)

    def at_head(k):
        return (d, flip(h, k))

    def at_dp(r):
        return (flip(d, r), h)

    def p_load(t, size):
        return pltpu.make_async_copy(p_h.at[:, t, :, pl.ds(0, size)], p_v.at[t, :, :, pl.ds(0, size)], p_sem.at[t])

    barrier_signal([at_head(k) for k in (1, 2, 3)] + [at_dp(r) for r in range(1, n_dp)])
    load_qkv = pltpu.make_async_copy(qkv_h, qkv, ld.at[0])
    load_qkv.start()
    for t in range(tiles):
        p_load(t, min(t + 1, reach) * TILE).start()
    load_gath = pltpu.make_async_copy(gath_h, gath, ld.at[1])
    load_gath.start()
    later = [pltpu.make_async_copy(a, b, ld.at[2 + i]) for i, (a, b) in enumerate(((w_h, w_ref), (x_h, x_ref), (res_h, res)))]
    for copy in later:
        copy.start()
    low_s[...] = gres[...].T.astype(BF16)
    for j in range(per_block):
        outs = []
        for b in range(4):
            outs += unpack(ctxf[b, j * size_t : (j + 1) * size_t, :])
        ctxa[j * TILE : (j + 1) * TILE, :] = jnp.concatenate(outs, axis=1)

    def proj_rows(i, carry):
        at = pl.ds(pl.multiple_of(i * TILE, TILE), TILE)
        pgall[at, :] = dot(low_s[at, :], ctxa[...]).astype(BF16)
        return carry

    lax.fori_loop(0, width // TILE, proj_rows, 0)
    sm_all = sm_ref[...]
    for e in range(n_dp):
        smt[e] = (pltpu.roll(sm_all, width - e * share, 1) if e else sm_all)[:, :128]
    dkt[...] = jnp.zeros_like(dkt)
    dvt[...] = jnp.zeros_like(dvt)
    barrier_wait(3 + n_dp - 1)

    def send_ctx(k):
        return remote(gctx.at[flip(h, k)], gcr.at[h], gc_s.at[k], gc_r.at[k], at_head(k))

    for k in (2, 3, 1):
        send_ctx(k).start()

    def send_prod(r):
        rows = pl.ds(r * cap, cap)
        return remote(prod_h.at[rows, :], prodr.at[rows, :], pr_s.at[r], pr_r.at[r], at_dp(r))

    pairs = n_dp // 2
    side, place = lax.rem(d, 2), lax.div(d, 2)
    pair_order = list(range(pairs // 2, pairs)) + list(range(1, pairs // 2))

    def dp_rows(index):
        return pl.ds(pl.multiple_of(index * share, share), share)

    def send_px(j):
        return remote(pgall.at[dp_rows(2 * j + 1 - side), :], pgx.at[j], px_s.at[j], px_r.at[j], at_dp(1))

    def send_pz(r):
        return remote(pga.at[flip(place, r)], pgz.at[r], pz_s.at[r], pz_r.at[r], at_dp(2 * r))

    def send_ph(k):
        return remote(pgh.at[flip(h, k)], pghr.at[k], ph_s.at[k], ph_r.at[k], at_head(k))

    for j in range(pairs):
        send_px(j).start()
    for r in order:
        send_prod(r).start()
    prod_own = pltpu.make_async_copy(prod_h.at[pl.ds(0, cap), :], prodr.at[pl.ds(0, cap), :], pr_s.at[0])
    prod_own.start()
    gcr[h] = gctx[h]

    sm_head = [remote(smh, smr.at[k], sh_s.at[k], sh_r.at[k], at_head(k)) for k in (1, 2, 3)]
    bg_head = [remote(bg_ref.at[flip(h, k)], bgr.at[k], bg_s.at[k], bg_r.at[k], at_head(k)) for k in (1, 2, 3)]
    up_half = width // 2
    up_cross = [
        remote(upc_h.at[pl.ds(i * up_half, up_half), :], upr_o.at[pl.ds(i * up_half, up_half), :], uc_s.at[i], uc_r.at[i], cross)
        for i in range(2)
    ]

    for copy in bg_head:
        copy.start()

    def send_sm(r):
        return remote(smt.at[flip(d, r)], smd.at[r], sd_s.at[r], sd_r.at[r], at_dp(r))

    for r in order:
        send_sm(r).start()

    load_qkv.wait()

    def wait_block(b):
        for k in (1, 2, 3):

            @pl.when(flip(h, k) == b)
            def _():
                remote(gctx.at[0], gcr.at[b], gc_s.at[k], gc_r.at[k], at_head(k)).wait_recv()

    def attention(t, size, unrolled):
        b, sub = lax.div(t, per_block), lax.rem(t, per_block)

        @pl.when(sub == 0)
        def _():
            wait_block(b)

        p_load(t, size).wait()
        rows = pl.ds(pl.multiple_of(t * TILE, TILE), TILE)
        win = pl.ds(pl.multiple_of((t + 1) * TILE - size, TILE), size)
        grad = gcr[b, pl.ds(pl.multiple_of(sub * size_t, size_t), size_t), :]
        meets = unpack(grad.astype(F32) * ctx[t].astype(F32))
        gs, gts = unpack(grad), unpack_t(flip_t(grad))
        qts = unpack_t(flip_t(pack([qkv[0, a, rows, :] for a in range(heads)])))
        for a in range(heads):
            delta_s[a] = jnp.sum(meets[a], axis=1, keepdims=True)
            g_s[a], gt_s[a], qt_s[a] = gs[a], gts[a], qts[a]

        def head(a, carry):
            p = p_v[t, a, :, :size]
            ds = (p.astype(F32) * (dot(g_s[a], qkv[2, a, win, :], ((1,), (1,))) - delta_s[a])).astype(BF16)
            dq_s[a] = dot(ds, qkv[1, a, win, :]) * (hd ** (-0.5))
            at = pl.ds(pl.multiple_of(a * hd, hd), hd)
            dkt[at, win] += dot(qt_s[a], ds)
            dvt[at, win] += dot(gt_s[a], p)
            return carry

        if unrolled:
            for a in range(heads):
                head(a, 0)
        else:
            lax.fori_loop(0, heads, head, 0)
        dq = jnp.concatenate([dq_s[a] for a in range(heads)], axis=1)
        grads[rows, :cols] = dq.astype(BF16)
        gradst[:cols, rows] = dq.T.astype(BF16)

    half = tiles // 2

    def both_halves(i, carry):
        @pl.when(i == 1)
        def _():
            for copy in up_cross:
                copy.start()

        turn = lax.rem(i + lax.div(h, 2), 2)

        @pl.when(turn == 0)
        def _():
            for t in range(half):
                attention(t, (t + 1) * TILE, False)

        @pl.when(turn == 1)
        def _():
            def high_tile(t, inner):
                attention(t, reach * TILE, UNROLL_B)
                return inner

            lax.fori_loop(half, tiles, high_tile, 0)

        return carry

    lax.fori_loop(0, 2, both_halves, 0)

    for copy in later:
        copy.wait()

    def settle(t, carry):
        at = pl.ds(pl.multiple_of(t * TILE, TILE), TILE)
        both = jnp.concatenate([dkt[:, at], dvt[:, at]], axis=0)
        gradst[cols:, at] = both.astype(BF16)
        grads[at, cols:] = both.T.astype(BF16)
        return carry

    lax.fori_loop(0, tiles, settle, 0)

    pieces = 2
    piece = tok // pieces

    def normed_piece(index, i):
        at = pl.ds(pl.multiple_of(index * tok + i * piece, piece), piece)
        total = dot(grads[at, :cols], w_ref[0])
        for c in range(1, 3):
            total += dot(grads[at, c * cols : (c + 1) * cols], w_ref[c])
        return total

    def part(i):
        return pl.ds(pl.multiple_of(i * piece, piece), piece)

    def gn_sib(j, i):
        return remote(gsend.at[j, part(i), :], grecv.at[j, part(i), :], gn_s.at[j, i], gn_r.at[j, i], sib)

    def gn_cross(i):
        return remote(gacc.at[part(i), :], grecv.at[2, part(i), :], gx_s.at[i], gx_r.at[i], cross)

    def across(i, carry):
        gsend[1, part(i), :] = normed_piece(flip(h, 3), i).astype(BF16)
        gn_sib(1, i).start()
        mine = normed_piece(flip(h, 2), i)
        gn_sib(1, i).wait_recv()
        gacc[part(i), :] = (mine + grecv[1, part(i), :].astype(F32)).astype(BF16)
        gn_cross(i).start()
        return carry

    lax.fori_loop(0, pieces, across, 0)
    for j in range(pairs):
        send_px(j).wait_recv()
        pga[j] = (pgall[dp_rows(2 * j + side), :].astype(F32) + pgx[j].astype(F32)).astype(BF16)
    for r in pair_order:
        send_pz(r).start()

    load_gath.wait()
    for c in range(3):
        comb[:, c * cols : (c + 1) * cols] = dot(gradst[c * cols : (c + 1) * cols, :], gath[...]).T.astype(BF16)
    ones = jnp.ones((8, group), BF16)
    qb[...] = jnp.concatenate([dot(ones, grads[:, :cols])[:1], dot(ones, grads[:, 2 * cols :])[:1]], axis=1)

    def send_side(j):
        return remote(comb.at[dp_rows(2 * j + 1 - side), :], combx.at[j], qx_s.at[j], qx_r.at[j], at_dp(1))

    def send_qg(r):
        return remote(comba.at[flip(place, r)], combr.at[r], qg_s.at[r], qg_r.at[r], at_dp(2 * r))

    def send_qb(r):
        return remote(qb, qbr.at[r], qb_s.at[r], qb_r.at[r], at_dp(r))

    for j in range(pairs):
        send_side(j).start()
    for r in order:
        send_qb(r).start()
    def beside(i, carry):
        gsend[0, part(i), :] = normed_piece(flip(h, 1), i).astype(BF16)
        gn_sib(0, i).start()
        own_s[part(i), :] = normed_piece(h, i)
        return carry

    lax.fori_loop(0, pieces, beside, 0)

    for j in range(pairs):
        send_side(j).wait_recv()
        comba[j] = (comb[dp_rows(2 * j + side), :].astype(F32) + combx[j].astype(F32)).astype(BF16)
    for r in pair_order:
        send_qg(r).start()
    for r in order:
        send_sm(r).wait_recv()
    total = smt[d]
    for r in range(1, n_dp):
        total += smd[r]
    smh[...] = total
    for copy in sm_head:
        copy.start()
    hot, flat_row, slot_row = slot_layouts(routes_ref[...], n_dp, cap)
    expert_row = jnp.sum(hot * lax.broadcasted_iota(jnp.int32, hot.shape, 0).astype(F32), axis=0, keepdims=True)
    flat_x = jnp.bitwise_xor(expert_row.astype(jnp.int32), d) * cap + slot_row
    flat_col = row_to_col(flat_x.astype(F32)).astype(jnp.int32)
    for r in order:
        send_prod(r).wait_recv()
    prod_own.wait()
    fcol[...] = flat_col

    def mix(i, carry):
        at = pl.ds(pl.multiple_of(i * 128, 128), 128)
        pick = (fcol[at, :] == lax.broadcasted_iota(jnp.int32, (128, slots), 1)).astype(F32).astype(BF16)
        mixed_o[at, :] = (res[at, :] + gate_ref[at, :] * dot(pick, prodr[...])).astype(BF16)
        return carry

    lax.fori_loop(0, tok // 128, mix, 0)
    gain, bias = g1_ref[...][None, :], b1_ref[...][None, :]

    def norm_back(i, carry):
        at = pl.ds(pl.multiple_of(i * 64, 64), 64)
        own = own_s[at, :] + grecv[0, at, :].astype(F32) + grecv[2, at, :].astype(F32)
        _, scaled, inverse = normalize(x_ref[at, :].astype(F32), gain, bias)
        igrad_o[at, :] = gres[at, :] + norm_backward(own, scaled, inverse, gain)
        return (carry[0] + jnp.sum(own * scaled, axis=0, keepdims=True), carry[1] + jnp.sum(own, axis=0, keepdims=True))

    sums = (jnp.zeros((1, width), F32),) * 2
    for i in range(pieces):
        gn_sib(0, i).wait_recv()
        gn_cross(i).wait_recv()
        sums = lax.fori_loop(i * (piece // 64), (i + 1) * (piece // 64), norm_back, sums)
    gain_sum, bias_sum = sums
    en[0:1, :] = gain_sum
    en[1:2, :] = bias_sum
    en_head = [remote(en, enr.at[k], eh_s.at[k], eh_r.at[k], at_head(k)) for k in (1, 2, 3)]
    for copy in en_head:
        copy.start()
    for r in pair_order:
        send_pz(r).wait_recv()
    total = pgall[dp_rows(d), :].astype(F32) + pgx[place].astype(F32)
    for r in range(1, pairs):
        total += pgz[r].astype(F32)
    for b in range(4):
        pgh[b] = total[:, b * cols : (b + 1) * cols].astype(BF16)
    for k in (2, 3, 1):
        send_ph(k).start()
    for copy in en_head:
        copy.wait_recv()
    ent[...] = en[...] + enr[1] + enr[2] + enr[3]
    en_dp = [remote(ent, enq.at[r], ed_s.at[r], ed_r.at[r], at_dp(r)) for r in range(1, n_dp)]
    for copy in en_dp:
        copy.start()

    for r in pair_order:
        send_qg(r).wait_recv()
    for r in order:
        send_qb(r).wait_recv()
    total = comb[dp_rows(d), :].astype(F32) + combx[place].astype(F32)
    for r in range(1, pairs):
        total += combr[r].astype(F32)
    comb_o[:, : 3 * cols] = total
    total = pgh[h].astype(F32)
    for k in (1, 2, 3):
        send_ph(k).wait_recv()
        total += pghr[k].astype(F32)
    comb_o[:, 3 * cols :] = total
    sums = qb[...]
    for r in range(1, n_dp):
        sums += qbr[r]
    qb_o[...] = sums
    for copy in sm_head:
        copy.wait_recv()
    sums_o[...] = smh[...] + smr[1] + smr[2] + smr[3]
    for copy in bg_head:
        copy.wait_recv()
    bgs_o[...] = bg_ref[h] + bgr[1] + bgr[2] + bgr[3]
    for copy in en_dp:
        copy.wait_recv()
    total = ent[...]
    for r in range(1, n_dp):
        total += enq[r]
    ends_o[...] = total

    for k in (1, 2, 3):
        send_ctx(k).wait_send()
    for r in order:
        send_prod(r).wait_send()
        send_qb(r).wait_send()
        send_sm(r).wait_send()
    for r in pair_order:
        send_qg(r).wait_send()
    for j in range(pairs):
        send_side(j).wait_send()
    for copy in up_cross:
        copy.wait()
    for k in (1, 2, 3):
        send_ph(k).wait_send()
    for r in pair_order:
        send_pz(r).wait_send()
    for j in range(pairs):
        send_px(j).wait_send()
    for copy in [gn_cross(i) for i in range(pieces)] + [gn_sib(j, i) for j in range(2) for i in range(pieces)] + sm_head + bg_head + en_head + en_dp:
        copy.wait_send()


def stage_b(n_dp, gctx, qkv, probs, ctx, ctxf, gath, w, x, g1, b1, gres, res, gate, routes, prod, upc, sm, bg):
    tok, width = x.shape
    _, heads, group, hd = qkv.shape
    cols = heads * hd
    span = probs.shape[3]
    share = width // n_dp
    sds = jax.ShapeDtypeStruct
    vm = pltpu.VMEM
    return pl.pallas_call(
        functools.partial(kernel_b, n_dp),
        out_shape=(
            sds((tok, width), BF16),
            sds((tok, width), F32),
            sds(upc.shape, BF16),
            sds((share, width), F32),
            sds((1, 2 * cols), F32),
            sds((sm.shape[0], 128), F32),
            sds((2, width), F32),
            sds(bg.shape[1:], F32),
        ),
        in_specs=[VM, ANY, ANY, VM, VM, ANY, ANY, ANY, VM, VM, VM, ANY, VM, VM, ANY, ANY, VM, VM],
        out_specs=(VM, VM, ANY) + (VM,) * 5,
        scratch_shapes=[
            vm((3, cols, width), BF16), vm((tok, width), BF16), vm((tok, width), F32),
            vm(gctx.shape, BF16), vm((3, heads, group, hd), BF16), vm((group // TILE, heads, TILE, span), BF16), vm((group, width), BF16),
            vm(prod.shape, BF16),
            vm((heads, TILE, hd), BF16), vm((heads, hd, TILE), BF16), vm((heads, hd, TILE), BF16), vm((heads, TILE, 1), F32),
            vm((heads, TILE, hd), F32), vm((tok, width), F32), vm((tok, 1), jnp.int32), vm((cols, group), F32), vm((cols, group), F32), vm((group, 3 * cols), BF16), vm((3 * cols, group), BF16),
            vm((2, tok, width), BF16), vm((tok, width), BF16), vm((3, tok, width), BF16),
            vm((width, 3 * cols), BF16), vm((n_dp // 2, share, 3 * cols), BF16), vm((n_dp // 2, share, 3 * cols), BF16),
            vm((n_dp // 2, share, 3 * cols), BF16),
            vm((tok, width), BF16), vm((width, width), BF16), vm((n_dp // 2, share, width), BF16), vm((n_dp // 2, share, width), BF16),
            vm((n_dp // 2, share, width), BF16), vm((4, share, cols), BF16), vm((4, share, cols), BF16), vm((width, tok), BF16),
            vm((1, 2 * cols), F32), vm((n_dp, 1, 2 * cols), F32),
            vm((4, sm.shape[0], 128), F32), vm((n_dp, sm.shape[0], 128), F32), vm((n_dp, sm.shape[0], 128), F32),
            vm((sm.shape[0], 128), F32),
            vm((2, width), F32), vm((4, 2, width), F32), vm((2, width), F32), vm((n_dp, 2, width), F32),
            vm((4,) + bg.shape[1:], F32),
            DMA((5,)), DMA((group // TILE,)), DMA((4,)), DMA((4,)), DMA((n_dp,)), DMA((n_dp,)), DMA((2,)), DMA((2,)), DMA((2, 2)), DMA((2, 2)),
            DMA((2,)), DMA((2,)), DMA((n_dp // 2,)), DMA((n_dp // 2,)), DMA((n_dp // 2,)), DMA((n_dp // 2,)),
            DMA((n_dp // 2,)), DMA((n_dp // 2,)), DMA((n_dp // 2,)), DMA((n_dp // 2,)), DMA((4,)), DMA((4,)), DMA((n_dp,)), DMA((n_dp,)),
            DMA((4,)), DMA((4,)), DMA((n_dp,)), DMA((n_dp,)), DMA((4,)), DMA((4,)), DMA((n_dp,)), DMA((n_dp,)), DMA((4,)), DMA((4,)),
        ],
        compiler_params=pltpu.CompilerParams(collective_id=2, has_side_effects=True, vmem_limit_bytes=VMEM_LIMIT),
    )(gctx, qkv, probs, ctx, ctxf, gath, w.transpose(0, 2, 1), x, g1, b1, gres, res, gate, routes.T, prod, upc, sm, bg)


def kernel_f(
    n_dp, mixed, igrad, upo, upr, dno, dnr, comb, qb, sums, ends, bgs, bal,
    mixed_o, bal_o, igrad_o, g1_o, b1_o, qkv_o, qkvb_o, proj_o, pb_o, g2_o, b2_o, router_o, up_o, upb_o, down_o, downb_o,
):
    mixed_o[...] = mixed[...]
    igrad_o[...] = igrad[...]
    up_o[0] = upo[...].astype(F32) + upr[...].astype(F32)
    down_o[0] = dno[...].astype(F32) + dnr[...].astype(F32)

    @pl.when(pl.program_id(0) == 0)
    def _():
        d = lax.axis_index("dp")
        device = d * 4 + lax.axis_index("head")
        width = ends.shape[1]
        part = g1_o.shape[0]
        cols = qkv_o.shape[2]
        hd = cols // 3
        share = qkvb_o.shape[2]
        bal_o[...] = bal[0]
        shift = lax.rem(width - device * part, width)
        mine = pltpu.roll(sums[...], lax.rem(128 - lax.axis_index("head") * part, 128), 1)[:, :part]
        tail = pltpu.roll(jnp.concatenate([ends[...], jnp.zeros((6, width), F32)], axis=0), shift, 1)[:, :part]
        g1_o[...] = tail[0]
        b1_o[...] = tail[1]
        g2_o[...] = mine[0]
        b2_o[...] = mine[1]
        pb_o[...] = mine[2]
        router_o[...] = mine[8 : 8 + n_dp]
        for c in range(3):
            qkv_o[c] = comb[:, c * cols : (c + 1) * cols]
        proj_o[...] = comb[:, 3 * cols :].T
        turned = pltpu.roll(jnp.broadcast_to(qb[...], (8, 2 * cols)), lax.rem(2 * cols - d * share, 2 * cols), 1)
        for a in range(3):
            for c in range(2):
                at = c * cols + a * hd
                qkvb_o[a, c : c + 1, :] = turned[:1, at : at + share]
        upb_o[...] = bgs[0:1, :]
        downb_o[...] = bgs[1:2, : downb_o.shape[1]]


def stage_f(n_dp, mixed, igrad, upo, upr, dno, dnr, comb, qb, sums, ends, bgs, bal):
    tok, width = mixed.shape
    cols = qb.shape[1] // 2
    part = width // (4 * n_dp)
    share = width // n_dp
    steps = 4
    sds = jax.ShapeDtypeStruct

    def rows(shape):
        if len(shape) == 3:
            return pl.BlockSpec((1, shape[1] // steps, shape[2]), lambda i: (0, i, 0))
        return pl.BlockSpec((shape[0] // steps, shape[1]), lambda i: (i, 0))

    def whole(shape):
        return pl.BlockSpec(shape, lambda i: (0,) * len(shape))

    args = (mixed, igrad, upo, upr, dno, dnr, comb, qb, sums, ends, bgs, bal)
    outs = (
        sds((tok, width), BF16), sds((1,), F32), sds((tok, width), F32), sds((part,), F32), sds((part,), F32),
        sds((3, share, cols), F32), sds((3, 2, cols // 3 // n_dp), F32), sds((cols, share), F32), sds((part,), F32), sds((part,), F32),
        sds((part,), F32), sds((n_dp, part), F32), sds((1,) + upo.shape, F32), sds((1, upo.shape[1]), F32),
        sds((1,) + dno.shape, F32), sds((1, width // 4), F32),
    )
    return pl.pallas_call(
        functools.partial(kernel_f, n_dp),
        out_shape=outs,
        grid=(steps,),
        in_specs=[rows(a.shape) for a in args[:6]] + [whole(a.shape) for a in args[6:]],
        out_specs=tuple(rows(o.shape) if i in (0, 2, 12, 14) else whole(o.shape) for i, o in enumerate(outs)),
        compiler_params=pltpu.CompilerParams(vmem_limit_bytes=VMEM_LIMIT),
    )(*args)


def local(
    block_input, norm1_gain, norm1_bias, qkv_weight, qkv_bias, proj_weight, proj_bias, norm2_gain, norm2_bias, router_weight,
    up_weight, up_bias, down_weight, down_bias, routes, lengths, cotangent,
):
    tok, width = block_input.shape
    experts = router_weight.shape[1]
    cap = 2 * tok // experts
    gath, qkv, probs, ctx, ctxf, projf, cots = stage_a(
        experts, block_input, norm1_gain, norm1_bias, qkv_weight, qkv_bias, proj_weight, routes, cotangent, lengths, cap
    )
    res, gate, prod, gres, gctx, upc, upo, dno, dnr, sm, bg, balance = stage_m(
        experts, block_input, ctxf, projf, proj_bias, norm2_gain, norm2_bias, router_weight, routes, cotangent, cots,
        up_weight, up_bias, down_weight, down_bias,
    )
    mixed, igrad, upr, comb, qb, sums, ends, bgs = stage_b(
        experts, gctx, qkv, probs, ctx, ctxf, gath, qkv_weight, block_input, norm1_gain, norm1_bias, gres, res, gate, routes, prod,
        upc, sm, bg,
    )
    outs = list(stage_f(experts, mixed, igrad, upo, upr, dno, dnr, comb, qb, sums, ends, bgs, balance))
    outs[6] = outs[6].transpose(1, 0, 2)
    outs[11] = outs[11].T
    return tuple(outs)


def solution(mesh):
    placed = (
        P(("dp", "head"), None), P(), P(), P(None, None, "head"), P(None, "head", None), P("head", None), P(), P(), P(), P(),
        P("dp", None, None), P("dp", None), P("dp", None, None), P("dp", None), P(("dp", "head"), None), P("dp", None),
        P(("dp", "head"), None),
    )
    tokens = P(("dp", "head"))
    return jax.shard_map(
        local,
        mesh=mesh,
        in_specs=placed,
        out_specs=(
            P(("dp", "head"), None), tokens, P(("dp", "head"), None), tokens, tokens, P(None, "dp", "head"), P(None, "head", "dp"),
            P("head", "dp"), tokens, tokens, tokens, P(("dp", "head"), None), P("dp", None, "head"), P("dp", "head"),
            P("dp", "head", None), P("dp", "head"),
        ),
        check_vma=False,
    )
```

```python
import functools
import jax
import jax.numpy as jnp
from jax import lax
from jax.experimental import pallas as pl
from jax.experimental.pallas import tpu as pltpu
from jax.sharding import PartitionSpec as P

EPSILON = 1e-05
BAL_COEF = 0.01
HIGHEST = lax.Precision.HIGHEST
NEG_LARGE = -1e30
MESH = pl.DeviceIdType.MESH
F32 = jnp.float32
BF16 = jnp.bfloat16
TILE = 256
VMEM_LIMIT = 61 << 20
UNROLL_A = True
UNROLL_B = True


def flip(index, bits):
    out, bit = index, 1
    while bit <= bits:
        if bits & bit:
            out = out + bit - 2 * bit * lax.rem(lax.div(index, bit), 2)
        bit *= 2
    return out


def remote(src, dst, send_sem, recv_sem, device):
    return pltpu.make_async_remote_copy(
        src_ref=src, dst_ref=dst, send_sem=send_sem, recv_sem=recv_sem, device_id=device, device_id_type=MESH
    )


def dot(left, right, dims=((1,), (0,)), precision=None):
    return lax.dot_general(left, right, (dims, ((), ())), precision=precision, preferred_element_type=F32)


def normalize(values, gain, bias):
    average = jnp.mean(values, axis=-1, keepdims=True)
    centred = values - average
    variance = jnp.mean(centred * centred, axis=-1, keepdims=True)
    inverse = lax.rsqrt(variance + EPSILON)
    scaled = centred * inverse
    return (scaled * gain + bias, scaled, inverse)


def norm_backward(grad_normed, scaled, inverse, gain):
    grad_scaled = grad_normed * gain
    first_mean = jnp.mean(grad_scaled, axis=-1, keepdims=True)
    second_mean = jnp.mean(grad_scaled * scaled, axis=-1, keepdims=True)
    return inverse * (grad_scaled - first_mean - scaled * second_mean)


def slot_layouts(routes, experts, cap):
    rows = routes.shape[1]
    count = max(8, experts)
    expert = lax.broadcasted_iota(jnp.int32, (count, rows), 0)
    hot = (routes == expert).astype(F32)
    upto = lax.broadcasted_iota(jnp.int32, (rows, rows), 0) <= lax.broadcasted_iota(jnp.int32, (rows, rows), 1)
    rank = dot(hot.astype(BF16), upto.astype(F32).astype(BF16))
    slot_row = jnp.sum((rank - 1.0) * hot, axis=0, keepdims=True)
    flat_row = jnp.sum((rank - 1.0 + cap * expert.astype(F32)) * hot, axis=0, keepdims=True)
    return hot, flat_row.astype(jnp.int32), slot_row.astype(jnp.int32)


def barrier_signal(peers):
    barrier = pltpu.get_barrier_semaphore()
    for peer in peers:
        pl.semaphore_signal(barrier, inc=1, device_id=peer, device_id_type=MESH)


def barrier_wait(count):
    pl.semaphore_wait(pltpu.get_barrier_semaphore(), count)


def kernel_a(
    n_dp, x_ref, g1_ref, b1_ref, w_ref, qb_ref, proj_ref, routes_ref, cot_ref, len_ref,
    gath_o, qkv_o, p_o, ctx_o, ctxf_o, projf_o, cots_o,
    gath, qkv, p_st, bias_s, ctx_s, out_s, disp,
    ag_s, ag_r, pj_s, pj_r, cx_s, cx_r, ct_s, ct_r, p_sem, loc,
):
    tok, width = x_ref.shape
    heads = qb_ref.shape[0]
    hd = qb_ref.shape[2]
    group = 4 * tok
    tiles = group // TILE
    reach = group // 2 // TILE + 1
    cap = cots_o.shape[0] // n_dp
    d = lax.axis_index("dp")
    h = lax.axis_index("head")
    barrier_signal([(d, flip(h, k)) for k in (1, 2, 3)] + [(flip(d, r), h) for r in range(1, n_dp)])

    def block(index):
        return pl.ds(pl.multiple_of(index * tok, tok), tok)

    gain, bias = g1_ref[...][None, :], b1_ref[...][None, :]

    def norm_rows(i, carry):
        normed, _, _ = normalize(x_ref[pl.ds(pl.multiple_of(i * 64, 64), 64), :].astype(F32), gain, bias)
        gath[pl.ds(pl.multiple_of(h * tok + i * 64, 64), 64), :] = normed.astype(BF16)
        return carry

    lax.fori_loop(0, tok // 64, norm_rows, 0)
    barrier_wait(3 + n_dp - 1)

    chunks = 4
    step = tok // chunks

    def part(index, i):
        return gath.at[pl.ds(pl.multiple_of(index * tok + i * step, step), step), :]

    sib, cross, diag = flip(h, 1), flip(h, 2), flip(h, 3)
    to_cross = [remote(part(h, i), part(h, i), ag_s.at[i], ag_r.at[i], (d, cross)) for i in range(chunks)]
    to_sib = remote(gath.at[block(h), :], gath.at[block(h), :], ag_s.at[2 * chunks], ag_r.at[2 * chunks], (d, sib))
    onward = [
        remote(part(cross, i), part(cross, i), ag_s.at[chunks + i], ag_r.at[chunks + i], (d, sib)) for i in range(chunks)
    ]
    for copy in to_cross:
        copy.start()
    to_sib.start()
    proj_copies = [
        remote(proj_ref, projf_o.at[h], pj_s.at[k], pj_r.at[k], (d, flip(h, k))) for k in (1, 2, 3)
    ]

    hot_t, flat_row, slot_row = slot_layouts(routes_ref[...], n_dp, cap)
    slot_iota = lax.broadcasted_iota(jnp.int32, (cap, tok), 0)

    def dispatch(e, carry):
        hot = (flat_row == slot_iota + e * cap).astype(F32).astype(BF16)
        disp[pl.ds(pl.multiple_of(e * cap, cap), cap), :] = dot(hot, cot_ref[...]).astype(BF16)
        return carry

    lax.fori_loop(0, n_dp, dispatch, 0)

    def slots(index):
        return pl.ds(pl.multiple_of(index * cap, cap), cap)

    cot_copies = [
        remote(disp.at[slots(flip(d, r)), :], cots_o.at[pl.ds(r * cap, cap), :], ct_s.at[r], ct_r.at[r], (flip(d, r), h))
        for r in range(1, n_dp)
    ]
    for copy in cot_copies:
        copy.start()
    cot_own = pltpu.make_async_copy(disp.at[slots(d), :], cots_o.at[pl.ds(0, cap), :], ct_s.at[0])
    cot_own.start()

    def project(index):
        def rows_of(i, carry):
            at = pl.ds(pl.multiple_of(index * tok + i * TILE, TILE), TILE)
            rows = gath[at, :]
            for c in range(3):
                out = dot(rows, w_ref[c], ((1,), (1,)))
                for a in range(heads):
                    piece = out[:, a * hd : (a + 1) * hd]
                    if c != 1:
                        piece = piece + qb_ref[a, c // 2 : c // 2 + 1, :]
                    piece = piece.astype(BF16)
                    if c == 0:
                        piece = piece * jnp.asarray(hd ** (-0.5), BF16)
                    qkv[c, a, at, :] = piece
            return carry

        lax.fori_loop(0, tok // TILE, rows_of, 0)

    project(h)
    to_sib.wait_recv()
    project(sib)
    for i in range(chunks):
        to_cross[i].wait_recv()
        onward[i].start()
    for copy in proj_copies:
        copy.start()
    proj_own = pltpu.make_async_copy(proj_ref, projf_o.at[h], loc.at[0])
    proj_own.start()
    project(cross)
    for i in range(chunks):
        onward[i].wait_recv()
    project(diag)
    gath_copy = pltpu.make_async_copy(gath, gath_o, loc.at[1])
    gath_copy.start()
    qkv_copy = pltpu.make_async_copy(qkv, qkv_o, loc.at[2])
    qkv_copy.start()

    ends = [len_ref[0, 0]]
    for i in range(1, len_ref.shape[1] - 1):
        ends.append(ends[-1] + len_ref[0, i])

    per_block = tok // TILE
    size_t = TILE * 3 // 2
    low_tiles = reach - 1

    def p_copy(t, a, size):
        return pltpu.make_async_copy(p_st.at[a, :, pl.ds(0, size)], p_o.at[a, t, :, pl.ds(0, size)], p_sem.at[a])

    def ctx_rows(t):
        return pl.ds(pl.multiple_of(lax.rem(t, per_block) * size_t, size_t), size_t)

    def ctx_send(t):
        owner = lax.div(t, per_block)
        return remote(ctx_s.at[t], ctxf_o.at[h, ctx_rows(t), :], cx_s.at[t], cx_r.at[h, lax.rem(t, per_block)], (d, owner))

    def ctx_keep(t):
        return pltpu.make_async_copy(ctx_s.at[t], ctxf_o.at[h, ctx_rows(t), :], cx_s.at[t])

    def tile_step(t, size, before, unrolled):
        first = (t + 1) * TILE - size
        rows = pl.ds(pl.multiple_of(t * TILE, TILE), TILE)
        win = pl.ds(pl.multiple_of(first, TILE), size)
        row = t * TILE + lax.broadcasted_iota(jnp.int32, (TILE, 1), 0)
        start = jnp.zeros((TILE, 1), jnp.int32)
        for end in ends:
            start = jnp.where(row >= end, end, start)
        col = first + lax.broadcasted_iota(jnp.int32, (TILE, size), 1)
        bias_s[:, :size] = jnp.where((col >= start) & (col <= row), 0.0, NEG_LARGE)

        def attend(a, carry):
            s = dot(qkv[0, a, rows, :], qkv[1, a, win, :], ((1,), (1,))) + bias_s[:, :size]
            top = jnp.max(s, axis=1, keepdims=True)
            e = jnp.exp(s - top)
            total = jnp.sum(e, axis=1, keepdims=True)
            p = (e * (1.0 / total)).astype(BF16)
            if before:
                p_copy(t, a, before).wait()
            p_st[a, :, :size] = p
            p_copy(t, a, size).start()
            out_s[a] = dot(p, qkv[2, a, win, :])
            return carry

        if unrolled:
            for a in range(heads):
                attend(a, 0)
        else:
            lax.fori_loop(0, heads, attend, 0)
        ctx_s[t] = pack([out_s[a] for a in range(heads)]).astype(BF16)

        @pl.when(h != lax.div(t, per_block))
        def _():
            ctx_send(t).start()

        @pl.when(h == lax.div(t, per_block))
        def _():
            ctx_keep(t).start()

    before = 0
    for t in range(low_tiles):
        tile_step(t, (t + 1) * TILE, before, t >= 3)
        before = (t + 1) * TILE
    span = reach * TILE
    p_st[:, :, before:] = jnp.zeros((heads, TILE, span - before), BF16)
    for a in range(heads):
        p_copy(low_tiles - 1, a, before).wait()
        p_copy(low_tiles - 1, a, span).start()

    def high_tile(t, carry):
        tile_step(t, span, span, UNROLL_A)
        return carry

    lax.fori_loop(low_tiles, tiles, high_tile, 0)
    ctx_copy = pltpu.make_async_copy(ctx_s, ctx_o, loc.at[3])
    ctx_copy.start()
    for a in range(heads):
        p_copy(tiles - 1, a, span).wait()

    def sent(t, carry):
        @pl.when(h != lax.div(t, per_block))
        def _():
            ctx_send(t).wait_send()

        @pl.when(h == lax.div(t, per_block))
        def _():
            ctx_keep(t).wait()

        return carry

    lax.fori_loop(0, tiles, sent, 0)
    for k in (1, 2, 3):
        peer = flip(h, k)
        for sub in range(per_block):
            remote(
                ctx_s.at[0], ctxf_o.at[peer, pl.ds(sub * (TILE * 3 // 2), TILE * 3 // 2), :], cx_s.at[0], cx_r.at[peer, sub], (d, peer)
            ).wait_recv()
    for copy in to_cross:
        copy.wait_send()
    to_sib.wait_send()
    for copy in onward:
        copy.wait_send()
    for k in (1, 2, 3):
        proj_copies[k - 1].wait_send()
        peer = flip(h, k)
        remote(proj_ref, projf_o.at[peer], pj_s.at[k], pj_r.at[k], (d, peer)).wait_recv()
    for copy in cot_copies:
        copy.wait()
    for copy in (cot_own, proj_own, gath_copy, qkv_copy, ctx_copy):
        copy.wait()


VM = pl.BlockSpec(memory_space=pltpu.VMEM)
SM = pl.BlockSpec(memory_space=pltpu.SMEM)
ANY = pl.BlockSpec(memory_space=pl.ANY)
DMA = pltpu.SemaphoreType.DMA


def stage_a(n_dp, x, g1, b1, w, qb, proj, routes, cot, lengths, cap):
    tok, width = x.shape
    heads, hd = qb.shape[1:]
    w, qb, routes = w.transpose(0, 2, 1), qb.transpose(1, 0, 2), routes.T
    group = 4 * tok
    tiles = group // TILE
    span = (group // 2 // TILE + 1) * TILE
    cols = heads * hd
    sds = jax.ShapeDtypeStruct
    return pl.pallas_call(
        functools.partial(kernel_a, n_dp),
        out_shape=(
            sds((group, width), BF16),
            sds((3, heads, group, hd), BF16),
            sds((heads, tiles, TILE, span), BF16),
            sds((tiles, TILE * 3 // 2, 128), BF16),
            sds((4, tok * 3 // 2, 128), BF16),
            sds((4, cols, width), BF16),
            sds((n_dp * cap, width), BF16),
        ),
        in_specs=[VM] * 8 + [SM],
        out_specs=(ANY,) * 7,
        scratch_shapes=[
            pltpu.VMEM((group, width), BF16),
            pltpu.VMEM((3, heads, group, hd), BF16),
            pltpu.VMEM((heads, TILE, span), BF16),
            pltpu.VMEM((TILE, span), F32),
            pltpu.VMEM((tiles, TILE * 3 // 2, 128), BF16),
            pltpu.VMEM((heads, TILE, hd), F32),
            pltpu.VMEM((n_dp * cap, width), BF16),
            DMA((9,)), DMA((9,)), DMA((4,)), DMA((4,)), DMA((tiles,)), DMA((4, tok // TILE)),
            DMA((n_dp,)), DMA((n_dp,)), DMA((heads,)), DMA((4,)),
        ],
        compiler_params=pltpu.CompilerParams(collective_id=0, has_side_effects=True, vmem_limit_bytes=VMEM_LIMIT),
    )(x, g1, b1, w, qb, proj, routes, cot, lengths)


def far_first(n_dp):
    half = n_dp // 2
    return list(range(half, n_dp)) + [r for r in range(2, half)] + [1]


def gelu_parts(u):
    return 0.5 * lax.erf(u * 0.7071067811865476) + 0.5, jnp.exp(u * u * -0.5) * 0.3989422804014327


def split3(value):
    high = value.astype(BF16)
    rest = value - high.astype(F32)
    middle = rest.astype(BF16)
    return high, middle, (rest - middle.astype(F32)).astype(BF16)


def fold3(stacked):
    count = stacked.shape[0] // 3
    return stacked[:count] + stacked[count : 2 * count] + stacked[2 * count :]


def differ(index, other, count):
    out, bit = 0, 1
    while bit < count:
        one, two = lax.rem(lax.div(index, bit), 2), lax.rem(lax.div(other, bit), 2)
        out = out + bit * (one + two - 2 * one * two)
        bit *= 2
    return out


def row_to_col(row):
    return jnp.broadcast_to(row, (128, row.shape[1])).T[:, :1]


def col_to_rows(col):
    return jnp.broadcast_to(col, (col.shape[0], 128)).T[:8]


def kernel_m(
    n_dp, x_ref, ctxf, projf, pb_ref, g2_ref, b2_ref, rt_ref, routes_ref, cot_ref, cots, up_h, upb_ref, down_h, downb_ref,
    res_o, gate_o, prod_o, gres_o, gctx_o, upc_h, upo_h, dno_h, dnr_o, sm_o, bg_o, bal_o,
    res, upc_o, upo_o, dno_o, stat, nhigh, nlow, low_s, gates_s, left_s, fcol, disp, gsend, rows, rowst, grecv, up, down, ghu, hid, gg, gacc, gin, ggs, ginr, ggr, dsend, dacc, drecv, urecv,
    ld, ra_s, ra_r, ga_s, ga_r, rb_s, rb_r, gb_s, gb_r, ds_s, ds_r, us_s, us_r, out_sem,
):
    tok, width = x_ref.shape
    ff = up.shape[1]
    slots = rows.shape[0]
    cap = slots // n_dp
    per = TILE // cap
    groups = slots // TILE
    experts = n_dp
    quarter = ff // 4
    size_t = TILE * 3 // 2
    hd = 64
    d = lax.axis_index("dp")
    h = lax.axis_index("head")
    sib, cross = (d, flip(h, 1)), (d, flip(h, 2))
    loads = [pltpu.make_async_copy(down_h.at[0], down, ld.at[0]), pltpu.make_async_copy(up_h.at[0], up, ld.at[1])]
    for copy in loads:
        copy.start()
    barrier_signal([(d, flip(h, k)) for k in (1, 2, 3)] + [(flip(d, r), h) for r in range(1, n_dp)])

    proj = projf[...].reshape(width, width)
    for i in range(tok // TILE):
        heads = []
        for b in range(4):
            heads += unpack(ctxf[b, i * size_t : (i + 1) * size_t, :])
        at = slice(i * TILE, (i + 1) * TILE)
        res[at, :] = x_ref[at, :].astype(F32) + dot(jnp.concatenate(heads, axis=1), proj) + pb_ref[...][None, :]
    gain, bias = g2_ref[...][None, :], b2_ref[...][None, :]
    chunk = 64

    def norm_rows(i, carry):
        at = pl.ds(pl.multiple_of(i * chunk, chunk), chunk)
        residual = res[at, :]
        average = jnp.mean(residual, axis=-1, keepdims=True)
        centred = residual - average
        inverse = lax.rsqrt(jnp.mean(centred * centred, axis=-1, keepdims=True) + EPSILON)
        stat[0, at, :] = average
        stat[1, at, :] = inverse
        normed = centred * inverse * gain + bias
        high = normed.astype(BF16)
        nhigh[at, :] = high
        nlow[at, :] = (normed - high.astype(F32)).astype(BF16)
        return carry

    lax.fori_loop(0, tok // chunk, norm_rows, 0)

    router3 = jnp.concatenate(split3(rt_ref[...]), axis=0)
    logits = fold3(dot(router3, nhigh[...], ((1,), (1,))) + dot(router3, nlow[...], ((1,), (1,))))
    raised = jnp.exp(logits - jnp.max(logits, axis=0, keepdims=True))
    prob = raised / jnp.sum(raised, axis=0, keepdims=True)
    hot, flat_row, slot_row = slot_layouts(routes_ref[...], experts, cap)
    gate_row = jnp.sum(prob * hot, axis=0, keepdims=True)
    gate_o[...] = row_to_col(gate_row)
    fraction = jnp.mean(hot, axis=1, keepdims=True)
    bal_o[...] = experts * jnp.sum(fraction * jnp.mean(prob, axis=1, keepdims=True), axis=0, keepdims=True)

    expert_row = jnp.sum(hot * lax.broadcasted_iota(jnp.int32, hot.shape, 0).astype(F32), axis=0, keepdims=True)
    other_row = jnp.bitwise_xor(expert_row.astype(jnp.int32), d)
    flat_x = other_row * cap + slot_row
    at_slot = (slot_row == lax.broadcasted_iota(jnp.int32, (128, tok), 0)).astype(F32).astype(BF16)
    other_hot = (other_row == lax.broadcasted_iota(jnp.int32, hot.shape, 0)).astype(F32)
    gates3 = jnp.concatenate([other_hot * part.astype(F32) for part in split3(gate_row)], axis=0).astype(BF16)
    gates = fold3(dot(gates3, at_slot, ((1,), (1,))))
    barrier_wait(3 + n_dp - 1)
    order = far_first(n_dp)

    def slot_block(r):
        return pl.ds(pl.multiple_of(r * cap, cap), cap)

    def send_rows(r):
        at = slot_block(r)
        return remote(disp.at[at, :], rows.at[at, :], ra_s.at[r], ra_r.at[r], (differ(d, r, n_dp), h))

    def send_gate(r):
        return remote(gsend.at[r], grecv.at[r], ga_s.at[r], ga_r.at[r], (differ(d, r, n_dp), h))

    slot_iota = lax.broadcasted_iota(jnp.int32, (cap, tok), 0)

    gates_s[...] = gates

    def fill(i, carry):
        r = lax.rem(i + n_dp // 2, n_dp)
        hits = (flat_x == slot_iota + r * cap).astype(F32).astype(BF16)
        gsend[r] = jnp.broadcast_to(gates_s[pl.ds(r, 1), :], (8, 128))
        block = dot(hits, nhigh[...]).astype(BF16)

        @pl.when(r != 0)
        def _():
            disp[slot_block(r), :] = block
            send_rows(r).start()
            send_gate(r).start()

        @pl.when(r == 0)
        def _():
            rows[:cap, :] = block
            grecv[0] = gsend[0]

        return carry

    lax.fori_loop(0, n_dp, fill, 0)

    loads[0].wait()

    def hidden_grad(i, carry):
        at = pl.ds(pl.multiple_of(lax.div(i, 4) * TILE, TILE), TILE)
        cols = pl.ds(pl.multiple_of(lax.rem(i, 4) * quarter, quarter), quarter)
        ghu[at, cols] = dot(cots[at, :], down[cols, :], ((1,), (1,))).astype(BF16)
        return carry

    lax.fori_loop(0, 4 * groups, hidden_grad, 0)
    loads[1].wait()

    step = quarter

    def send_back(r):
        at = slot_block(r)
        return remote(gin.at[at, :], ginr.at[at, :], rb_s.at[r], rb_r.at[r], (differ(d, r, n_dp), h))

    def send_gg(r):
        return remote(ggs.at[lax.div(r, per)], ggr.at[r], gb_s.at[r], gb_r.at[r], (differ(d, r, n_dp), h))

    def group_step(g, carry):
        for i in range(per):
            r = g * per + i

            @pl.when(r != 0)
            def _():
                send_rows(r).wait_recv()
                send_gate(r).wait_recv()

        at = pl.ds(pl.multiple_of(g * TILE, TILE), TILE)
        gate = jnp.concatenate([grecv[g * per + i].T[:cap, :1] for i in range(per)], axis=0)
        gacc[...] = jnp.zeros_like(gacc)
        gg[...] = jnp.zeros_like(gg)

        def expert(f, carry):
            cols = pl.ds(pl.multiple_of(f * step, step), step)
            u = dot(rows[at, :], up[:, cols]) + upb_ref[:, cols]
            share, density = gelu_parts(u)
            low = (u * share).astype(BF16)
            back = ghu[at, cols].astype(F32)
            hid[at, cols] = low
            meet = low.astype(F32) * back
            folded = meet[:, :128]
            for j in range(1, step // 128):
                folded += meet[:, j * 128 : (j + 1) * 128]
            gg[...] += folded
            pre = (gate * back * (share + u * density)).astype(BF16)
            ghu[at, cols] = pre
            gacc[...] += dot(pre, up[:, cols], ((1,), (1,)))
            return carry

        lax.fori_loop(0, ff // step, expert, 0)
        gin[at, :] = gacc[...].astype(BF16)
        cot_g = cots[at, :].astype(F32)
        gg_col = jnp.sum(gg[...], axis=1, keepdims=True) + jnp.sum(cot_g * downb_ref[...], axis=1, keepdims=True)
        ggs[g] = col_to_rows(gg_col)
        for i in range(per):
            r = g * per + i

            @pl.when(r != 0)
            def _():
                send_back(r).start()
                send_gg(r).start()

        cots[at, :] = (gate * cot_g).astype(BF16)
        rowst[:, at] = flip_t(rows[at, :])
        return carry

    lax.fori_loop(0, groups, group_step, 0)
    ginr[:cap, :] = gin[:cap, :]
    ggr[0] = ggs[0]

    third = quarter // 3

    def block_cols(index):
        return pl.ds(pl.multiple_of(index * quarter, quarter), quarter)

    def down_block(index, ref):
        def body(i, carry):
            cols = pl.ds(pl.multiple_of(index * quarter + i * third, third), third)
            ref[pl.ds(pl.multiple_of(i * third, third), third), :] = dot(hid[:, cols], cots[...], ((0,), (0,))).astype(BF16)
            return carry

        lax.fori_loop(0, 3, body, 0)

    def up_block(index, ref):
        part = width // 3

        def body(i, carry):
            at = pl.ds(pl.multiple_of(i * part, part), part)
            ref[at, :] = dot(rowst[at, :], ghu[:, block_cols(index)]).astype(BF16)
            return carry

        lax.fori_loop(0, 3, body, 0)

    def add_into(ref, other):
        def body(i, carry):
            at = pl.ds(pl.multiple_of(i * 64, 64), 64)
            ref[at, :] = (ref[at, :].astype(F32) + other[at, :].astype(F32)).astype(BF16)
            return carry

        lax.fori_loop(0, ref.shape[0] // 64, body, 0)

    down_sib = [remote(dsend.at[i], drecv.at[i], ds_s.at[i], ds_r.at[i], sib) for i in range(2)]
    down_cross = remote(dacc, dnr_o, ds_s.at[2], ds_r.at[2], cross)
    up_sib = [remote(dsend.at[i], urecv.at[i], us_s.at[i], us_r.at[i], sib) for i in range(2)]
    down_block(flip(h, 3), dsend.at[1])
    down_sib[1].start()
    down_block(flip(h, 2), dacc)
    down_sib[1].wait_recv()
    add_into(dacc, drecv.at[1])
    down_cross.start()
    down_block(flip(h, 1), dsend.at[0])
    down_sib[0].start()
    for r in order:
        send_rows(r).wait_send()

    def produce(i, carry):
        at = pl.ds(pl.multiple_of(i * TILE, TILE), TILE)
        disp[at, :] = (dot(hid[at, :], down[...]) + downb_ref[...]).astype(BF16)
        return carry

    lax.fori_loop(0, groups, produce, 0)
    prod_copy = pltpu.make_async_copy(disp, prod_o, out_sem.at[0])
    prod_copy.start()
    outs = [
        pltpu.make_async_copy(a, b, out_sem.at[1 + i])
        for i, (a, b) in enumerate(((res, res_o), (upc_o, upc_h), (upo_o, upo_h), (dno_o, dno_h)))
    ]
    outs[0].start()
    for copy in down_sib:
        copy.wait_send()
    up_block(flip(h, 3), dsend.at[1])
    up_sib[1].start()
    up_block(flip(h, 1), dsend.at[0])
    up_sib[0].start()
    up_block(flip(h, 2), upc_o)
    up_block(h, upo_o)
    down_block(h, dno_o)
    ones = jnp.ones((8, slots), BF16)
    up_bias = dot(ones, ghu[...])
    down_bias = dot(ones, cots[...])
    short = width // 4
    for b in range(4):
        bg_o[b, 0:1, :] = up_bias[:1, b * quarter : (b + 1) * quarter]
        bg_o[b, 1:2, :short] = down_bias[:1, b * short : (b + 1) * short]
    up_sib[1].wait_recv()
    add_into(upc_o, urecv.at[1])
    outs[1].start()
    up_sib[0].wait_recv()
    add_into(upo_o, urecv.at[0])
    outs[2].start()
    down_sib[0].wait_recv()
    add_into(dno_o, drecv.at[0])
    outs[3].start()

    flat_col = row_to_col(flat_x.astype(F32)).astype(jnp.int32)
    for r in order:
        send_gg(r).wait_recv()
    slot_gg = [ggr[r][:1, (r % per) * cap : (r % per) * cap + cap] for r in range(n_dp)]
    slot_gg = jnp.concatenate(slot_gg, axis=0)
    grad_gate = jnp.sum(
        fold3(dot(jnp.concatenate(split3(slot_gg), axis=0), at_slot[:cap])) * other_hot, axis=0, keepdims=True
    )
    grad_prob = hot * grad_gate + (BAL_COEF * experts / tok) * fraction
    grad_logits = prob * (grad_prob - jnp.sum(prob * grad_prob, axis=0, keepdims=True))
    high, middle, low = split3(grad_logits)
    grads3 = jnp.concatenate([high, middle, low], axis=0)
    r_high, r_middle, r_low = split3(rt_ref[...])
    inner = 6 * experts
    padded = -(-inner // 128) * 128
    left = [v.astype(F32) for v in (high, high, high, middle, middle, low)]
    left = jnp.concatenate(left + [jnp.zeros((padded - inner, tok), F32)], axis=0).T.astype(BF16)
    right = jnp.concatenate([r_high, r_middle, r_low, r_high, r_middle, r_high, jnp.zeros((padded - inner, width), BF16)], axis=0)
    sm_o[...] = jnp.zeros_like(sm_o)
    sm_o[8 : 8 + experts, :] = fold3(dot(grads3, nhigh[...]) + dot(grads3, nlow[...]))
    for r in order:
        send_back(r).wait_recv()
    left_s[...] = left
    fcol[...] = flat_col
    part = 128

    def finish(i, carry):
        gain_sum, bias_sum, res_sum = carry
        at = pl.ds(pl.multiple_of(i * part, part), part)
        pick = (fcol[at, :] == lax.broadcasted_iota(jnp.int32, (part, slots), 1)).astype(F32).astype(BF16)
        grad_normed = dot(pick, ginr[...]) + dot(left_s[at, :], right)
        inverse = stat[1, at, :]
        scaled = (res[at, :] - stat[0, at, :]) * inverse
        grad_res = cot_ref[at, :].astype(F32) + norm_backward(grad_normed, scaled, inverse, gain)
        gres_o[at, :] = grad_res
        low_s[at, :] = grad_res.astype(BF16)
        return (
            gain_sum + jnp.sum(grad_normed * scaled, axis=0, keepdims=True),
            bias_sum + jnp.sum(grad_normed, axis=0, keepdims=True),
            res_sum + jnp.sum(grad_res, axis=0, keepdims=True),
        )

    gain_sum, bias_sum, res_sum = lax.fori_loop(0, tok // part, finish, (jnp.zeros((1, width), F32),) * 3)

    def turn_back(i, carry):
        back = dot(low_s[pl.ds(pl.multiple_of(i * TILE, TILE), TILE), :], proj, ((1,), (1,)))
        for b in range(4):
            heads = [back[:, (3 * b + a) * hd : (3 * b + a + 1) * hd] for a in range(3)]
            gctx_o[b, pl.ds(pl.multiple_of(i * size_t, size_t), size_t), :] = pack(heads).astype(BF16)
        return carry

    lax.fori_loop(0, tok // TILE, turn_back, 0)
    sm_o[0:1, :] = gain_sum
    sm_o[1:2, :] = bias_sum
    sm_o[2:3, :] = res_sum
    down_cross.wait()
    for copy in up_sib:
        copy.wait_send()
    for r in order:
        send_gate(r).wait_send()
        send_back(r).wait_send()
        send_gg(r).wait_send()
    prod_copy.wait()
    for copy in outs:
        copy.wait()


def stage_m(n_dp, x, ctxf, projf, pb, g2, b2, router, routes, cot, cots, up, upb, down, downb):
    tok, width = x.shape
    slots = cots.shape[0]
    ff = up.shape[2]
    groups = slots // TILE
    quarter = ff // 4
    sds = jax.ShapeDtypeStruct
    vm = pltpu.VMEM
    return pl.pallas_call(
        functools.partial(kernel_m, n_dp),
        out_shape=(
            sds((tok, width), F32),
            sds((tok, 1), F32),
            sds((slots, width), BF16),
            sds((tok, width), F32),
            sds(ctxf.shape, BF16),
            sds((width, quarter), BF16),
            sds((width, quarter), BF16),
            sds((quarter, width), BF16),
            sds((quarter, width), BF16),
            sds((8 + n_dp, width), F32),
            sds((4, 2, quarter), F32),
            sds((1, 1), F32),
        ),
        in_specs=[VM] * 10 + [ANY, VM, ANY, VM],
        out_specs=(ANY, VM, ANY, VM, VM, ANY, ANY, ANY, ANY, VM, VM, VM),
        scratch_shapes=[
            vm((tok, width), F32), vm((width, quarter), BF16), vm((width, quarter), BF16), vm((quarter, width), BF16),
            vm((2, tok, 1), F32),
            vm((tok, width), BF16),
            vm((tok, width), BF16),
            vm((tok, width), BF16),
            vm((n_dp, 128), F32),
            vm((tok, -(-6 * n_dp // 128) * 128), BF16),
            vm((tok, 1), jnp.int32),
            vm((slots, width), BF16),
            vm((n_dp, 8, 128), F32),
            vm((slots, width), BF16),
            vm((width, slots), BF16),
            vm((n_dp, 8, 128), F32),
            vm((width, ff), BF16),
            vm((ff, width), BF16),
            vm((slots, ff), BF16),
            vm((slots, ff), BF16),
            vm((TILE, 128), F32),
            vm((TILE, width), F32),
            vm((slots, width), BF16),
            vm((groups, 8, TILE), F32),
            vm((slots, width), BF16),
            vm((n_dp, 8, TILE), F32),
            vm((2, quarter, width), BF16),
            vm((quarter, width), BF16),
            vm((2, quarter, width), BF16),
            vm((2, width, quarter), BF16),
            DMA((2,)), DMA((n_dp,)), DMA((n_dp,)), DMA((n_dp,)), DMA((n_dp,)), DMA((n_dp,)), DMA((n_dp,)),
            DMA((n_dp,)), DMA((n_dp,)), DMA((3,)), DMA((3,)), DMA((2,)), DMA((2,)), DMA((5,)),
        ],
        compiler_params=pltpu.CompilerParams(collective_id=1, has_side_effects=True, vmem_limit_bytes=VMEM_LIMIT),
    )(x, ctxf, projf, pb, g2, b2, router.T, routes.T, cot, cots, up, upb, down, downb)


def pack(outs):
    half = outs[2].shape[0] // 2
    return jnp.concatenate(
        [jnp.concatenate(outs[:2], axis=1), jnp.concatenate([outs[2][:half], outs[2][half:]], axis=1)], axis=0
    )


def unpack(tile):
    rows = tile.shape[0] * 2 // 3
    third = jnp.concatenate([tile[rows:, :64], tile[rows:, 64:]], axis=0)
    return [tile[:rows, :64], tile[:rows, 64:], third]


def unpack_t(tile):
    rows = tile.shape[1] * 2 // 3
    third = jnp.concatenate([tile[:64, rows:], tile[64:, rows:]], axis=1)
    return [tile[:64, :rows], tile[64:, :rows], third]


def flip_t(value):
    return value.astype(F32).T.astype(BF16)


def kernel_b(
    n_dp, gctx, qkv_h, p_h, ctx, ctxf, gath_h, w_h, x_h, g1_ref, b1_ref, gres, res_h, gate_ref, routes_ref, prod_h, upc_h, sm_ref, bg_ref,
    mixed_o, igrad_o, upr_o, comb_o, qb_o, sums_o, ends_o, bgs_o,
    w_ref, x_ref, res, gcr, qkv, p_v, gath, prodr, g_s, gt_s, qt_s, delta_s, dq_s, own_s, fcol, dkt, dvt, grads, gradst, gsend, gacc, grecv, comb, combx, comba, combr, ctxa, pgall, pgx, pga, pgz, pgh, pghr, low_s,
    qb, qbr, smr, smd, smt, smh, en, enr, ent, enq, bgr,
    ld, p_sem, gc_s, gc_r, pr_s, pr_r, uc_s, uc_r, gn_s, gn_r, gx_s, gx_r, qx_s, qx_r, qg_s, qg_r, px_s, px_r, pz_s, pz_r, ph_s, ph_r, qb_s, qb_r,
    sh_s, sh_r, sd_s, sd_r, eh_s, eh_r, ed_s, ed_r, bg_s, bg_r,
):
    tok, width = x_ref.shape
    heads, group, hd = qkv.shape[1:]
    cols = heads * hd
    tiles = group // TILE
    reach = group // 2 // TILE + 1
    per_block = tok // TILE
    slots = prod_h.shape[0]
    cap = slots // n_dp
    share = width // n_dp
    size_t = TILE * 3 // 2
    d = lax.axis_index("dp")
    h = lax.axis_index("head")
    sib, cross = (d, flip(h, 1)), (d, flip(h, 2))
    order = far_first(n_dp)

    def at_head(k):
        return (d, flip(h, k))

    def at_dp(r):
        return (flip(d, r), h)

    def p_load(t, size):
        return pltpu.make_async_copy(p_h.at[:, t, :, pl.ds(0, size)], p_v.at[t, :, :, pl.ds(0, size)], p_sem.at[t])

    barrier_signal([at_head(k) for k in (1, 2, 3)] + [at_dp(r) for r in range(1, n_dp)])
    load_qkv = pltpu.make_async_copy(qkv_h, qkv, ld.at[0])
    load_qkv.start()
    for t in range(tiles):
        p_load(t, min(t + 1, reach) * TILE).start()
    load_gath = pltpu.make_async_copy(gath_h, gath, ld.at[1])
    load_gath.start()
    later = [pltpu.make_async_copy(a, b, ld.at[2 + i]) for i, (a, b) in enumerate(((w_h, w_ref), (x_h, x_ref), (res_h, res)))]
    for copy in later:
        copy.start()
    low_s[...] = gres[...].T.astype(BF16)
    for j in range(per_block):
        outs = []
        for b in range(4):
            outs += unpack(ctxf[b, j * size_t : (j + 1) * size_t, :])
        ctxa[j * TILE : (j + 1) * TILE, :] = jnp.concatenate(outs, axis=1)

    def proj_rows(i, carry):
        at = pl.ds(pl.multiple_of(i * TILE, TILE), TILE)
        pgall[at, :] = dot(low_s[at, :], ctxa[...]).astype(BF16)
        return carry

    lax.fori_loop(0, width // TILE, proj_rows, 0)
    sm_all = sm_ref[...]
    for e in range(n_dp):
        smt[e] = (pltpu.roll(sm_all, width - e * share, 1) if e else sm_all)[:, :128]
    dkt[...] = jnp.zeros_like(dkt)
    dvt[...] = jnp.zeros_like(dvt)
    barrier_wait(3 + n_dp - 1)

    def send_ctx(k):
        return remote(gctx.at[flip(h, k)], gcr.at[h], gc_s.at[k], gc_r.at[k], at_head(k))

    for k in (2, 3, 1):
        send_ctx(k).start()

    def send_prod(r):
        rows = pl.ds(r * cap, cap)
        return remote(prod_h.at[rows, :], prodr.at[rows, :], pr_s.at[r], pr_r.at[r], at_dp(r))

    pairs = n_dp // 2
    side, place = lax.rem(d, 2), lax.div(d, 2)
    pair_order = list(range(pairs // 2, pairs)) + list(range(1, pairs // 2))

    def dp_rows(index):
        return pl.ds(pl.multiple_of(index * share, share), share)

    def send_px(j):
        return remote(pgall.at[dp_rows(2 * j + 1 - side), :], pgx.at[j], px_s.at[j], px_r.at[j], at_dp(1))

    def send_pz(r):
        return remote(pga.at[flip(place, r)], pgz.at[r], pz_s.at[r], pz_r.at[r], at_dp(2 * r))

    def send_ph(k):
        return remote(pgh.at[flip(h, k)], pghr.at[k], ph_s.at[k], ph_r.at[k], at_head(k))

    for j in range(pairs):
        send_px(j).start()
    for r in order:
        send_prod(r).start()
    prod_own = pltpu.make_async_copy(prod_h.at[pl.ds(0, cap), :], prodr.at[pl.ds(0, cap), :], pr_s.at[0])
    prod_own.start()
    gcr[h] = gctx[h]

    sm_head = [remote(smh, smr.at[k], sh_s.at[k], sh_r.at[k], at_head(k)) for k in (1, 2, 3)]
    bg_head = [remote(bg_ref.at[flip(h, k)], bgr.at[k], bg_s.at[k], bg_r.at[k], at_head(k)) for k in (1, 2, 3)]
    up_half = width // 2
    up_cross = [
        remote(upc_h.at[pl.ds(i * up_half, up_half), :], upr_o.at[pl.ds(i * up_half, up_half), :], uc_s.at[i], uc_r.at[i], cross)
        for i in range(2)
    ]

    for copy in bg_head:
        copy.start()

    def send_sm(r):
        return remote(smt.at[flip(d, r)], smd.at[r], sd_s.at[r], sd_r.at[r], at_dp(r))

    for r in order:
        send_sm(r).start()

    load_qkv.wait()

    def wait_block(b):
        for k in (1, 2, 3):

            @pl.when(flip(h, k) == b)
            def _():
                remote(gctx.at[0], gcr.at[b], gc_s.at[k], gc_r.at[k], at_head(k)).wait_recv()

    def attention(t, size, unrolled):
        b, sub = lax.div(t, per_block), lax.rem(t, per_block)

        @pl.when(sub == 0)
        def _():
            wait_block(b)

        p_load(t, size).wait()
        rows = pl.ds(pl.multiple_of(t * TILE, TILE), TILE)
        win = pl.ds(pl.multiple_of((t + 1) * TILE - size, TILE), size)
        grad = gcr[b, pl.ds(pl.multiple_of(sub * size_t, size_t), size_t), :]
        meets = unpack(grad.astype(F32) * ctx[t].astype(F32))
        gs, gts = unpack(grad), unpack_t(flip_t(grad))
        qts = unpack_t(flip_t(pack([qkv[0, a, rows, :] for a in range(heads)])))
        for a in range(heads):
            delta_s[a] = jnp.sum(meets[a], axis=1, keepdims=True)
            g_s[a], gt_s[a], qt_s[a] = gs[a], gts[a], qts[a]

        def head(a, carry):
            p = p_v[t, a, :, :size]
            ds = (p.astype(F32) * (dot(g_s[a], qkv[2, a, win, :], ((1,), (1,))) - delta_s[a])).astype(BF16)
            dq_s[a] = dot(ds, qkv[1, a, win, :]) * (hd ** (-0.5))
            at = pl.ds(pl.multiple_of(a * hd, hd), hd)
            dkt[at, win] += dot(qt_s[a], ds)
            dvt[at, win] += dot(gt_s[a], p)
            return carry

        if unrolled:
            for a in range(heads):
                head(a, 0)
        else:
            lax.fori_loop(0, heads, head, 0)
        dq = jnp.concatenate([dq_s[a] for a in range(heads)], axis=1)
        grads[rows, :cols] = dq.astype(BF16)
        gradst[:cols, rows] = dq.T.astype(BF16)

    half = tiles // 2

    def both_halves(i, carry):
        @pl.when(i == 1)
        def _():
            for copy in up_cross:
                copy.start()

        turn = lax.rem(i + lax.div(h, 2), 2)

        @pl.when(turn == 0)
        def _():
            for t in range(half):
                attention(t, (t + 1) * TILE, t >= 2)

        @pl.when(turn == 1)
        def _():
            def high_tile(t, inner):
                attention(t, reach * TILE, UNROLL_B)
                return inner

            lax.fori_loop(half, tiles, high_tile, 0)

        return carry

    lax.fori_loop(0, 2, both_halves, 0)

    for copy in later:
        copy.wait()

    def settle(t, carry):
        at = pl.ds(pl.multiple_of(t * TILE, TILE), TILE)
        both = jnp.concatenate([dkt[:, at], dvt[:, at]], axis=0)
        gradst[cols:, at] = both.astype(BF16)
        grads[at, cols:] = both.T.astype(BF16)
        return carry

    lax.fori_loop(0, tiles, settle, 0)

    pieces = 2
    piece = tok // pieces

    def normed_piece(index, i):
        at = pl.ds(pl.multiple_of(index * tok + i * piece, piece), piece)
        total = dot(grads[at, :cols], w_ref[0])
        for c in range(1, 3):
            total += dot(grads[at, c * cols : (c + 1) * cols], w_ref[c])
        return total

    def part(i):
        return pl.ds(pl.multiple_of(i * piece, piece), piece)

    def gn_sib(j, i):
        return remote(gsend.at[j, part(i), :], grecv.at[j, part(i), :], gn_s.at[j, i], gn_r.at[j, i], sib)

    def gn_cross(i):
        return remote(gacc.at[part(i), :], grecv.at[2, part(i), :], gx_s.at[i], gx_r.at[i], cross)

    def across(i, carry):
        gsend[1, part(i), :] = normed_piece(flip(h, 3), i).astype(BF16)
        gn_sib(1, i).start()
        mine = normed_piece(flip(h, 2), i)
        gn_sib(1, i).wait_recv()
        gacc[part(i), :] = (mine + grecv[1, part(i), :].astype(F32)).astype(BF16)
        gn_cross(i).start()
        return carry

    lax.fori_loop(0, pieces, across, 0)
    for j in range(pairs):
        send_px(j).wait_recv()
        pga[j] = (pgall[dp_rows(2 * j + side), :].astype(F32) + pgx[j].astype(F32)).astype(BF16)
    for r in pair_order:
        send_pz(r).start()

    load_gath.wait()
    for c in range(3):
        comb[:, c * cols : (c + 1) * cols] = dot(gradst[c * cols : (c + 1) * cols, :], gath[...]).T.astype(BF16)
    ones = jnp.ones((8, group), BF16)
    qb[...] = jnp.concatenate([dot(ones, grads[:, :cols])[:1], dot(ones, grads[:, 2 * cols :])[:1]], axis=1)

    def send_side(j):
        return remote(comb.at[dp_rows(2 * j + 1 - side), :], combx.at[j], qx_s.at[j], qx_r.at[j], at_dp(1))

    def send_qg(r):
        return remote(comba.at[flip(place, r)], combr.at[r], qg_s.at[r], qg_r.at[r], at_dp(2 * r))

    def send_qb(r):
        return remote(qb, qbr.at[r], qb_s.at[r], qb_r.at[r], at_dp(r))

    for j in range(pairs):
        send_side(j).start()
    for r in order:
        send_qb(r).start()
    def beside(i, carry):
        gsend[0, part(i), :] = normed_piece(flip(h, 1), i).astype(BF16)
        gn_sib(0, i).start()
        own_s[part(i), :] = normed_piece(h, i)
        return carry

    lax.fori_loop(0, pieces, beside, 0)

    for j in range(pairs):
        send_side(j).wait_recv()
        comba[j] = (comb[dp_rows(2 * j + side), :].astype(F32) + combx[j].astype(F32)).astype(BF16)
    for r in pair_order:
        send_qg(r).start()
    for r in order:
        send_sm(r).wait_recv()
    total = smt[d]
    for r in range(1, n_dp):
        total += smd[r]
    smh[...] = total
    for copy in sm_head:
        copy.start()
    hot, flat_row, slot_row = slot_layouts(routes_ref[...], n_dp, cap)
    expert_row = jnp.sum(hot * lax.broadcasted_iota(jnp.int32, hot.shape, 0).astype(F32), axis=0, keepdims=True)
    flat_x = jnp.bitwise_xor(expert_row.astype(jnp.int32), d) * cap + slot_row
    flat_col = row_to_col(flat_x.astype(F32)).astype(jnp.int32)
    for r in order:
        send_prod(r).wait_recv()
    prod_own.wait()
    fcol[...] = flat_col

    def mix(i, carry):
        at = pl.ds(pl.multiple_of(i * 128, 128), 128)
        pick = (fcol[at, :] == lax.broadcasted_iota(jnp.int32, (128, slots), 1)).astype(F32).astype(BF16)
        mixed_o[at, :] = (res[at, :] + gate_ref[at, :] * dot(pick, prodr[...])).astype(BF16)
        return carry

    lax.fori_loop(0, tok // 128, mix, 0)
    gain, bias = g1_ref[...][None, :], b1_ref[...][None, :]

    def norm_back(i, carry):
        at = pl.ds(pl.multiple_of(i * 64, 64), 64)
        own = own_s[at, :] + grecv[0, at, :].astype(F32) + grecv[2, at, :].astype(F32)
        _, scaled, inverse = normalize(x_ref[at, :].astype(F32), gain, bias)
        igrad_o[at, :] = gres[at, :] + norm_backward(own, scaled, inverse, gain)
        return (carry[0] + jnp.sum(own * scaled, axis=0, keepdims=True), carry[1] + jnp.sum(own, axis=0, keepdims=True))

    sums = (jnp.zeros((1, width), F32),) * 2
    for i in range(pieces):
        gn_sib(0, i).wait_recv()
        gn_cross(i).wait_recv()
        sums = lax.fori_loop(i * (piece // 64), (i + 1) * (piece // 64), norm_back, sums)
    gain_sum, bias_sum = sums
    en[0:1, :] = gain_sum
    en[1:2, :] = bias_sum
    en_head = [remote(en, enr.at[k], eh_s.at[k], eh_r.at[k], at_head(k)) for k in (1, 2, 3)]
    for copy in en_head:
        copy.start()
    for r in pair_order:
        send_pz(r).wait_recv()
    total = pgall[dp_rows(d), :].astype(F32) + pgx[place].astype(F32)
    for r in range(1, pairs):
        total += pgz[r].astype(F32)
    for b in range(4):
        pgh[b] = total[:, b * cols : (b + 1) * cols].astype(BF16)
    for k in (2, 3, 1):
        send_ph(k).start()
    for copy in en_head:
        copy.wait_recv()
    ent[...] = en[...] + enr[1] + enr[2] + enr[3]
    en_dp = [remote(ent, enq.at[r], ed_s.at[r], ed_r.at[r], at_dp(r)) for r in range(1, n_dp)]
    for copy in en_dp:
        copy.start()

    for r in pair_order:
        send_qg(r).wait_recv()
    for r in order:
        send_qb(r).wait_recv()
    total = comb[dp_rows(d), :].astype(F32) + combx[place].astype(F32)
    for r in range(1, pairs):
        total += combr[r].astype(F32)
    comb_o[:, : 3 * cols] = total
    total = pgh[h].astype(F32)
    for k in (1, 2, 3):
        send_ph(k).wait_recv()
        total += pghr[k].astype(F32)
    comb_o[:, 3 * cols :] = total
    sums = qb[...]
    for r in range(1, n_dp):
        sums += qbr[r]
    qb_o[...] = sums
    for copy in sm_head:
        copy.wait_recv()
    sums_o[...] = smh[...] + smr[1] + smr[2] + smr[3]
    for copy in bg_head:
        copy.wait_recv()
    bgs_o[...] = bg_ref[h] + bgr[1] + bgr[2] + bgr[3]
    for copy in en_dp:
        copy.wait_recv()
    total = ent[...]
    for r in range(1, n_dp):
        total += enq[r]
    ends_o[...] = total

    for k in (1, 2, 3):
        send_ctx(k).wait_send()
    for r in order:
        send_prod(r).wait_send()
        send_qb(r).wait_send()
        send_sm(r).wait_send()
    for r in pair_order:
        send_qg(r).wait_send()
    for j in range(pairs):
        send_side(j).wait_send()
    for copy in up_cross:
        copy.wait()
    for k in (1, 2, 3):
        send_ph(k).wait_send()
    for r in pair_order:
        send_pz(r).wait_send()
    for j in range(pairs):
        send_px(j).wait_send()
    for copy in [gn_cross(i) for i in range(pieces)] + [gn_sib(j, i) for j in range(2) for i in range(pieces)] + sm_head + bg_head + en_head + en_dp:
        copy.wait_send()


def stage_b(n_dp, gctx, qkv, probs, ctx, ctxf, gath, w, x, g1, b1, gres, res, gate, routes, prod, upc, sm, bg):
    tok, width = x.shape
    _, heads, group, hd = qkv.shape
    cols = heads * hd
    span = probs.shape[3]
    share = width // n_dp
    sds = jax.ShapeDtypeStruct
    vm = pltpu.VMEM
    return pl.pallas_call(
        functools.partial(kernel_b, n_dp),
        out_shape=(
            sds((tok, width), BF16),
            sds((tok, width), F32),
            sds(upc.shape, BF16),
            sds((share, width), F32),
            sds((1, 2 * cols), F32),
            sds((sm.shape[0], 128), F32),
            sds((2, width), F32),
            sds(bg.shape[1:], F32),
        ),
        in_specs=[VM, ANY, ANY, VM, VM, ANY, ANY, ANY, VM, VM, VM, ANY, VM, VM, ANY, ANY, VM, VM],
        out_specs=(VM, VM, ANY) + (VM,) * 5,
        scratch_shapes=[
            vm((3, cols, width), BF16), vm((tok, width), BF16), vm((tok, width), F32),
            vm(gctx.shape, BF16), vm((3, heads, group, hd), BF16), vm((group // TILE, heads, TILE, span), BF16), vm((group, width), BF16),
            vm(prod.shape, BF16),
            vm((heads, TILE, hd), BF16), vm((heads, hd, TILE), BF16), vm((heads, hd, TILE), BF16), vm((heads, TILE, 1), F32),
            vm((heads, TILE, hd), F32), vm((tok, width), F32), vm((tok, 1), jnp.int32), vm((cols, group), F32), vm((cols, group), F32), vm((group, 3 * cols), BF16), vm((3 * cols, group), BF16),
            vm((2, tok, width), BF16), vm((tok, width), BF16), vm((3, tok, width), BF16),
            vm((width, 3 * cols), BF16), vm((n_dp // 2, share, 3 * cols), BF16), vm((n_dp // 2, share, 3 * cols), BF16),
            vm((n_dp // 2, share, 3 * cols), BF16),
            vm((tok, width), BF16), vm((width, width), BF16), vm((n_dp // 2, share, width), BF16), vm((n_dp // 2, share, width), BF16),
            vm((n_dp // 2, share, width), BF16), vm((4, share, cols), BF16), vm((4, share, cols), BF16), vm((width, tok), BF16),
            vm((1, 2 * cols), F32), vm((n_dp, 1, 2 * cols), F32),
            vm((4, sm.shape[0], 128), F32), vm((n_dp, sm.shape[0], 128), F32), vm((n_dp, sm.shape[0], 128), F32),
            vm((sm.shape[0], 128), F32),
            vm((2, width), F32), vm((4, 2, width), F32), vm((2, width), F32), vm((n_dp, 2, width), F32),
            vm((4,) + bg.shape[1:], F32),
            DMA((5,)), DMA((group // TILE,)), DMA((4,)), DMA((4,)), DMA((n_dp,)), DMA((n_dp,)), DMA((2,)), DMA((2,)), DMA((2, 2)), DMA((2, 2)),
            DMA((2,)), DMA((2,)), DMA((n_dp // 2,)), DMA((n_dp // 2,)), DMA((n_dp // 2,)), DMA((n_dp // 2,)),
            DMA((n_dp // 2,)), DMA((n_dp // 2,)), DMA((n_dp // 2,)), DMA((n_dp // 2,)), DMA((4,)), DMA((4,)), DMA((n_dp,)), DMA((n_dp,)),
            DMA((4,)), DMA((4,)), DMA((n_dp,)), DMA((n_dp,)), DMA((4,)), DMA((4,)), DMA((n_dp,)), DMA((n_dp,)), DMA((4,)), DMA((4,)),
        ],
        compiler_params=pltpu.CompilerParams(collective_id=2, has_side_effects=True, vmem_limit_bytes=VMEM_LIMIT),
    )(gctx, qkv, probs, ctx, ctxf, gath, w.transpose(0, 2, 1), x, g1, b1, gres, res, gate, routes.T, prod, upc, sm, bg)


def kernel_f(
    n_dp, mixed, igrad, upo, upr, dno, dnr, comb, qb, sums, ends, bgs, bal,
    mixed_o, bal_o, igrad_o, g1_o, b1_o, qkv_o, qkvb_o, proj_o, pb_o, g2_o, b2_o, router_o, up_o, upb_o, down_o, downb_o,
):
    mixed_o[...] = mixed[...]
    igrad_o[...] = igrad[...]
    up_o[0] = upo[...].astype(F32) + upr[...].astype(F32)
    down_o[0] = dno[...].astype(F32) + dnr[...].astype(F32)

    @pl.when(pl.program_id(0) == 0)
    def _():
        d = lax.axis_index("dp")
        device = d * 4 + lax.axis_index("head")
        width = ends.shape[1]
        part = g1_o.shape[0]
        cols = qkv_o.shape[2]
        hd = cols // 3
        share = qkvb_o.shape[2]
        bal_o[...] = bal[0]
        shift = lax.rem(width - device * part, width)
        mine = pltpu.roll(sums[...], lax.rem(128 - lax.axis_index("head") * part, 128), 1)[:, :part]
        tail = pltpu.roll(jnp.concatenate([ends[...], jnp.zeros((6, width), F32)], axis=0), shift, 1)[:, :part]
        g1_o[...] = tail[0]
        b1_o[...] = tail[1]
        g2_o[...] = mine[0]
        b2_o[...] = mine[1]
        pb_o[...] = mine[2]
        router_o[...] = mine[8 : 8 + n_dp]
        for c in range(3):
            qkv_o[c] = comb[:, c * cols : (c + 1) * cols]
        proj_o[...] = comb[:, 3 * cols :].T
        turned = pltpu.roll(jnp.broadcast_to(qb[...], (8, 2 * cols)), lax.rem(2 * cols - d * share, 2 * cols), 1)
        for a in range(3):
            for c in range(2):
                at = c * cols + a * hd
                qkvb_o[a, c : c + 1, :] = turned[:1, at : at + share]
        upb_o[...] = bgs[0:1, :]
        downb_o[...] = bgs[1:2, : downb_o.shape[1]]


def stage_f(n_dp, mixed, igrad, upo, upr, dno, dnr, comb, qb, sums, ends, bgs, bal):
    tok, width = mixed.shape
    cols = qb.shape[1] // 2
    part = width // (4 * n_dp)
    share = width // n_dp
    steps = 4
    sds = jax.ShapeDtypeStruct

    def rows(shape):
        if len(shape) == 3:
            return pl.BlockSpec((1, shape[1] // steps, shape[2]), lambda i: (0, i, 0))
        return pl.BlockSpec((shape[0] // steps, shape[1]), lambda i: (i, 0))

    def whole(shape):
        return pl.BlockSpec(shape, lambda i: (0,) * len(shape))

    args = (mixed, igrad, upo, upr, dno, dnr, comb, qb, sums, ends, bgs, bal)
    outs = (
        sds((tok, width), BF16), sds((1,), F32), sds((tok, width), F32), sds((part,), F32), sds((part,), F32),
        sds((3, share, cols), F32), sds((3, 2, cols // 3 // n_dp), F32), sds((cols, share), F32), sds((part,), F32), sds((part,), F32),
        sds((part,), F32), sds((n_dp, part), F32), sds((1,) + upo.shape, F32), sds((1, upo.shape[1]), F32),
        sds((1,) + dno.shape, F32), sds((1, width // 4), F32),
    )
    return pl.pallas_call(
        functools.partial(kernel_f, n_dp),
        out_shape=outs,
        grid=(steps,),
        in_specs=[rows(a.shape) for a in args[:6]] + [whole(a.shape) for a in args[6:]],
        out_specs=tuple(rows(o.shape) if i in (0, 2, 12, 14) else whole(o.shape) for i, o in enumerate(outs)),
        compiler_params=pltpu.CompilerParams(vmem_limit_bytes=VMEM_LIMIT),
    )(*args)


def local(
    block_input, norm1_gain, norm1_bias, qkv_weight, qkv_bias, proj_weight, proj_bias, norm2_gain, norm2_bias, router_weight,
    up_weight, up_bias, down_weight, down_bias, routes, lengths, cotangent,
):
    tok, width = block_input.shape
    experts = router_weight.shape[1]
    cap = 2 * tok // experts
    gath, qkv, probs, ctx, ctxf, projf, cots = stage_a(
        experts, block_input, norm1_gain, norm1_bias, qkv_weight, qkv_bias, proj_weight, routes, cotangent, lengths, cap
    )
    res, gate, prod, gres, gctx, upc, upo, dno, dnr, sm, bg, balance = stage_m(
        experts, block_input, ctxf, projf, proj_bias, norm2_gain, norm2_bias, router_weight, routes, cotangent, cots,
        up_weight, up_bias, down_weight, down_bias,
    )
    mixed, igrad, upr, comb, qb, sums, ends, bgs = stage_b(
        experts, gctx, qkv, probs, ctx, ctxf, gath, qkv_weight, block_input, norm1_gain, norm1_bias, gres, res, gate, routes, prod,
        upc, sm, bg,
    )
    outs = list(stage_f(experts, mixed, igrad, upo, upr, dno, dnr, comb, qb, sums, ends, bgs, balance))
    outs[6] = outs[6].transpose(1, 0, 2)
    outs[11] = outs[11].T
    return tuple(outs)


def solution(mesh):
    placed = (
        P(("dp", "head"), None), P(), P(), P(None, None, "head"), P(None, "head", None), P("head", None), P(), P(), P(), P(),
        P("dp", None, None), P("dp", None), P("dp", None, None), P("dp", None), P(("dp", "head"), None), P("dp", None),
        P(("dp", "head"), None),
    )
    tokens = P(("dp", "head"))
    return jax.shard_map(
        local,
        mesh=mesh,
        in_specs=placed,
        out_specs=(
            P(("dp", "head"), None), tokens, P(("dp", "head"), None), tokens, tokens, P(None, "dp", "head"), P(None, "head", "dp"),
            P("head", "dp"), tokens, tokens, tokens, P(("dp", "head"), None), P("dp", None, "head"), P("dp", "head"),
            P("dp", "head", None), P("dp", "head"),
        ),
        check_vma=False,
    )
```
